512 devices in a mesh: wide: 64 (over y_lo, x, z), narrow: 8 (over y_hi, core).
Axes of the slice: x: 4, y: 8 (y_hi: 4, y_lo: 2; y = y_hi * 2 + y_lo), z: 8, core: 2. Of those that a mesh axis runs over, the one named last changes fastest.
Arguments:
- alignment_rows: bfloat16 [128, 512, 256], P('wide', 'narrow'), may hold values from -6 to 6
- pair_output_gradient: bfloat16 [512, 512, 128], P('wide', 'narrow'), may hold values from -6 to 6
- layer_norm_gain: float32 [256], replicated, may hold values from 0.5 to 1.5
- layer_norm_bias: float32 [256], replicated, may hold values from -3 to 3
- projection_weight: bfloat16 [2, 256, 32], replicated, may hold values from -0.375 to 0.375
- projection_bias: float32 [2, 32], replicated, may hold values from -3 to 3
- output_weight: bfloat16 [1024, 128], replicated, may hold values from -0.1875 to 0.1875
Outputs:
- alignment_gradient: bfloat16 [128, 512, 256], P('wide', 'narrow')
- projection_gradient: float32 [2, 256, 32], replicated
- projection_bias_gradient: float32 [2, 32], replicated
- output_weight_gradient: float32 [1024, 128], replicated
- layer_norm_gradient: float32 [2, 256], replicated
The draws below stay inside these ranges and needn't reach their ends.
All inputs are finite; a program needn't handle non-finite values.
Results may differ from the reference program's by a relative error of at most 0.012.
Values may be sent and summed in bfloat16 or wider, within the bound.
A program may use at most 64 MiB of HBM per device.

```python
import jax
import jax.numpy as jnp
from jax import lax

ALIGNMENT_WIDTH = 256
FACTOR_CHANNELS = 32
PAIR_WIDTH = 128
OUTER = 1024
ALIGNED_SEQUENCES = 128
CROP_RESIDUES = 512


def shard_levels(key, extent, split, low, high):
    loudness = 1.0
    for dim, blocks in split:
        steps = jax.random.uniform(jax.random.fold_in(jax.random.fold_in(key, 6), dim), (blocks,), jnp.float32, low / len(split), high / len(split))
        loudness = loudness * jnp.repeat(jnp.exp(steps), extent[dim] // blocks).reshape((-1,) + (1,) * (len(extent) - 1 - dim))
    return loudness


def centred(stream_key, shape, spread, most, split=(), kind=jnp.bfloat16):
    loudness = shard_levels(stream_key, shape, split, -0.22, 0.18) if split else 1.0
    array = jax.random.normal(stream_key, shape, jnp.float32) * spread * loudness
    return jnp.minimum(jnp.maximum(array, -most), most).astype(kind)


def setup_inputs(seed: int = 0) -> dict:
    key_of = jax.random.split(jax.random.key(seed), 8)
    return {
        "alignment_rows": centred(key_of[0], (ALIGNED_SEQUENCES, CROP_RESIDUES, ALIGNMENT_WIDTH), 1.0, 6.0, ((0, 64), (1, 8))),
        "pair_output_gradient": centred(key_of[1], (CROP_RESIDUES, CROP_RESIDUES, PAIR_WIDTH), 1.0, 6.0, ((0, 64), (1, 8))),
        "layer_norm_gain": jnp.clip(1.0 + 0.1 * jax.random.normal(key_of[2], (ALIGNMENT_WIDTH,), jnp.float32), 0.5, 1.5),
        "layer_norm_bias": centred(key_of[3], (ALIGNMENT_WIDTH,), 0.5, 3.0, (), jnp.float32),
        "projection_weight": centred(key_of[4], (2, ALIGNMENT_WIDTH, FACTOR_CHANNELS), ALIGNMENT_WIDTH ** -0.5, 0.375),
        "projection_bias": centred(key_of[5], (2, FACTOR_CHANNELS), 0.5, 3.0, (), jnp.float32),
        "output_weight": centred(key_of[6], (OUTER, PAIR_WIDTH), OUTER ** -0.5, 0.1875),
    }


def reference(alignment_rows, pair_output_gradient, layer_norm_gain, layer_norm_bias, projection_weight, projection_bias, output_weight):
    value_rows = alignment_rows.astype(jnp.float32)
    centre = value_rows - lax.optimization_barrier(jnp.mean(value_rows, axis=-1, keepdims=True))
    inverse_deviation = lax.rsqrt(lax.optimization_barrier(jnp.mean(centre * centre, axis=-1, keepdims=True)) + 1e-05)
    normalized_rows = centre * inverse_deviation
    scaled_product = (normalized_rows * layer_norm_gain + layer_norm_bias).astype(jnp.bfloat16)
    flattened_rows = scaled_product.reshape(ALIGNED_SEQUENCES * CROP_RESIDUES, ALIGNMENT_WIDTH)
    row_factor = (jnp.dot(flattened_rows, projection_weight[0], preferred_element_type=jnp.float32) + projection_bias[0]).astype(jnp.bfloat16)
    col_factor = (jnp.dot(flattened_rows, projection_weight[1], preferred_element_type=jnp.float32) + projection_bias[1]).astype(jnp.bfloat16)
    row_wide = row_factor.reshape(ALIGNED_SEQUENCES, CROP_RESIDUES, FACTOR_CHANNELS).astype(jnp.float32)
    col_wide = col_factor.reshape(ALIGNED_SEQUENCES, CROP_RESIDUES, FACTOR_CHANNELS).astype(jnp.float32)
    block_rows = 64

    def scan_block(running, first_row):
        weight_acc, col_acc = running
        row_slice = lax.dynamic_slice_in_dim(row_wide, first_row, block_rows, 1)
        grad_block = lax.dynamic_slice_in_dim(pair_output_gradient, first_row, block_rows, 0).reshape(block_rows * CROP_RESIDUES, PAIR_WIDTH)
        outer_prod = jnp.einsum('sip,sjq->ijpq', row_slice, col_wide) / ALIGNED_SEQUENCES
        outer_b = outer_prod.astype(jnp.bfloat16).reshape(block_rows * CROP_RESIDUES, OUTER)
        weight_acc = weight_acc + jnp.dot(outer_b.T, grad_block, preferred_element_type=jnp.float32)
        upstream = jnp.dot(grad_block, output_weight.T, preferred_element_type=jnp.float32).astype(jnp.bfloat16)
        upstream = upstream.reshape(block_rows, CROP_RESIDUES, FACTOR_CHANNELS, FACTOR_CHANNELS).astype(jnp.float32)
        row_part = jnp.einsum('ijpq,sjq->sip', upstream, col_wide) / ALIGNED_SEQUENCES
        col_acc = col_acc + jnp.einsum('ijpq,sip->sjq', upstream, row_slice) / ALIGNED_SEQUENCES
        return ((weight_acc, col_acc), row_part)
    starts = (jnp.arange(CROP_RESIDUES // block_rows) * block_rows).astype(jnp.int32)
    init = (jnp.zeros((OUTER, PAIR_WIDTH), jnp.float32), jnp.zeros((ALIGNED_SEQUENCES, CROP_RESIDUES, FACTOR_CHANNELS), jnp.float32))
    (output_weight_gradient, col_grad), row_parts = lax.scan(scan_block, init, starts)
    row_grad = jnp.transpose(row_parts, (1, 0, 2, 3)).reshape(ALIGNED_SEQUENCES, CROP_RESIDUES, FACTOR_CHANNELS)
    row_b = row_grad.astype(jnp.bfloat16).reshape(ALIGNED_SEQUENCES * CROP_RESIDUES, FACTOR_CHANNELS)
    col_b = col_grad.astype(jnp.bfloat16).reshape(ALIGNED_SEQUENCES * CROP_RESIDUES, FACTOR_CHANNELS)
    scaled_product_gradient = jnp.dot(row_b, projection_weight[0].T, preferred_element_type=jnp.float32) + jnp.dot(col_b, projection_weight[1].T, preferred_element_type=jnp.float32)
    scaled_product_gradient = scaled_product_gradient.reshape(ALIGNED_SEQUENCES, CROP_RESIDUES, ALIGNMENT_WIDTH)
    projection_gradient = jnp.stack([jnp.dot(flattened_rows.T, row_b, preferred_element_type=jnp.float32), jnp.dot(flattened_rows.T, col_b, preferred_element_type=jnp.float32)])
    projection_bias_gradient = jnp.stack([lax.optimization_barrier(jnp.sum(row_grad, axis=(0, 1))), lax.optimization_barrier(jnp.sum(col_grad, axis=(0, 1)))])
    layer_norm_gradient = jnp.stack([lax.optimization_barrier(jnp.sum(scaled_product_gradient * normalized_rows, axis=(0, 1))), lax.optimization_barrier(jnp.sum(scaled_product_gradient, axis=(0, 1)))])
    gain_applied = scaled_product_gradient * layer_norm_gain
    alignment_gradient = inverse_deviation * (gain_applied - lax.optimization_barrier(jnp.mean(gain_applied, axis=-1, keepdims=True)) - normalized_rows * lax.optimization_barrier(jnp.mean(gain_applied * normalized_rows, axis=-1, keepdims=True)))
    return (alignment_gradient.astype(jnp.bfloat16), projection_gradient, projection_bias_gradient, output_weight_gradient, layer_norm_gradient)
```

```python
import jax
import jax.numpy as jnp
from jax import lax
from jax.experimental import pallas as pl
from jax.experimental.pallas import tpu as pltpu
from jax.sharding import PartitionSpec as P

FACTOR_CHANNELS = 32
PAIR_WIDTH = 128
OUTER = 1024
PLANE = 8
DEPTH = 8
NARROW = 8
MESH_ID = pl.DeviceIdType.MESH
OFFSETS = (4, 3, 5, 2, 6, 1, 7)


def in_order(pieces, dim):
    pieces = jnp.moveaxis(pieces, 0, dim)
    lengths = pieces.shape
    return pieces.reshape(*lengths[:dim], lengths[dim] * lengths[dim + 1], *lengths[dim + 2 :])


def copy_for_each(array, axis):
    copies = jnp.broadcast_to(array, (lax.axis_size(axis), *array.shape))
    return lax.all_to_all(copies, axis, split_axis=0, concat_axis=0, tiled=True)


def gather_directly(array, axis, dim):
    return in_order(copy_for_each(array, axis), dim)


def in_blocks(array, dim, length):
    lengths = array.shape
    pieces = array.reshape(*lengths[:dim], length, lengths[dim] // length, *lengths[dim + 1 :])
    return jnp.moveaxis(pieces, dim, 0)


def sum_at_owner(array, axis, dim):
    pieces = in_blocks(array, dim, lax.axis_size(axis))
    arrived = lax.all_to_all(pieces, axis, split_axis=0, concat_axis=0, tiled=True)
    return arrived.sum(axis=0)


def summed_on_arrival(array, axis, dim):
    pieces = in_blocks(array, dim, lax.axis_size(axis))
    arrived = lax.all_to_all(pieces, axis, split_axis=0, concat_axis=0, tiled=True)
    return arrived.astype(jnp.float32).sum(axis=0)


def total(ref):
    acc = ref[0].astype(jnp.float32)
    for k in range(1, 8):
        acc = acc + ref[k].astype(jnp.float32)
    return acc


def reduce_kernel(
    big_ref, small_ref, big_out, small_out,
    big_send, big_plane, small_plane, big_part, small_part, big_depth, small_depth,
    big_two, small_two, big_narrow, small_narrow, big_three, small_three, big_gather, big_half,
    send_sem, recv_sem,
):
    wide = lax.axis_index("wide")
    narrow = lax.axis_index("narrow")
    plane = wide // DEPTH
    depth = wide % DEPTH
    barrier = pltpu.get_barrier_semaphore()

    def peer(kind, k):
        if kind == "plane":
            return (k * DEPTH + depth, narrow)
        if kind == "depth":
            return (plane * DEPTH + k, narrow)
        return (wide, k)

    place = {"plane": plane, "depth": depth, "narrow": narrow}

    for kind in ("plane", "depth", "narrow"):
        for d in OFFSETS:
            k = (place[kind] + d) % 8
            pl.semaphore_signal(barrier, 1, device_id=peer(kind, k), device_id_type=MESH_ID)
    big_send[...] = big_ref[...].astype(jnp.bfloat16).reshape(8, 128, 128)
    pl.semaphore_wait(barrier, 21)

    def copies(stage, kind, source, target):
        me = place[kind]
        made = []
        for d in OFFSETS:
            k = (me + d) % 8
            made.append(
                pltpu.make_async_remote_copy(
                    src_ref=source(k),
                    dst_ref=target.at[me],
                    send_sem=send_sem.at[stage, d],
                    recv_sem=recv_sem.at[stage, d],
                    device_id=peer(kind, k),
                    device_id_type=MESH_ID,
                )
            )
        for c in made:
            c.start()
        return made

    def finish(made):
        for c in made:
            c.wait()

    one = copies(0, "plane", lambda k: big_send.at[k], big_plane)
    two = copies(1, "plane", lambda k: small_ref.at[k], small_plane)
    big_plane[plane] = big_send[plane]
    small_plane[plane] = small_ref[plane]
    finish(two)
    small_part[...] = total(small_plane)
    three = copies(2, "depth", lambda k: small_part, small_depth)
    small_depth[depth] = small_part[...]
    finish(one)
    big_part[...] = total(big_plane).reshape(8, 16, 128)
    four = copies(3, "depth", lambda k: big_part.at[k], big_depth)
    big_depth[depth] = big_part[depth]
    finish(three)
    small_two[...] = total(small_depth)
    five = copies(4, "narrow", lambda k: small_two, small_narrow)
    small_narrow[narrow] = small_two[...]
    finish(four)
    big_two[...] = total(big_depth)
    six = copies(5, "narrow", lambda k: big_two, big_narrow)
    big_narrow[narrow] = big_two[...]
    finish(five)
    small_three[...] = total(small_narrow)
    seven = copies(6, "plane", lambda k: small_three, small_out)
    small_out[plane] = small_three[...]
    finish(six)
    big_three[...] = total(big_narrow)
    eight = copies(7, "depth", lambda k: big_three, big_gather)
    big_gather[depth] = big_three[...]
    finish(eight)
    big_half[...] = big_gather[...].astype(jnp.bfloat16).reshape(128, 128)
    nine = copies(8, "plane", lambda k: big_half, big_out)
    big_out[plane] = big_half[...]
    finish(seven)
    finish(nine)


def all_sums(big, small):
    vmem = pl.BlockSpec(memory_space=pltpu.VMEM)
    f32, b16 = jnp.float32, jnp.bfloat16
    return pl.pallas_call(
        reduce_kernel,
        out_shape=(
            jax.ShapeDtypeStruct((8, 128, 128), b16),
            jax.ShapeDtypeStruct((8, 24, 128), f32),
        ),
        in_specs=[vmem, vmem],
        out_specs=(vmem, vmem),
        scratch_shapes=[
            pltpu.VMEM((8, 128, 128), b16),
            pltpu.VMEM((8, 128, 128), b16),
            pltpu.VMEM((8, 24, 128), f32),
            pltpu.VMEM((8, 16, 128), f32),
            pltpu.VMEM((24, 128), f32),
            pltpu.VMEM((8, 16, 128), f32),
            pltpu.VMEM((8, 24, 128), f32),
            pltpu.VMEM((16, 128), f32),
            pltpu.VMEM((24, 128), f32),
            pltpu.VMEM((8, 16, 128), f32),
            pltpu.VMEM((8, 24, 128), f32),
            pltpu.VMEM((16, 128), f32),
            pltpu.VMEM((24, 128), f32),
            pltpu.VMEM((8, 16, 128), f32),
            pltpu.VMEM((128, 128), b16),
            pltpu.SemaphoreType.DMA((9, 8)),
            pltpu.SemaphoreType.DMA((9, 8)),
        ],
        compiler_params=pltpu.CompilerParams(collective_id=0, has_side_effects=True),
    )(big, small)


def shards(
    alignment_rows,
    pair_output_gradient,
    layer_norm_gain,
    layer_norm_bias,
    projection_weight,
    projection_bias,
    output_weight,
):
    sequence_deviation = alignment_rows.shape[0]
    column_residue = alignment_rows.shape[1]
    row_res = pair_output_gradient.shape[0]
    total_seq = sequence_deviation * lax.axis_size("wide")
    value_rows = alignment_rows.astype(jnp.float32)
    centre = value_rows - jnp.mean(value_rows, axis=-1, keepdims=True)
    inverse_deviation = lax.rsqrt(jnp.mean(centre * centre, axis=-1, keepdims=True) + 1e-05)
    normalized_rows = centre * inverse_deviation
    scaled_product = (normalized_rows * layer_norm_gain + layer_norm_bias).astype(jnp.bfloat16)
    factors = jnp.einsum(
        "src,kch->kshr", scaled_product, projection_weight, preferred_element_type=jnp.float32
    )
    factors = (factors + projection_bias[:, None, :, None]).astype(jnp.bfloat16)
    row_factor = factors[0]
    col_factor = factors[1]
    row_local = gather_directly(row_factor, "narrow", 2)
    row_regrouped = lax.all_to_all(row_local, "wide", split_axis=2, concat_axis=0, tiled=True)
    col_whole = gather_directly(col_factor, "wide", 0)
    block_rows = row_res // 4
    weight_acc = jnp.zeros((OUTER, PAIR_WIDTH), jnp.float32)
    row_parts = []
    upstream_blocks = []
    for block_index in range(4):
        row_slice = row_regrouped[:, :, block_index * block_rows : (block_index + 1) * block_rows]
        grad_block = pair_output_gradient[
            block_index * block_rows : (block_index + 1) * block_rows
        ].reshape(block_rows * column_residue, PAIR_WIDTH)
        outer_prod = jnp.einsum(
            "spi,sqj->ijpq", row_slice, col_whole, preferred_element_type=jnp.float32
        )
        outer_b = (
            (outer_prod / total_seq)
            .astype(jnp.bfloat16)
            .reshape(block_rows * column_residue, OUTER)
        )
        weight_acc = weight_acc + jnp.einsum(
            "nk,ne->ke", outer_b, grad_block, preferred_element_type=jnp.float32
        )
        upstream = jnp.einsum(
            "ne,ke->nk", grad_block, output_weight, preferred_element_type=jnp.float32
        )
        upstream = upstream.astype(jnp.bfloat16).reshape(
            block_rows, column_residue, FACTOR_CHANNELS, FACTOR_CHANNELS
        )
        row_part = jnp.einsum(
            "ijpq,sqj->spi", upstream, col_whole, preferred_element_type=jnp.float32
        )
        row_parts.append(row_part / total_seq)
        upstream_blocks.append(upstream)
    row_partial = jnp.concatenate(row_parts, axis=2)
    upstream_all = jnp.concatenate(upstream_blocks, axis=0)
    col_grad = sum_at_owner(
        jnp.einsum("ijpq,spi->sqj", upstream_all, row_regrouped, preferred_element_type=jnp.float32)
        / total_seq,
        "wide",
        0,
    )
    moved_rows = lax.all_to_all(
        row_partial.astype(jnp.bfloat16), "wide", split_axis=0, concat_axis=2, tiled=True
    ).astype(row_partial.dtype)
    row_grad = summed_on_arrival(moved_rows.astype(jnp.bfloat16), "narrow", 2)
    factor_grad = jnp.stack([row_grad, col_grad])
    factor_grad_b = factor_grad.astype(jnp.bfloat16)
    scaled_product_gradient = jnp.einsum(
        "kshr,kch->src", factor_grad_b, projection_weight, preferred_element_type=jnp.float32
    )
    proj_local = jnp.einsum(
        "src,kshr->khc", scaled_product, factor_grad_b, preferred_element_type=jnp.float32
    )
    bias_local = jnp.sum(factor_grad, axis=(1, 3))
    norm_local = jnp.stack(
        [
            jnp.sum(scaled_product_gradient * normalized_rows, axis=(0, 1)),
            jnp.sum(scaled_product_gradient, axis=(0, 1)),
        ]
    )
    gain_applied = scaled_product_gradient * layer_norm_gain
    alignment_gradient = inverse_deviation * (
        gain_applied
        - jnp.mean(gain_applied, axis=-1, keepdims=True)
        - normalized_rows * jnp.mean(gain_applied * normalized_rows, axis=-1, keepdims=True)
    )
    small = jnp.concatenate(
        [
            proj_local.reshape(128, 128),
            norm_local.reshape(4, 128),
            jnp.pad(bias_local.reshape(1, 64), ((0, 59), (0, 64))),
        ]
    ).reshape(8, 24, 128)
    big_sum, small_sum = all_sums(weight_acc, small)
    small_sum = small_sum.reshape(192, 128)
    proj = small_sum[:128].reshape(2, FACTOR_CHANNELS, 256)
    return (
        alignment_gradient.astype(jnp.bfloat16),
        jnp.transpose(proj, (0, 2, 1)),
        small_sum[132, :64].reshape(2, FACTOR_CHANNELS),
        big_sum.reshape(OUTER, PAIR_WIDTH).astype(jnp.float32),
        small_sum[128:132].reshape(2, 256),
    )


def solution(mesh):
    return jax.shard_map(
        shards,
        mesh=mesh,
        in_specs=(P("wide", "narrow", None), P("wide", "narrow", None), P(), P(), P(), P(), P()),
        out_specs=(P("wide", "narrow", None), P(), P(), P(), P()),
        check_vma=False,
    )
```

```python
import jax
import jax.numpy as jnp
from jax import lax
from jax.experimental import pallas as pl
from jax.experimental.pallas import tpu as pltpu
from jax.sharding import PartitionSpec as P

F32, B16 = jnp.float32, jnp.bfloat16
MESH_ID = pl.DeviceIdType.MESH
OFFSETS = (4, 3, 5, 2, 6, 1, 7)
STAGES = 17
SEQUENCES = 128
(
    ROW_DEPTH, COL_DEPTH, ROW_PAIR, COL_PLANE, COLG_PLANE, ROWG_PAIR, BIG_PLANE, ROWG_DEPTH, COLG_DEPTH,
    BIG_DEPTH, SMALL_PLANE, BIG_NARROW, SMALL_DEPTH, BIG_BACK, SMALL_NARROW, BIG_OUT, SMALL_OUT,
) = range(STAGES)


def dot(a, b, dims):
    return lax.dot_general(a, b, ((dims[:1], dims[1:]), ((), ())), preferred_element_type=F32)


def total(ref):
    acc = ref[0].astype(F32)
    for k in range(1, 8):
        acc = acc + ref[k].astype(F32)
    return acc


def lanes(shape):
    return lax.broadcasted_iota(jnp.int32, shape, len(shape) - 1)


def half_swap(x):
    return pltpu.roll(x, 64, 1)


def kernel(
    x_ref, pair_ref, gain_ref, shift_ref, weight_ref, bias_ref, out_weight_ref,
    align_out, proj_out, bias_out, norm_out, big_out,
    normed, scaled, scaled32, inverse, row_tmp,
    row_send, col_send, row_got, col_got, col_wide, row_next, col_next,
    row_pair, col_plane, pair_order, weight32, weight_order, upstream, rows, rows_t, cols, outer,
    colg_send, colg_got, rowg_acc, rowg_send, rowg_got, rowg_next, rowg_depth, rowg,
    colg_wide, colg_next, colg_depth, scaled_grad,
    big_send, big_plane, big_part, big_depth, big_two, big_narrow, big_three, big_back, big_half,
    small_in, small_plane, small_part, small_depth, small_two, small_narrow, small_three, small_all,
    send_sem, recv_sem,
):
    wide = lax.axis_index("wide")
    narrow = lax.axis_index("narrow")
    plane = wide // 8
    depth = wide % 8
    own_pair = plane == narrow
    other_pair = plane != narrow
    barrier = pltpu.get_barrier_semaphore()
    place = {"plane": plane, "depth": depth, "narrow": narrow}

    def peer(kind, k):
        if kind == "plane":
            return (k * 8 + depth, narrow)
        if kind == "depth":
            return (plane * 8 + k, narrow)
        return (wide, k)

    def holder(d):
        return (narrow * 8 + depth, (narrow + d) % 8)

    def source(d):
        return (((plane + d) % 8) * 8 + depth, plane)

    def greet(device):
        pl.semaphore_signal(barrier, 1, device_id=device, device_id_type=MESH_ID)

    for kind in ("plane", "depth", "narrow"):
        for d in OFFSETS:
            greet(peer(kind, (place[kind] + d) % 8))
    for d in range(1, 8):
        greet(holder(d))
        greet(source(d))

    @pl.when(other_pair)
    def _():
        greet(holder(0))
        greet(source(0))

    def copies(stage, kind, give, target):
        me = place[kind]
        made = []
        for d in OFFSETS:
            k = (me + d) % 8
            c = pltpu.make_async_remote_copy(
                src_ref=give(k),
                dst_ref=target(me),
                send_sem=send_sem.at[stage, d],
                recv_sem=recv_sem.at[stage, d],
                device_id=peer(kind, k),
                device_id_type=MESH_ID,
            )
            c.start()
            made.append(c)
        return made

    def finish(made):
        for c in made:
            c.wait()

    def pair_copies(stage, device, tag, give, target, own):
        made = []
        for d in range(8):
            c = pltpu.make_async_remote_copy(
                src_ref=give(d),
                dst_ref=target.at[tag],
                send_sem=send_sem.at[stage, d],
                recv_sem=recv_sem.at[stage, tag],
                device_id=device(d),
                device_id_type=MESH_ID,
            )
            k = (tag + d) % 8
            arrival = pltpu.make_async_remote_copy(
                src_ref=give(d),
                dst_ref=target.at[k],
                send_sem=send_sem.at[stage, d],
                recv_sem=recv_sem.at[stage, k],
                device_id=device(d),
                device_id_type=MESH_ID,
            )
            made.append((c, arrival))
        for c, _ in made[1:]:
            c.start()

        @pl.when(other_pair)
        def _():
            made[0][0].start()

        @pl.when(own_pair)
        def _():
            own()

        return made

    def pair_finish(made):
        for c, arrival in made[1:]:
            c.wait_send()
            arrival.wait_recv()

        @pl.when(other_pair)
        def _():
            made[0][0].wait_send()
            made[0][1].wait_recv()

    value = x_ref[...].astype(F32)
    centre = value - jnp.mean(value, axis=-1, keepdims=True)
    inv = lax.rsqrt(jnp.mean(centre * centre, axis=-1, keepdims=True) + 1e-05)
    norm = centre * inv
    inverse[...] = jnp.broadcast_to(inv, (128, 128))
    normed[...] = norm
    scaled_b = (norm * gain_ref[...] + shift_ref[...]).astype(B16)
    scaled[...] = scaled_b
    for c in range(2):
        scaled32[c] = scaled_b[:, c * 128 : c * 128 + 128].astype(F32)

    def every_fourth(g):
        both = [scaled32[c, pl.ds(g, 32, stride=4), :] for c in range(2)]
        return jnp.concatenate(both, axis=1).astype(B16)

    w_row = weight_ref[0:32, :]
    w_col = weight_ref[32:64, :]
    w_row4 = jnp.concatenate([w_row] * 4, axis=0)
    sub = lax.broadcasted_iota(jnp.int32, (32, 32), 0)
    diagonal = sub == lanes((32, 32))
    row_bias = jnp.sum(jnp.where(diagonal, bias_ref[0:1, :], 0.0), axis=1, keepdims=True)
    col_bias = jnp.sum(jnp.where(diagonal, bias_ref[1:2, :], 0.0), axis=1, keepdims=True)
    lane128 = lanes((32, 128))
    sub128 = lax.broadcasted_iota(jnp.int32, (32, 128), 0)
    row_bias4 = jnp.sum(jnp.where(sub128 == lane128 % 32, row_bias, 0.0), axis=0, keepdims=True)
    group = lane128 // 32
    row_fac = jnp.zeros((32, 128), F32)
    for g in range(4):
        row_fac = jnp.where(group == g, dot(every_fourth(g), w_row4, (1, 1)), row_fac)
    row_tmp[...] = (row_fac + row_bias4).astype(B16).astype(F32)
    row_send[...] = jnp.zeros((64, 128), F32)
    for r in range(2):
        for h in range(2):
            row_send[pl.ds(r * 2 + h, 8, stride=8), :] = row_tmp[pl.ds(r * 16 + h, 8, stride=2), :]
    col_send[...] = (dot(w_col, scaled_b, (1, 1)) + col_bias).astype(B16)
    pl.semaphore_wait(barrier, jnp.where(other_pair, 37, 35))

    def eight(ref, k):
        return ref.at[pl.ds(pl.multiple_of(k * 8, 8), 8)]

    row_depth_c = copies(ROW_DEPTH, "depth", lambda k: eight(row_send, k), lambda m: eight(row_got, m))
    col_depth_c = copies(COL_DEPTH, "depth", lambda k: col_send, lambda m: col_got.at[m])
    mine = pl.ds(pl.multiple_of(depth * 8, 8), 8)
    row_got[mine, :] = row_send[mine, :]
    col_got[depth] = col_send[...]

    for g in range(4):
        for h in range(2):
            i = h * 4 + g
            pair_order[pl.ds(g * 128 + h * 64, 64), :] = pair_ref[pl.ds(i * 64, 64), :]
    weight32[...] = out_weight_ref[...].astype(F32)

    def reorder(q, _):
        weight_order[q] = weight32[pl.ds(q, 32, stride=32), :].astype(B16)
        return 0

    lax.fori_loop(0, 32, reorder, 0)

    def up(b, _):
        w = weight_order[pl.ds(b * 2, 2)].reshape(64, 128)
        res = dot(w, pair_order[...], (1, 1)).astype(B16)
        for t in range(2):
            for g in range(4):
                upstream[b, pl.ds(g * 32, 32), pl.ds(t * 128, 128)] = res[t * 32 : t * 32 + 32, g * 128 : g * 128 + 128]
        return 0

    lax.fori_loop(0, 16, up, 0)

    finish(row_depth_c)
    for h in range(2):
        both = [row_got[pl.ds(r * 2 + h, 8, stride=8), :] for r in range(2)]
        row_next[h] = jnp.concatenate(both, axis=0).astype(B16)

    def keep_row():
        row_pair[plane] = row_next[...]

    row_pair_c = pair_copies(ROW_PAIR, holder, plane, lambda d: row_next, row_pair, keep_row)

    finish(col_depth_c)
    col_wide[...] = col_got[...].astype(F32).reshape(256, 128)
    low8 = lanes((8, 128)) < 64

    def spread(b, _):
        x0 = col_wide[pl.ds(b * 2, 8, stride=32), :]
        x1 = col_wide[pl.ds(b * 2 + 1, 8, stride=32), :]
        r0 = jnp.where(low8, x0, half_swap(x1))
        r1 = jnp.where(low8, half_swap(x0), x1)
        col_next[b] = jnp.concatenate([r0, r1], axis=0).astype(B16)
        return 0

    lax.fori_loop(0, 16, spread, 0)
    col_plane_c = copies(COL_PLANE, "plane", lambda k: col_next, lambda m: col_plane.at[m])
    col_plane[plane] = col_next[...]

    pair_finish(row_pair_c)
    for h in range(2):
        rows[pl.ds(h * 128, 128), :] = row_pair[:, h].reshape(128, 128)
    rows_t[...] = rows[...].astype(F32).T.astype(B16)
    low = lanes((128, 128)) < 64

    def col_grad(b, _):
        r = dot(rows[...], upstream[b], (1, 0))
        a = jnp.where(low, r[:128, :128], r[128:, 128:])
        c = jnp.where(low, r[:128, 128:], r[128:, :128])
        out = (a + half_swap(c)) * (1.0 / SEQUENCES)
        colg_send[:, b] = out.astype(B16).reshape(8, 16, 128)
        return 0

    lax.fori_loop(0, 16, col_grad, 0)
    colg_plane_c = copies(COLG_PLANE, "plane", lambda k: colg_send.at[k], lambda m: colg_got.at[m])
    colg_got[plane] = colg_send[plane]

    finish(col_plane_c)
    rowg_acc[...] = jnp.zeros((128, 256), F32)

    def row_grad(b, _):
        c = col_plane[:, b].reshape(128, 128).astype(F32)
        s = half_swap(c)
        cols[b, pl.ds(0, 128), pl.ds(0, 128)] = jnp.where(low, c, 0.0).astype(B16)
        cols[b, pl.ds(128, 128), pl.ds(0, 128)] = jnp.where(low, 0.0, s).astype(B16)
        cols[b, pl.ds(0, 128), pl.ds(128, 128)] = jnp.where(low, s, 0.0).astype(B16)
        cols[b, pl.ds(128, 128), pl.ds(128, 128)] = jnp.where(low, 0.0, c).astype(B16)
        rowg_acc[...] += dot(upstream[b], cols[b], (1, 1))
        return 0

    lax.fori_loop(0, 16, row_grad, 0)
    grad_t = (rowg_acc[...].T * (1.0 / SEQUENCES)).astype(B16)
    for h in range(2):
        rowg_send[:, h] = grad_t[h * 128 : h * 128 + 128].reshape(8, 16, 128)

    def keep_rowg():
        rowg_got[narrow] = rowg_send[plane]

    rowg_pair_c = pair_copies(
        ROWG_PAIR, source, narrow, lambda d: rowg_send.at[(plane + d) % 8], rowg_got, keep_rowg
    )

    def outer_prod(b, _):
        o = (dot(rows_t[...], cols[b], (1, 0)) * (1.0 / SEQUENCES)).astype(B16)
        for t in range(2):
            for g in range(4):
                outer[b * 2 + t, :, pl.ds(g * 128, 128)] = o[g * 32 : g * 32 + 32, t * 128 : t * 128 + 128]
        return 0

    lax.fori_loop(0, 16, outer_prod, 0)

    def weight_grad(k, _):
        o = outer[pl.ds(k * 4, 4)].reshape(128, 512)
        big_send[k] = dot(o, pair_order[...], (1, 0)).astype(B16)
        return 0

    lax.fori_loop(0, 8, weight_grad, 0)
    big_plane_c = copies(BIG_PLANE, "plane", lambda k: big_send.at[k], lambda m: big_plane.at[m])
    big_plane[plane] = big_send[plane]

    pair_finish(rowg_pair_c)
    row_sum = total(rowg_got)
    rowg_next[...] = jnp.zeros((64, 128), F32)
    for h in range(2):
        for r in range(2):
            rowg_next[pl.ds(r * 2 + h, 8, stride=8), :] = row_sum[h, r * 8 : r * 8 + 8, :]
    rowg_depth_c = copies(ROWG_DEPTH, "depth", lambda k: eight(rowg_next, k), lambda m: eight(rowg_depth, m))
    rowg_depth[mine, :] = rowg_next[mine, :]

    finish(colg_plane_c)

    def collect(b, _):
        acc = colg_got[0, b].astype(F32)
        for k in range(1, 8):
            acc = acc + colg_got[k, b].astype(F32)
        y0, y1 = acc[:8], acc[8:]
        colg_wide[pl.ds(b * 2, 8, stride=32), :] = jnp.where(low8, y0, half_swap(y1))
        colg_wide[pl.ds(b * 2 + 1, 8, stride=32), :] = jnp.where(low8, half_swap(y0), y1)
        return 0

    lax.fori_loop(0, 16, collect, 0)
    colg_next[...] = colg_wide[...].astype(B16).reshape(8, 32, 128)
    colg_depth_c = copies(COLG_DEPTH, "depth", lambda k: colg_next.at[k], lambda m: colg_depth.at[m])
    colg_depth[depth] = colg_next[depth]

    finish(big_plane_c)
    big_part[...] = total(big_plane).reshape(8, 16, 128)
    big_depth_c = copies(BIG_DEPTH, "depth", lambda k: big_part.at[k], lambda m: big_depth.at[m])
    big_depth[depth] = big_part[depth]

    finish(rowg_depth_c)
    for h in range(2):
        for r in range(2):
            rowg[pl.ds(r * 16 + h, 8, stride=2), :] = rowg_depth[pl.ds(r * 2 + h, 8, stride=8), :]
    row_g = rowg[...]
    row_gb = row_g.astype(B16)
    row_fold = jnp.sum(row_g, axis=0, keepdims=True)
    row_fold = row_fold + pltpu.roll(row_fold, 32, 1) + pltpu.roll(row_fold, 64, 1) + pltpu.roll(row_fold, 96, 1)
    finish(colg_depth_c)
    col_g = total(colg_depth)
    col_gb = col_g.astype(B16)
    col_sum = jnp.sum(col_g, axis=1, keepdims=True)
    col_fold = jnp.sum(jnp.where(sub128 == lane128, col_sum, 0.0), axis=0, keepdims=True)
    from_cols = dot(col_gb, w_col, (0, 0))
    for c in range(2):
        scaled_grad[c] = from_cols[:, c * 128 : c * 128 + 128]
    proj_col = dot(col_gb, scaled[...], (1, 0))
    proj_row4 = jnp.zeros((128, 256), F32)
    for g in range(4):
        masked = jnp.where(group == g, row_gb.astype(F32), 0.0).astype(B16)
        more = dot(masked, w_row4, (1, 0))
        for c in range(2):
            spot = (c, pl.ds(g, 32, stride=4), slice(None))
            scaled_grad[spot] = scaled_grad[spot] + more[:, c * 128 : c * 128 + 128]
        proj_row4 = proj_row4 + dot(masked, every_fourth(g), (0, 0))
    proj_row = proj_row4[0:32] + proj_row4[32:64] + proj_row4[64:96] + proj_row4[96:128]
    grad = jnp.concatenate([scaled_grad[0], scaled_grad[1]], axis=1)
    norm = normed[...]
    gain_grad = jnp.sum(grad * norm, axis=0, keepdims=True)
    shift_grad = jnp.sum(grad, axis=0, keepdims=True)
    small_in[pl.ds(0, 32), :] = proj_row[:, :128]
    small_in[pl.ds(32, 32), :] = proj_col[:, :128]
    small_in[pl.ds(64, 32), :] = proj_row[:, 128:]
    small_in[pl.ds(96, 32), :] = proj_col[:, 128:]
    small_in[pl.ds(128, 64), :] = jnp.zeros((64, 128), F32)
    small_in[pl.ds(128, 1), :] = gain_grad[:, :128]
    small_in[pl.ds(129, 1), :] = gain_grad[:, 128:]
    small_in[pl.ds(130, 1), :] = shift_grad[:, :128]
    small_in[pl.ds(131, 1), :] = shift_grad[:, 128:]
    small_in[pl.ds(132, 1), :] = row_fold
    small_in[pl.ds(133, 1), :] = col_fold

    def strip(ref, k):
        return ref.at[pl.ds(pl.multiple_of(k * 24, 8), 24)]

    small_plane_c = copies(SMALL_PLANE, "plane", lambda k: strip(small_in, k), lambda m: small_plane.at[m])
    small_plane[plane] = small_in[pl.ds(pl.multiple_of(plane * 24, 8), 24), :]

    inv = inverse[...][:, :1]
    gained = grad * gain_ref[...]
    align = inv * (
        gained
        - jnp.mean(gained, axis=-1, keepdims=True)
        - norm * jnp.mean(gained * norm, axis=-1, keepdims=True)
    )
    align_out[...] = align.astype(B16)

    finish(big_depth_c)
    big_two[...] = total(big_depth)
    big_narrow_c = copies(BIG_NARROW, "narrow", lambda k: big_two, lambda m: big_narrow.at[m])
    big_narrow[narrow] = big_two[...]

    finish(small_plane_c)
    small_part[...] = total(small_plane)
    small_depth_c = copies(SMALL_DEPTH, "depth", lambda k: small_part, lambda m: small_depth.at[m])
    small_depth[depth] = small_part[...]

    finish(big_narrow_c)
    big_three[...] = total(big_narrow)
    big_back_c = copies(BIG_BACK, "depth", lambda k: big_three, lambda m: big_back.at[m])
    big_back[depth] = big_three[...]

    finish(small_depth_c)
    small_two[...] = total(small_depth)
    small_narrow_c = copies(SMALL_NARROW, "narrow", lambda k: small_two, lambda m: small_narrow.at[m])
    small_narrow[narrow] = small_two[...]

    finish(big_back_c)
    big_half[...] = big_back[...].astype(B16).reshape(128, 128)
    big_out_c = copies(BIG_OUT, "plane", lambda k: big_half, lambda m: big_out.at[m])
    big_out[plane] = big_half[...]

    finish(small_narrow_c)
    small_three[...] = total(small_narrow)
    small_out_c = copies(SMALL_OUT, "plane", lambda k: small_three, lambda m: strip(small_all, m))
    small_all[pl.ds(pl.multiple_of(plane * 24, 8), 24), :] = small_three[...]

    finish(small_out_c)
    proj_out[:, pl.ds(0, 128)] = small_all[pl.ds(0, 64), :]
    proj_out[:, pl.ds(128, 128)] = small_all[pl.ds(64, 64), :]
    norm_out[:, pl.ds(0, 128)] = small_all[pl.ds(128, 2, stride=2), :]
    norm_out[:, pl.ds(128, 128)] = small_all[pl.ds(129, 2, stride=2), :]
    bias_out[...] = small_all[pl.ds(132, 2), pl.ds(0, 32)]
    finish(big_out_c)


def everything(x, pair, gain, shift, weight, bias, out_weight):
    vmem = pl.BlockSpec(memory_space=pltpu.VMEM)
    scratch = [
        ((128, 256), F32), ((128, 256), B16), ((2, 128, 128), F32), ((128, 128), F32), ((32, 128), F32),
        ((64, 128), F32), ((32, 128), B16), ((64, 128), F32), ((8, 32, 128), B16), ((256, 128), F32),
        ((2, 16, 128), B16), ((16, 16, 128), B16),
        ((8, 2, 16, 128), B16), ((8, 16, 16, 128), B16), ((512, 128), B16), ((1024, 128), F32),
        ((32, 32, 128), B16), ((16, 128, 256), B16), ((256, 128), B16), ((128, 256), B16),
        ((16, 256, 256), B16), ((32, 32, 512), B16),
        ((8, 16, 16, 128), B16), ((8, 16, 16, 128), B16), ((128, 256), F32), ((8, 2, 16, 128), B16),
        ((8, 2, 16, 128), B16), ((64, 128), F32), ((64, 128), F32), ((32, 128), F32),
        ((256, 128), F32), ((8, 32, 128), B16), ((8, 32, 128), B16), ((2, 128, 128), F32),
        ((8, 128, 128), B16), ((8, 128, 128), B16), ((8, 16, 128), F32), ((8, 16, 128), F32), ((16, 128), F32),
        ((8, 16, 128), F32), ((16, 128), F32), ((8, 16, 128), F32), ((128, 128), B16),
        ((192, 128), F32), ((8, 24, 128), F32), ((24, 128), F32), ((8, 24, 128), F32), ((24, 128), F32),
        ((8, 24, 128), F32), ((24, 128), F32), ((192, 128), F32),
    ]
    return pl.pallas_call(
        kernel,
        out_shape=(
            jax.ShapeDtypeStruct((128, 256), B16),
            jax.ShapeDtypeStruct((64, 256), F32),
            jax.ShapeDtypeStruct((2, 32), F32),
            jax.ShapeDtypeStruct((2, 256), F32),
            jax.ShapeDtypeStruct((8, 128, 128), B16),
        ),
        in_specs=[vmem] * 7,
        out_specs=(vmem,) * 5,
        scratch_shapes=[pltpu.VMEM(shape, kind) for shape, kind in scratch]
        + [pltpu.SemaphoreType.DMA((STAGES, 8)), pltpu.SemaphoreType.DMA((STAGES, 8))],
        compiler_params=pltpu.CompilerParams(
            collective_id=0, has_side_effects=True, vmem_limit_bytes=56 * 1024 * 1024
        ),
    )(x, pair, gain, shift, weight, bias, out_weight)


def shards(
    alignment_rows,
    pair_output_gradient,
    layer_norm_gain,
    layer_norm_bias,
    projection_weight,
    projection_bias,
    output_weight,
):
    align, proj, bias, norm, big = everything(
        alignment_rows.reshape(128, 256),
        pair_output_gradient.reshape(512, 128),
        layer_norm_gain.reshape(1, 256),
        layer_norm_bias.reshape(1, 256),
        jnp.transpose(projection_weight, (0, 2, 1)).reshape(64, 256),
        projection_bias,
        output_weight,
    )
    weight_grad = jnp.transpose(big.reshape(32, 32, 128), (1, 0, 2)).reshape(1024, 128)
    return (
        align.reshape(2, 64, 256),
        jnp.transpose(proj.reshape(2, 32, 256), (0, 2, 1)),
        bias,
        weight_grad.astype(F32),
        norm,
    )


def solution(mesh):
    return jax.shard_map(
        shards,
        mesh=mesh,
        in_specs=(P("wide", "narrow", None), P("wide", "narrow", None), P(), P(), P(), P(), P()),
        out_specs=(P("wide", "narrow", None), P(), P(), P(), P()),
        check_vma=False,
    )
```

```python
import jax
import jax.numpy as jnp
from jax import lax
from jax.experimental import pallas as pl
from jax.experimental.pallas import tpu as pltpu
from jax.sharding import PartitionSpec as P

F32, B16 = jnp.float32, jnp.bfloat16
MESH_ID = pl.DeviceIdType.MESH
OFFSETS = (4, 3, 5, 2, 6, 1, 7)
STAGES = 17
SEQUENCES = 128
(
    ROW_DEPTH, COL_DEPTH, ROW_PAIR, COL_PLANE, COLG_PLANE, ROWG_PAIR, BIG_PLANE, ROWG_DEPTH, COLG_DEPTH,
    BIG_DEPTH, SMALL_PLANE, BIG_NARROW, SMALL_DEPTH, BIG_BACK, SMALL_NARROW, BIG_OUT, SMALL_OUT,
) = range(STAGES)


def dot(a, b, dims):
    return lax.dot_general(a, b, ((dims[:1], dims[1:]), ((), ())), preferred_element_type=F32)


def total(ref):
    acc = ref[0].astype(F32)
    for k in range(1, 8):
        acc = acc + ref[k].astype(F32)
    return acc


def lanes(shape):
    return lax.broadcasted_iota(jnp.int32, shape, len(shape) - 1)


def half_swap(x):
    return pltpu.roll(x, 64, 1)


def kernel(
    x_ref, pair_hbm, gain_ref, shift_ref, weight_ref, bias_ref, out_weight_hbm,
    align_out, proj_out, bias_out, norm_out, weight_out,
    normed, scaled, scaled32, inverse, row_tmp,
    row_send, col_send, row_got, col_got, col_wide, row_next, col_next,
    row_pair, col_plane, pair_ref, out_weight_ref, pair_two, weight32, weight_order, upstream, rows, rows_t, outer,
    colg_send, colg_got, rowg_send, rowg_got, rowg_next, rowg_depth, rowg,
    colg_wide, colg_next, colg_depth, scaled_grad,
    big_send, big_plane, big_part, big_depth, big_two, big_narrow, big_three, big_back, big_half, big_all,
    small_in, small_plane, small_part, small_depth, small_two, small_narrow, small_three, small_all,
    send_sem, recv_sem, local_sem,
):
    wide = lax.axis_index("wide")
    narrow = lax.axis_index("narrow")
    plane = wide // 8
    depth = wide % 8
    own_pair = plane == narrow
    other_pair = plane != narrow
    barrier = pltpu.get_barrier_semaphore()
    fetch_pair = pltpu.make_async_copy(pair_hbm, pair_ref, local_sem.at[0])
    fetch_weight = pltpu.make_async_copy(out_weight_hbm, out_weight_ref, local_sem.at[1])
    fetch_pair.start()
    fetch_weight.start()
    place = {"plane": plane, "depth": depth, "narrow": narrow}

    def peer(kind, k):
        if kind == "plane":
            return (k * 8 + depth, narrow)
        if kind == "depth":
            return (plane * 8 + k, narrow)
        return (wide, k)

    def holder(d):
        return (narrow * 8 + depth, (narrow + d) % 8)

    def source(d):
        return (((plane + d) % 8) * 8 + depth, plane)

    def greet(device):
        pl.semaphore_signal(barrier, 1, device_id=device, device_id_type=MESH_ID)

    for kind in ("plane", "depth", "narrow"):
        for d in OFFSETS:
            greet(peer(kind, (place[kind] + d) % 8))
    for d in range(1, 8):
        greet(holder(d))
        greet(source(d))

    @pl.when(other_pair)
    def _():
        greet(holder(0))
        greet(source(0))

    def copies(stage, kind, give, target):
        me = place[kind]
        made = []
        for d in OFFSETS:
            k = (me + d) % 8
            c = pltpu.make_async_remote_copy(
                src_ref=give(k),
                dst_ref=target(me),
                send_sem=send_sem.at[stage, d],
                recv_sem=recv_sem.at[stage, d],
                device_id=peer(kind, k),
                device_id_type=MESH_ID,
            )
            c.start()
            made.append(c)
        return made

    def finish(made):
        for c in made:
            c.wait()

    def pair_copies(stage, device, tag, give, target, own):
        made = []
        for d in range(8):
            c = pltpu.make_async_remote_copy(
                src_ref=give(d),
                dst_ref=target.at[tag],
                send_sem=send_sem.at[stage, d],
                recv_sem=recv_sem.at[stage, tag],
                device_id=device(d),
                device_id_type=MESH_ID,
            )
            k = (tag + d) % 8
            arrival = pltpu.make_async_remote_copy(
                src_ref=give(d),
                dst_ref=target.at[k],
                send_sem=send_sem.at[stage, d],
                recv_sem=recv_sem.at[stage, k],
                device_id=device(d),
                device_id_type=MESH_ID,
            )
            made.append((c, arrival))
        for c, _ in made[1:]:
            c.start()

        @pl.when(other_pair)
        def _():
            made[0][0].start()

        @pl.when(own_pair)
        def _():
            own()

        return made

    def pair_finish(made):
        for c, arrival in made[1:]:
            c.wait_send()
            arrival.wait_recv()

        @pl.when(other_pair)
        def _():
            made[0][0].wait_send()
            made[0][1].wait_recv()

    value = x_ref[...].astype(F32)
    centre = value - jnp.mean(value, axis=-1, keepdims=True)
    inv = lax.rsqrt(jnp.mean(centre * centre, axis=-1, keepdims=True) + 1e-05)
    norm = centre * inv
    inverse[...] = jnp.broadcast_to(inv, (128, 128))
    normed[...] = norm
    scaled_b = (norm * gain_ref[...] + shift_ref[...]).astype(B16)
    scaled[...] = scaled_b
    for c in range(2):
        scaled32[c] = scaled_b[:, c * 128 : c * 128 + 128].astype(F32)

    def every_fourth(g):
        both = [scaled32[c, pl.ds(g, 32, stride=4), :] for c in range(2)]
        return jnp.concatenate(both, axis=1).astype(B16)

    w_row = weight_ref[0:32, :]
    w_col = weight_ref[32:64, :]
    w_row4 = jnp.concatenate([w_row] * 4, axis=0)
    sub = lax.broadcasted_iota(jnp.int32, (32, 32), 0)
    diagonal = sub == lanes((32, 32))
    row_bias = jnp.sum(jnp.where(diagonal, bias_ref[0:1, :], 0.0), axis=1, keepdims=True)
    col_bias = jnp.sum(jnp.where(diagonal, bias_ref[1:2, :], 0.0), axis=1, keepdims=True)
    lane128 = lanes((32, 128))
    sub128 = lax.broadcasted_iota(jnp.int32, (32, 128), 0)
    row_bias4 = jnp.sum(jnp.where(sub128 == lane128 % 32, row_bias, 0.0), axis=0, keepdims=True)
    group = lane128 // 32
    row_fac = jnp.zeros((32, 128), F32)
    for g in range(4):
        row_fac = jnp.where(group == g, dot(every_fourth(g), w_row4, (1, 1)), row_fac)
    row_tmp[...] = (row_fac + row_bias4).astype(B16).astype(F32)
    row_send[...] = jnp.zeros((64, 128), F32)
    for r in range(2):
        for h in range(2):
            row_send[pl.ds(r * 2 + h, 8, stride=8), :] = row_tmp[pl.ds(r * 16 + h, 8, stride=2), :]
    col_send[...] = (dot(w_col, scaled_b, (1, 1)) + col_bias).astype(B16)
    pl.semaphore_wait(barrier, jnp.where(other_pair, 37, 35))

    def eight(ref, k):
        return ref.at[pl.ds(pl.multiple_of(k * 8, 8), 8)]

    row_depth_c = copies(ROW_DEPTH, "depth", lambda k: eight(row_send, k), lambda m: eight(row_got, m))
    col_depth_c = copies(COL_DEPTH, "depth", lambda k: col_send, lambda m: col_got.at[m])
    mine = pl.ds(pl.multiple_of(depth * 8, 8), 8)
    row_got[mine, :] = row_send[mine, :]
    col_got[depth] = col_send[...]

    fetch_weight.wait()
    weight32[...] = out_weight_ref[...].astype(F32)
    for q in range(32):
        weight_order[pl.ds(q * 32, 32), :] = weight32[pl.ds(q, 32, stride=32), :].astype(B16)
    fetch_pair.wait()
    low32 = lane128 < 64

    def up(c, _):
        w = weight_order[pl.ds(pl.multiple_of(c * 256, 256), 256), :]
        res = dot(w, pair_ref[...], (1, 1))
        for b in range(4):
            for i in range(4):
                even = res[b * 64 : b * 64 + 32, i * 128 : i * 128 + 128]
                odd = res[b * 64 + 32 : b * 64 + 64, i * 128 : i * 128 + 128]
                spot = (c * 2 + b // 2, pl.ds(i * 64, 64), pl.ds((b % 2) * 128, 128))
                first = jnp.where(low32, even, half_swap(odd))
                second = jnp.where(low32, half_swap(even), odd)
                upstream[spot] = jnp.concatenate([first, second], axis=0).astype(B16)
        return 0

    lax.fori_loop(0, 4, up, 0)

    finish(row_depth_c)
    for h in range(2):
        both = [row_got[pl.ds(r * 2 + h, 8, stride=8), :] for r in range(2)]
        row_next[h] = jnp.concatenate(both, axis=0).astype(B16)

    def keep_row():
        row_pair[plane] = row_next[...]

    row_pair_c = pair_copies(ROW_PAIR, holder, plane, lambda d: row_next, row_pair, keep_row)

    finish(col_depth_c)
    col_wide[...] = col_got[...].astype(F32).reshape(256, 128)
    low8 = lanes((8, 128)) < 64

    for b in range(16):
        x0 = col_wide[pl.ds(b * 2, 8, stride=32), :]
        x1 = col_wide[pl.ds(b * 2 + 1, 8, stride=32), :]
        r0 = jnp.where(low8, x0, half_swap(x1))
        r1 = jnp.where(low8, half_swap(x0), x1)
        col_next[b] = jnp.concatenate([r0, r1], axis=0).astype(B16)
    col_plane_c = copies(COL_PLANE, "plane", lambda k: col_next, lambda m: col_plane.at[m])
    col_plane[plane] = col_next[...]

    pair_finish(row_pair_c)
    for h in range(2):
        rows[:, pl.ds(h * 128, 128)] = row_pair[:, h].reshape(128, 128)
    for t in range(8):
        r = (dot(rows[...], upstream[t], (1, 0)) * (1.0 / SEQUENCES)).astype(B16)
        for h in range(2):
            colg_send[:, t * 2 + h] = r[:, h * 128 : h * 128 + 128].reshape(8, 16, 128)
    colg_plane_c = copies(COLG_PLANE, "plane", lambda k: colg_send.at[k], lambda m: colg_got.at[m])
    colg_got[plane] = colg_send[plane]
    rows_t[...] = rows[...].astype(F32).T.astype(B16)
    pair_two[...] = jnp.zeros((1024, 256), B16)
    for i in range(8):
        for h in range(2):
            pair_two[pl.ds(i * 128 + h * 64, 64), pl.ds(h * 128, 128)] = pair_ref[pl.ds(i * 64, 64), :]

    finish(col_plane_c)

    def col_tile(t):
        both = [col_plane[:, t * 2 + h].reshape(128, 128) for h in range(2)]
        return jnp.concatenate(both, axis=1)

    row_part = dot(col_tile(0), upstream[0], (1, 1))
    for t in range(1, 8):
        row_part = row_part + dot(col_tile(t), upstream[t], (1, 1))
    row_part = (row_part * (1.0 / SEQUENCES)).astype(B16)
    for h in range(2):
        rowg_send[:, h] = row_part[:, h * 128 : h * 128 + 128].reshape(8, 16, 128)

    def keep_rowg():
        rowg_got[narrow] = rowg_send[plane]

    rowg_pair_c = pair_copies(
        ROWG_PAIR, source, narrow, lambda d: rowg_send.at[(plane + d) % 8], rowg_got, keep_rowg
    )

    for t in range(8):
        o = (dot(rows_t[...], col_tile(t), (1, 0)) * (1.0 / SEQUENCES)).astype(B16)
        for h in range(2):
            for i in range(8):
                outer[t * 2 + h, :, pl.ds(i * 128, 128)] = o[i * 32 : i * 32 + 32, h * 128 : h * 128 + 128]
    for c in range(2):
        res = dot(outer[pl.ds(c * 8, 8)].reshape(256, 1024), pair_two[...], (1, 0)).astype(B16)
        for k in range(4):
            for h in range(2):
                big_send[c * 4 + k, pl.ds(h * 64, 64), :] = res[k * 64 : k * 64 + 64, h * 128 : h * 128 + 128]
    big_plane_c = copies(BIG_PLANE, "plane", lambda k: big_send.at[k], lambda m: big_plane.at[m])
    big_plane[plane] = big_send[plane]

    pair_finish(rowg_pair_c)
    row_sum = total(rowg_got)
    rowg_next[...] = jnp.zeros((64, 128), F32)
    for h in range(2):
        for r in range(2):
            rowg_next[pl.ds(r * 2 + h, 8, stride=8), :] = row_sum[h, r * 8 : r * 8 + 8, :]
    rowg_depth_c = copies(ROWG_DEPTH, "depth", lambda k: eight(rowg_next, k), lambda m: eight(rowg_depth, m))
    rowg_depth[mine, :] = rowg_next[mine, :]

    finish(colg_plane_c)

    for b in range(16):
        acc = colg_got[0, b].astype(F32)
        for k in range(1, 8):
            acc = acc + colg_got[k, b].astype(F32)
        y0, y1 = acc[:8], acc[8:]
        colg_wide[pl.ds(b * 2, 8, stride=32), :] = jnp.where(low8, y0, half_swap(y1))
        colg_wide[pl.ds(b * 2 + 1, 8, stride=32), :] = jnp.where(low8, half_swap(y0), y1)
    colg_next[...] = colg_wide[...].astype(B16).reshape(8, 32, 128)
    colg_depth_c = copies(COLG_DEPTH, "depth", lambda k: colg_next.at[k], lambda m: colg_depth.at[m])
    colg_depth[depth] = colg_next[depth]

    finish(big_plane_c)
    big_part[...] = total(big_plane).reshape(8, 16, 128)
    big_depth_c = copies(BIG_DEPTH, "depth", lambda k: big_part.at[k], lambda m: big_depth.at[m])
    big_depth[depth] = big_part[depth]

    finish(rowg_depth_c)
    for h in range(2):
        for r in range(2):
            rowg[pl.ds(r * 16 + h, 8, stride=2), :] = rowg_depth[pl.ds(r * 2 + h, 8, stride=8), :]
    row_g = rowg[...]
    row_gb = row_g.astype(B16)
    row_fold = jnp.sum(row_g, axis=0, keepdims=True)
    row_fold = row_fold + pltpu.roll(row_fold, 32, 1) + pltpu.roll(row_fold, 64, 1) + pltpu.roll(row_fold, 96, 1)
    finish(colg_depth_c)
    col_g = total(colg_depth)
    col_gb = col_g.astype(B16)
    col_sum = jnp.sum(col_g, axis=1, keepdims=True)
    col_fold = jnp.sum(jnp.where(sub128 == lane128, col_sum, 0.0), axis=0, keepdims=True)
    from_cols = dot(col_gb, w_col, (0, 0))
    for c in range(2):
        scaled_grad[c] = from_cols[:, c * 128 : c * 128 + 128]
    proj_col = dot(col_gb, scaled[...], (1, 0))
    proj_row4 = jnp.zeros((128, 256), F32)
    for g in range(4):
        masked = jnp.where(group == g, row_gb.astype(F32), 0.0).astype(B16)
        more = dot(masked, w_row4, (1, 0))
        for c in range(2):
            spot = (c, pl.ds(g, 32, stride=4), slice(None))
            scaled_grad[spot] = scaled_grad[spot] + more[:, c * 128 : c * 128 + 128]
        proj_row4 = proj_row4 + dot(masked, every_fourth(g), (0, 0))
    proj_row = proj_row4[0:32] + proj_row4[32:64] + proj_row4[64:96] + proj_row4[96:128]
    grad = jnp.concatenate([scaled_grad[0], scaled_grad[1]], axis=1)
    norm = normed[...]
    gain_grad = jnp.sum(grad * norm, axis=0, keepdims=True)
    shift_grad = jnp.sum(grad, axis=0, keepdims=True)
    small_in[pl.ds(0, 32), :] = proj_row[:, :128]
    small_in[pl.ds(32, 32), :] = proj_col[:, :128]
    small_in[pl.ds(64, 32), :] = proj_row[:, 128:]
    small_in[pl.ds(96, 32), :] = proj_col[:, 128:]
    small_in[pl.ds(128, 64), :] = jnp.zeros((64, 128), F32)
    small_in[pl.ds(128, 1), :] = gain_grad[:, :128]
    small_in[pl.ds(129, 1), :] = gain_grad[:, 128:]
    small_in[pl.ds(130, 1), :] = shift_grad[:, :128]
    small_in[pl.ds(131, 1), :] = shift_grad[:, 128:]
    small_in[pl.ds(132, 1), :] = row_fold
    small_in[pl.ds(133, 1), :] = col_fold

    def strip(ref, k):
        return ref.at[pl.ds(pl.multiple_of(k * 24, 8), 24)]

    small_plane_c = copies(SMALL_PLANE, "plane", lambda k: strip(small_in, k), lambda m: small_plane.at[m])
    small_plane[plane] = small_in[pl.ds(pl.multiple_of(plane * 24, 8), 24), :]

    inv = inverse[...][:, :1]
    gained = grad * gain_ref[...]
    align = inv * (
        gained
        - jnp.mean(gained, axis=-1, keepdims=True)
        - norm * jnp.mean(gained * norm, axis=-1, keepdims=True)
    )
    align_out[...] = align.astype(B16)

    finish(big_depth_c)
    big_two[...] = total(big_depth)
    big_narrow_c = copies(BIG_NARROW, "narrow", lambda k: big_two, lambda m: big_narrow.at[m])
    big_narrow[narrow] = big_two[...]

    finish(small_plane_c)
    small_part[...] = total(small_plane).astype(B16)
    small_depth_c = copies(SMALL_DEPTH, "depth", lambda k: small_part, lambda m: small_depth.at[m])
    small_depth[depth] = small_part[...]

    finish(big_narrow_c)
    big_three[...] = total(big_narrow)
    big_back_c = copies(BIG_BACK, "depth", lambda k: big_three, lambda m: big_back.at[m])
    big_back[depth] = big_three[...]

    finish(small_depth_c)
    small_two[...] = total(small_depth).astype(B16)
    small_narrow_c = copies(SMALL_NARROW, "narrow", lambda k: small_two, lambda m: small_narrow.at[m])
    small_narrow[narrow] = small_two[...]

    finish(big_back_c)
    big_half[...] = big_back[...].astype(B16).reshape(128, 128)
    big_out_c = copies(BIG_OUT, "plane", lambda k: big_half, lambda m: big_all.at[m])
    big_all[plane] = big_half[...]

    finish(small_narrow_c)
    small_three[...] = total(small_narrow).astype(B16)
    small_out_c = copies(SMALL_OUT, "plane", lambda k: small_three, lambda m: small_all.at[m])
    small_all[plane] = small_three[...]

    finish(big_out_c)
    for k in range(8):
        for h in range(2):
            for b in range(2):
                piece = big_all[k, pl.ds((h * 2 + b) * 32, 32), :].astype(F32)
                weight_out[pl.ds(k * 4 + b * 2 + h, 32, stride=32), :] = piece
    finish(small_out_c)
    small = small_all[...].astype(F32).reshape(192, 128)
    proj_out[:, pl.ds(0, 128)] = small[0:64]
    proj_out[:, pl.ds(128, 128)] = small[64:128]
    norm_out[0:1, pl.ds(0, 128)] = small[128:129]
    norm_out[0:1, pl.ds(128, 128)] = small[129:130]
    norm_out[1:2, pl.ds(0, 128)] = small[130:131]
    norm_out[1:2, pl.ds(128, 128)] = small[131:132]
    bias_out[...] = small[132:134, :32]


def put_kernel(*refs):
    sem = refs[10]
    made = [pltpu.make_async_copy(refs[k], refs[5 + k], sem.at[k]) for k in range(5)]
    for c in made:
        c.start()
    for c in made:
        c.wait()


def put(results):
    return pl.pallas_call(
        put_kernel,
        out_shape=tuple(jax.ShapeDtypeStruct(r.shape, r.dtype) for r in results),
        in_specs=[pl.BlockSpec(memory_space=pltpu.VMEM)] * 5,
        out_specs=(pl.BlockSpec(memory_space=pl.ANY),) * 5,
        scratch_shapes=[pltpu.SemaphoreType.DMA((5,))],
    )(*[pltpu.with_memory_space_constraint(r, pltpu.VMEM) for r in results])


def everything(x, pair, gain, shift, weight, bias, out_weight):
    vmem = pl.BlockSpec(memory_space=pltpu.VMEM)
    hbm = pl.BlockSpec(memory_space=pl.ANY)
    scratch = [
        ((128, 256), F32), ((128, 256), B16), ((2, 128, 128), F32), ((128, 128), F32), ((32, 128), F32),
        ((64, 128), F32), ((32, 128), B16), ((64, 128), F32), ((8, 32, 128), B16), ((256, 128), F32),
        ((2, 16, 128), B16), ((16, 16, 128), B16),
        ((8, 2, 16, 128), B16), ((8, 16, 16, 128), B16), ((512, 128), B16), ((1024, 128), B16), ((1024, 256), B16),
        ((1024, 128), F32), ((1024, 128), B16), ((8, 256, 256), B16), ((128, 256), B16), ((256, 128), B16),
        ((16, 32, 1024), B16),
        ((8, 16, 16, 128), B16), ((8, 16, 16, 128), B16), ((8, 2, 16, 128), B16),
        ((8, 2, 16, 128), B16), ((64, 128), F32), ((64, 128), F32), ((32, 128), F32),
        ((256, 128), F32), ((8, 32, 128), B16), ((8, 32, 128), B16), ((2, 128, 128), F32),
        ((8, 128, 128), B16), ((8, 128, 128), B16), ((8, 16, 128), F32), ((8, 16, 128), F32), ((16, 128), F32),
        ((8, 16, 128), F32), ((16, 128), F32), ((8, 16, 128), F32), ((128, 128), B16),
        ((8, 128, 128), B16),
        ((192, 128), F32), ((8, 24, 128), F32), ((24, 128), B16), ((8, 24, 128), B16), ((24, 128), B16),
        ((8, 24, 128), B16), ((24, 128), B16), ((8, 24, 128), B16),
    ]
    return pl.pallas_call(
        kernel,
        out_shape=(
            pltpu.VMEM((128, 256), B16),
            pltpu.VMEM((64, 256), F32),
            pltpu.VMEM((2, 32), F32),
            pltpu.VMEM((2, 256), F32),
            pltpu.VMEM((1024, 128), F32),
        ),
        in_specs=[vmem, hbm, vmem, vmem, vmem, vmem, hbm],
        out_specs=(vmem,) * 5,
        scratch_shapes=[pltpu.VMEM(shape, kind) for shape, kind in scratch]
        + [pltpu.SemaphoreType.DMA((STAGES, 8)), pltpu.SemaphoreType.DMA((STAGES, 8)), pltpu.SemaphoreType.DMA((2,))],
        compiler_params=pltpu.CompilerParams(
            collective_id=0, has_side_effects=True, vmem_limit_bytes=56 * 1024 * 1024
        ),
    )(x, pair, gain, shift, weight, bias, out_weight)


def shards(
    alignment_rows,
    pair_output_gradient,
    layer_norm_gain,
    layer_norm_bias,
    projection_weight,
    projection_bias,
    output_weight,
):
    results = everything(
        alignment_rows.reshape(128, 256),
        pair_output_gradient.reshape(512, 128),
        layer_norm_gain.reshape(1, 256),
        layer_norm_bias.reshape(1, 256),
        jnp.transpose(projection_weight, (0, 2, 1)).reshape(64, 256),
        projection_bias,
        output_weight,
    )
    align, proj, bias, norm, weight_grad = put(results)
    return (
        align.reshape(2, 64, 256),
        jnp.transpose(proj.reshape(2, 32, 256), (0, 2, 1)),
        bias,
        weight_grad,
        norm,
    )


def solution(mesh):
    return jax.shard_map(
        shards,
        mesh=mesh,
        in_specs=(P("wide", "narrow", None), P("wide", "narrow", None), P(), P(), P(), P(), P()),
        out_specs=(P("wide", "narrow", None), P(), P(), P(), P()),
        check_vma=False,
    )
```

```python
import jax
import jax.numpy as jnp
from jax import lax
from jax.experimental import pallas as pl
from jax.experimental.pallas import tpu as pltpu
from jax.sharding import PartitionSpec as P

F32, B16 = jnp.float32, jnp.bfloat16
MESH_ID = pl.DeviceIdType.MESH
OFFSETS = (4, 3, 5, 2, 6, 1, 7)
STAGES = 20
SEQUENCES = 128
(
    ROW_DEPTH, COL_DEPTH, ROW_PAIR, COL_PLANE, COLG_PLANE, ROWG_PAIR, BIG_PLANE, ROWG_DEPTH, COLG_DEPTH,
    BIG_DEPTH, SMALL_PLANE, BIG_NARROW, SMALL_DEPTH, BIG_BACK, SMALL_NARROW, BIG_OUT, SMALL_OUT,
    PAIR_HALF, ROW_CORE, ROWG_CORE,
) = range(STAGES)


def dot(a, b, dims):
    return lax.dot_general(a, b, ((dims[:1], dims[1:]), ((), ())), preferred_element_type=F32)


def total(ref):
    acc = ref[0].astype(F32)
    for k in range(1, 8):
        acc = acc + ref[k].astype(F32)
    return acc


def lanes(shape):
    return lax.broadcasted_iota(jnp.int32, shape, len(shape) - 1)


def half_swap(x):
    return pltpu.roll(x, 64, 1)


def kernel(
    x_ref, pair_hbm, gain_ref, shift_ref, weight_ref, bias_ref, out_weight_hbm,
    align_out, proj_out, bias_out, norm_out, weight_out,
    normed, scaled, scaled32, inverse, row_tmp,
    row_send, col_send, row_got, col_got, col_wide, row_next, col_next,
    row_pair, col_plane, pair_ref, pair_tile, out_weight_ref, pair_two, weight32, weight_order, upstream, rows, rows_t, outer,
    colg_send, colg_got, rowg_acc, rowg_core, rowg_sum, rowg_send, rowg_got, rowg_next, rowg_depth, rowg,
    colg_wide, colg_next, colg_depth, scaled_grad,
    big_send, big_plane, big_part, big_depth, big_two, big_narrow, big_three, big_back, big_half, big_all,
    small_in, small_plane, small_part, small_depth, small_two, small_narrow, small_three, small_all,
    send_sem, recv_sem, local_sem,
):
    wide = lax.axis_index("wide")
    narrow = lax.axis_index("narrow")
    plane = wide // 8
    depth = wide % 8
    own_pair = plane == narrow
    other_pair = plane != narrow
    lead = plane % 2 == narrow % 2
    follow = plane % 2 != narrow % 2
    barrier = pltpu.get_barrier_semaphore()
    fetch_pair = pltpu.make_async_copy(pair_hbm, pair_ref, local_sem.at[0])
    fetch_weight = pltpu.make_async_copy(out_weight_hbm, out_weight_ref, local_sem.at[1])
    fetch_pair.start()
    fetch_weight.start()
    place = {"plane": plane, "depth": depth, "narrow": narrow}

    def peer(kind, k):
        if kind == "plane":
            return (k * 8 + depth, narrow)
        if kind == "depth":
            return (plane * 8 + k, narrow)
        return (wide, k)

    def holder(d):
        return (narrow * 8 + depth, (narrow + 2 * d) % 8)

    def source(d):
        return (((plane + d) % 8) * 8 + depth, plane)

    def greet(device):
        pl.semaphore_signal(barrier, 1, device_id=device, device_id_type=MESH_ID)

    for kind in ("plane", "depth", "narrow"):
        for d in OFFSETS:
            greet(peer(kind, (place[kind] + d) % 8))
    for d in range(1, 4):
        greet(holder(d))

    @pl.when(lead)
    def _():
        for d in range(1, 8):
            greet(source(d))

    @pl.when(lead & other_pair)
    def _():
        greet(source(0))

    @pl.when(other_pair)
    def _():
        greet(holder(0))

    def copies(stage, kind, give, target, size=1):
        me = place[kind]
        lead = pl.ds(pl.multiple_of(me * size, size), size) if size > 1 else me
        for d in OFFSETS:
            k = (me + d) % 8
            pltpu.make_async_remote_copy(
                src_ref=give(k),
                dst_ref=target.at[lead],
                send_sem=send_sem.at[stage],
                recv_sem=recv_sem.at[stage],
                device_id=peer(kind, k),
                device_id_type=MESH_ID,
            ).start()
        whole = target.at[pl.ds(0, 7 * size)]
        return pltpu.make_async_remote_copy(
            src_ref=whole,
            dst_ref=whole,
            send_sem=send_sem.at[stage],
            recv_sem=recv_sem.at[stage],
            device_id=peer(kind, (me + 1) % 8),
            device_id_type=MESH_ID,
        )

    def finish(c):
        c.wait()

    def sent(stage, device, source_ref, target_ref):
        return pltpu.make_async_remote_copy(
            src_ref=source_ref,
            dst_ref=target_ref,
            send_sem=send_sem.at[stage],
            recv_sem=recv_sem.at[stage],
            device_id=device,
            device_id_type=MESH_ID,
        )

    partner = (wide, narrow + 1 - 2 * (narrow % 2))

    def for_own(what):
        pl.when(own_pair)(lambda: what(True))
        pl.when(other_pair)(lambda: what(False))

    value = x_ref[...].astype(F32)
    centre = value - jnp.mean(value, axis=-1, keepdims=True)
    inv = lax.rsqrt(jnp.mean(centre * centre, axis=-1, keepdims=True) + 1e-05)
    norm = centre * inv
    inverse[...] = jnp.broadcast_to(inv, (128, 128))
    normed[...] = norm
    scaled_b = (norm * gain_ref[...] + shift_ref[...]).astype(B16)
    scaled[...] = scaled_b
    for c in range(2):
        scaled32[c] = scaled_b[:, c * 128 : c * 128 + 128].astype(F32)

    def every_fourth(g):
        both = [scaled32[c, pl.ds(g, 32, stride=4), :] for c in range(2)]
        return jnp.concatenate(both, axis=1).astype(B16)

    w_row = weight_ref[0:32, :]
    w_col = weight_ref[32:64, :]
    w_row4 = jnp.concatenate([w_row] * 4, axis=0)
    sub = lax.broadcasted_iota(jnp.int32, (32, 32), 0)
    diagonal = sub == lanes((32, 32))
    row_bias = jnp.sum(jnp.where(diagonal, bias_ref[0:1, :], 0.0), axis=1, keepdims=True)
    col_bias = jnp.sum(jnp.where(diagonal, bias_ref[1:2, :], 0.0), axis=1, keepdims=True)
    lane128 = lanes((32, 128))
    sub128 = lax.broadcasted_iota(jnp.int32, (32, 128), 0)
    row_bias4 = jnp.sum(jnp.where(sub128 == lane128 % 32, row_bias, 0.0), axis=0, keepdims=True)
    group = lane128 // 32
    row_fac = jnp.zeros((32, 128), F32)
    for g in range(4):
        row_fac = jnp.where(group == g, dot(every_fourth(g), w_row4, (1, 1)), row_fac)
    row_tmp[...] = (row_fac + row_bias4).astype(B16).astype(F32)
    for g in range(4):
        for r in range(2):
            row_send[pl.ds(g * 8 + r * 4, 4), :] = row_tmp[pl.ds(r * 16 + g * 4, 4), :]
    even_lane = lanes((16, 128)) // 32 % 2 == 0
    col_fac = dot(w_col, scaled_b, (1, 1)) + col_bias
    fac_a, fac_b = col_fac[:16], col_fac[16:]
    col_send[0] = jnp.where(even_lane, fac_a, pltpu.roll(fac_b, 32, 1)).astype(B16)
    col_send[1] = jnp.where(even_lane, pltpu.roll(fac_a, 96, 1), fac_b).astype(B16)
    pl.semaphore_wait(barrier, 25 + jnp.where(lead, 8, 0) - jnp.where(own_pair, 2, 0))

    def eight(ref, k):
        return ref.at[pl.ds(pl.multiple_of(k * 8, 8), 8)]

    parity = depth % 2
    row_depth_c = copies(ROW_DEPTH, "depth", lambda k: eight(row_send, k // 2), row_got, 8)
    col_depth_c = copies(COL_DEPTH, "depth", lambda k: col_send.at[k % 2], col_got)
    mine = pl.ds(pl.multiple_of(depth * 8, 8), 8)
    row_got[mine, :] = row_send[pl.ds(pl.multiple_of(depth // 2 * 8, 8), 8), :]
    col_got[depth] = col_send[parity]
    fetch_pair.wait()
    own_rows = pl.ds(pl.multiple_of(parity * 8, 8), 8)
    pair_half_c = pltpu.make_async_remote_copy(
        src_ref=pair_ref.at[:, pl.ds(pl.multiple_of((1 - parity) * 32, 32), 32)],
        dst_ref=pair_tile.at[own_rows],
        send_sem=send_sem.at[PAIR_HALF],
        recv_sem=recv_sem.at[PAIR_HALF],
        device_id=peer("depth", depth + 1 - 2 * parity),
        device_id_type=MESH_ID,
    )
    pair_half_c.start()
    pair_tile[own_rows] = pair_ref[:, pl.ds(pl.multiple_of(parity * 32, 32), 32), :]

    fetch_weight.wait()
    weight32[...] = out_weight_ref[...].astype(F32)
    for b in range(8):
        for c in range(4):
            q = c % 2 * 16 + b * 2 + c // 2
            weight_order[pl.ds((b * 4 + c) * 32, 32), :] = weight32[pl.ds(q, 32, stride=32), :].astype(B16)

    finish(row_depth_c)
    for g in range(4):
        both = [row_got[pl.ds(r * 4 + g, 8, stride=8), :] for r in range(2)]
        row_next[g] = jnp.concatenate(both, axis=0).astype(B16)

    for d in range(1, 4):
        sent(ROW_PAIR, holder(d), row_next, row_pair.at[plane]).start()

    @pl.when(other_pair)
    def _():
        sent(ROW_PAIR, holder(0), row_next, row_pair.at[plane]).start()

    @pl.when(own_pair)
    def _():
        row_pair[plane] = row_next[...]

    finish(col_depth_c)
    col_wide[...] = col_got[...].astype(F32).reshape(128, 128)
    low8 = lanes((8, 128)) < 64

    for b in range(8):
        x0 = col_wide[pl.ds(b * 2, 8, stride=16), :]
        x1 = col_wide[pl.ds(b * 2 + 1, 8, stride=16), :]
        r0 = jnp.where(low8, x0, half_swap(x1))
        r1 = jnp.where(low8, half_swap(x0), x1)
        col_next[b] = jnp.concatenate([r0, r1], axis=0).astype(B16)
    col_plane_c = copies(COL_PLANE, "plane", lambda k: col_next, col_plane)
    col_plane[plane] = col_next[...]

    low32 = lane128 < 64
    even32 = group % 2 == 0
    pair_half_c.wait()

    def up(t, _):
        tile = pair_tile[...].reshape(512, 128)
        for h in range(2):
            w = weight_order[pl.ds(pl.multiple_of(t * 256 + h * 128, 128), 128), :]
            res = dot(w, tile, (1, 1))
            for i in range(4):
                a = [res[c * 32 : c * 32 + 32, i * 128 : i * 128 + 128] for c in range(4)]
                first = [jnp.where(low32, a[c], half_swap(a[c + 2])) for c in range(2)]
                second = [jnp.where(low32, half_swap(a[c]), a[c + 2]) for c in range(2)]
                out = []
                for f in (first, second):
                    out.append(jnp.where(even32, f[0], pltpu.roll(f[1], 32, 1)))
                    out.append(jnp.where(even32, pltpu.roll(f[0], 96, 1), f[1]))
                upstream[t, pl.ds(i * 128, 128), pl.ds(h * 128, 128)] = jnp.concatenate(out, axis=0).astype(B16)
        return 0

    lax.fori_loop(0, 4, up, 0)

    pair_two[...] = jnp.zeros((2048, 512), B16)
    for i in range(16):
        for c in range(4):
            pair_two[pl.ds(i * 128 + c * 32, 32), pl.ds(c * 128, 128)] = pair_tile[i]

    def sent_rows(own):
        part = row_pair.at[pl.ds(0, 3 if own else 4)]
        sent(ROW_PAIR, partner, part, part).wait_send()

    for_own(sent_rows)

    @pl.when(lead)
    def _():
        def came(own):
            part = row_pair.at[pl.ds(0, 7 if own else 8)]
            sent(ROW_PAIR, partner, part, part).wait_recv()

        for_own(came)
        sent(ROW_CORE, partner, row_pair, row_pair).start()

    @pl.when(follow)
    def _():
        sent(ROW_CORE, partner, row_pair, row_pair).wait_recv()

    for g in range(4):
        rows[:, pl.ds(g * 128, 128)] = row_pair[:, g].reshape(128, 128)
    for t in range(4):
        r = (dot(rows[...], upstream[t], (1, 0)) * (1.0 / SEQUENCES)).astype(B16)
        for h in range(2):
            colg_send[:, t * 2 + h] = r[:, h * 128 : h * 128 + 128].reshape(8, 16, 128)
    colg_plane_c = copies(COLG_PLANE, "plane", lambda k: colg_send.at[k], colg_got)
    colg_got[plane] = colg_send[plane]
    rows_t[...] = rows[...].astype(F32).T.astype(B16)
    finish(col_plane_c)

    def col_tile(t):
        both = [col_plane[:, t * 2 + h].reshape(128, 128) for h in range(2)]
        return jnp.concatenate(both, axis=1)

    row_part = dot(col_tile(0), upstream[0], (1, 1))
    for t in range(1, 4):
        row_part = row_part + dot(col_tile(t), upstream[t], (1, 1))
    row_part = row_part * (1.0 / SEQUENCES)
    rowg_acc[...] = row_part
    row_part = row_part.astype(B16)
    for g in range(4):
        rowg_send[:, g] = row_part[:, g * 128 : g * 128 + 128].reshape(8, 16, 128)

    @pl.when(follow)
    def _():
        sent(ROWG_CORE, partner, rowg_send, rowg_core).start()

    for t in range(4):
        o = (dot(rows_t[...], col_tile(t), (1, 0)) * (1.0 / SEQUENCES)).astype(B16)
        for h in range(2):
            for i in range(16):
                outer[t * 2 + h, :, pl.ds(i * 128, 128)] = o[i * 32 : i * 32 + 32, h * 128 : h * 128 + 128]

    @pl.when(lead)
    def _():
        sent(ROWG_CORE, partner, rowg_send, rowg_core).wait_recv()
        for g in range(4):
            both = rowg_acc[:, pl.ds(g * 128, 128)] + rowg_core[:, g].reshape(128, 128).astype(F32)
            rowg_sum[:, g] = both.astype(B16).reshape(8, 16, 128)
        for d in range(1, 8):
            sent(ROWG_PAIR, source(d), rowg_sum.at[(plane + d) % 8], rowg_got.at[narrow // 2]).start()

    @pl.when(lead & other_pair)
    def _():
        sent(ROWG_PAIR, source(0), rowg_sum.at[plane], rowg_got.at[narrow // 2]).start()

    @pl.when(own_pair)
    def _():
        rowg_got[narrow // 2] = rowg_sum[plane]

    for g in range(2):
        res = dot(outer[pl.ds(g * 4, 4)].reshape(128, 2048), pair_two[...], (1, 0)).astype(B16)
        for k in range(4):
            for c in range(4):
                big_send[g * 4 + k, pl.ds(c * 32, 32), :] = res[k * 32 : k * 32 + 32, c * 128 : c * 128 + 128]
    big_plane_c = copies(BIG_PLANE, "plane", lambda k: big_send.at[k], big_plane)
    big_plane[plane] = big_send[plane]

    def came_rowg(own):
        part = rowg_got.at[pl.ds(0, 3 if own else 4)]
        sent(ROWG_PAIR, partner, part, part).wait_recv()

    for_own(came_rowg)
    row_sum = rowg_got[0].astype(F32)
    for k in range(1, 4):
        row_sum = row_sum + rowg_got[k].astype(F32)
    for g in range(4):
        for r in range(2):
            rowg_next[pl.ds(r * 4 + g, 8, stride=8), :] = row_sum[g, r * 8 : r * 8 + 8, :]
    rowg_depth_c = copies(ROWG_DEPTH, "depth", lambda k: eight(rowg_next, k), rowg_depth, 8)
    rowg_depth[mine, :] = rowg_next[mine, :]

    finish(colg_plane_c)

    for b in range(8):
        acc = colg_got[0, b].astype(F32)
        for k in range(1, 8):
            acc = acc + colg_got[k, b].astype(F32)
        y0, y1 = acc[:8], acc[8:]
        colg_wide[pl.ds(b * 2, 8, stride=16), :] = jnp.where(low8, y0, half_swap(y1))
        colg_wide[pl.ds(b * 2 + 1, 8, stride=16), :] = jnp.where(low8, half_swap(y0), y1)
    colg_next[...] = colg_wide[...].astype(B16).reshape(8, 16, 128)
    colg_depth_c = copies(COLG_DEPTH, "depth", lambda k: colg_next.at[k], colg_depth)
    colg_depth[depth] = colg_next[depth]

    finish(big_plane_c)
    big_part[...] = total(big_plane).astype(B16).reshape(8, 16, 128)
    big_depth_c = copies(BIG_DEPTH, "depth", lambda k: big_part.at[k], big_depth)
    big_depth[depth] = big_part[depth]

    finish(rowg_depth_c)
    for g in range(4):
        for r in range(2):
            one = rowg_depth[pl.ds(g * 16 + r * 4, 4), :] + rowg_depth[pl.ds(g * 16 + 8 + r * 4, 4), :]
            rowg[pl.ds(r * 16 + g * 4, 4), :] = one
    row_g = rowg[...]
    row_gb = row_g.astype(B16)
    row_fold = jnp.sum(row_g, axis=0, keepdims=True)
    row_fold = row_fold + pltpu.roll(row_fold, 32, 1) + pltpu.roll(row_fold, 64, 1) + pltpu.roll(row_fold, 96, 1)
    finish(colg_depth_c)
    half = []
    for h in range(2):
        one = colg_depth[h].astype(F32)
        for k in range(1, 4):
            one = one + colg_depth[k * 2 + h].astype(F32)
        half.append(one)
    col_g = jnp.concatenate(
        [
            jnp.where(even_lane, half[0], pltpu.roll(half[1], 32, 1)),
            jnp.where(even_lane, pltpu.roll(half[0], 96, 1), half[1]),
        ],
        axis=0,
    )
    col_gb = col_g.astype(B16)
    col_sum = jnp.sum(col_g, axis=1, keepdims=True)
    col_fold = jnp.sum(jnp.where(sub128 == lane128, col_sum, 0.0), axis=0, keepdims=True)
    from_cols = dot(col_gb, w_col, (0, 0))
    for c in range(2):
        scaled_grad[c] = from_cols[:, c * 128 : c * 128 + 128]
    proj_col = dot(col_gb, scaled[...], (1, 0))
    proj_row4 = jnp.zeros((128, 256), F32)
    for g in range(4):
        masked = jnp.where(group == g, row_gb.astype(F32), 0.0).astype(B16)
        more = dot(masked, w_row4, (1, 0))
        for c in range(2):
            spot = (c, pl.ds(g, 32, stride=4), slice(None))
            scaled_grad[spot] = scaled_grad[spot] + more[:, c * 128 : c * 128 + 128]
        proj_row4 = proj_row4 + dot(masked, every_fourth(g), (0, 0))
    proj_row = proj_row4[0:32] + proj_row4[32:64] + proj_row4[64:96] + proj_row4[96:128]
    grad = jnp.concatenate([scaled_grad[0], scaled_grad[1]], axis=1)
    norm = normed[...]
    gain_grad = jnp.sum(grad * norm, axis=0, keepdims=True)
    shift_grad = jnp.sum(grad, axis=0, keepdims=True)
    small_in[pl.ds(0, 32), :] = proj_row[:, :128]
    small_in[pl.ds(32, 32), :] = proj_col[:, :128]
    small_in[pl.ds(64, 32), :] = proj_row[:, 128:]
    small_in[pl.ds(96, 32), :] = proj_col[:, 128:]
    small_in[pl.ds(128, 64), :] = jnp.zeros((64, 128), F32)
    small_in[pl.ds(128, 1), :] = gain_grad[:, :128]
    small_in[pl.ds(129, 1), :] = gain_grad[:, 128:]
    small_in[pl.ds(130, 1), :] = shift_grad[:, :128]
    small_in[pl.ds(131, 1), :] = shift_grad[:, 128:]
    small_in[pl.ds(132, 1), :] = row_fold
    small_in[pl.ds(133, 1), :] = col_fold

    def strip(ref, k):
        return ref.at[pl.ds(pl.multiple_of(k * 24, 8), 24)]

    small_plane_c = copies(SMALL_PLANE, "plane", lambda k: strip(small_in, k), small_plane)
    small_plane[plane] = small_in[pl.ds(pl.multiple_of(plane * 24, 8), 24), :]

    inv = inverse[...][:, :1]
    gained = grad * gain_ref[...]
    align = inv * (
        gained
        - jnp.mean(gained, axis=-1, keepdims=True)
        - norm * jnp.mean(gained * norm, axis=-1, keepdims=True)
    )
    align_out[...] = align.astype(B16)

    finish(big_depth_c)
    big_two[...] = total(big_depth).astype(B16)
    big_narrow_c = copies(BIG_NARROW, "narrow", lambda k: big_two, big_narrow)
    big_narrow[narrow] = big_two[...]

    finish(small_plane_c)
    small_part[...] = total(small_plane).astype(B16)
    small_depth_c = copies(SMALL_DEPTH, "depth", lambda k: small_part, small_depth)
    small_depth[depth] = small_part[...]

    finish(big_narrow_c)
    big_three[...] = total(big_narrow).astype(B16)
    big_back_c = copies(BIG_BACK, "depth", lambda k: big_three, big_back)
    big_back[depth] = big_three[...]

    finish(small_depth_c)
    small_two[...] = total(small_depth).astype(B16)
    small_narrow_c = copies(SMALL_NARROW, "narrow", lambda k: small_two, small_narrow)
    small_narrow[narrow] = small_two[...]

    finish(big_back_c)
    big_half[...] = big_back[...].reshape(128, 128)
    big_out_c = copies(BIG_OUT, "plane", lambda k: big_half, big_all)
    big_all[plane] = big_half[...]

    finish(small_narrow_c)
    small_three[...] = total(small_narrow).astype(B16)
    small_out_c = copies(SMALL_OUT, "plane", lambda k: small_three, small_all)
    small_all[plane] = small_three[...]

    finish(big_out_c)
    for k in range(8):
        for c in range(4):
            piece = big_all[k, pl.ds(c * 32, 32), :].astype(F32)
            weight_out[pl.ds(c % 2 * 16 + k * 2 + c // 2, 32, stride=32), :] = piece
    @pl.when(lead)
    def _():
        sent(ROW_CORE, partner, row_pair, row_pair).wait_send()

        def sent_sums(own):
            part = rowg_sum.at[pl.ds(0, 7 if own else 8)]
            sent(ROWG_PAIR, partner, part, part).wait_send()

        for_own(sent_sums)

    @pl.when(follow)
    def _():
        sent(ROWG_CORE, partner, rowg_send, rowg_core).wait_send()

    finish(small_out_c)
    small = small_all[...].astype(F32).reshape(192, 128)
    proj_out[:, pl.ds(0, 128)] = small[0:64]
    proj_out[:, pl.ds(128, 128)] = small[64:128]
    norm_out[0:1, pl.ds(0, 128)] = small[128:129]
    norm_out[0:1, pl.ds(128, 128)] = small[129:130]
    norm_out[1:2, pl.ds(0, 128)] = small[130:131]
    norm_out[1:2, pl.ds(128, 128)] = small[131:132]
    bias_out[...] = small[132:134, :32]


def put_kernel(*refs):
    sem = refs[10]
    made = [pltpu.make_async_copy(refs[k], refs[5 + k], sem.at[k]) for k in range(5)]
    for c in made:
        c.start()
    for c in made:
        c.wait()


def put(results):
    return pl.pallas_call(
        put_kernel,
        out_shape=tuple(jax.ShapeDtypeStruct(r.shape, r.dtype) for r in results),
        in_specs=[pl.BlockSpec(memory_space=pltpu.VMEM)] * 5,
        out_specs=(pl.BlockSpec(memory_space=pl.ANY),) * 5,
        scratch_shapes=[pltpu.SemaphoreType.DMA((5,))],
    )(*[pltpu.with_memory_space_constraint(r, pltpu.VMEM) for r in results])


def everything(x, pair, gain, shift, weight, bias, out_weight):
    vmem = pl.BlockSpec(memory_space=pltpu.VMEM)
    hbm = pl.BlockSpec(memory_space=pl.ANY)
    scratch = [
        ((128, 256), F32), ((128, 256), B16), ((2, 128, 128), F32), ((128, 128), F32), ((32, 128), F32),
        ((32, 128), F32), ((2, 16, 128), B16), ((64, 128), F32), ((8, 16, 128), B16), ((128, 128), F32),
        ((4, 16, 128), B16), ((8, 16, 128), B16),
        ((8, 4, 16, 128), B16), ((8, 8, 16, 128), B16), ((8, 64, 128), B16), ((16, 32, 128), B16), ((1024, 128), B16),
        ((2048, 512), B16), ((1024, 128), F32), ((1024, 128), B16), ((4, 512, 256), B16), ((128, 512), B16),
        ((512, 128), B16), ((8, 32, 2048), B16),
        ((8, 8, 16, 128), B16), ((8, 8, 16, 128), B16), ((128, 512), F32), ((8, 4, 16, 128), B16), ((8, 4, 16, 128), B16),
        ((8, 4, 16, 128), B16),
        ((4, 4, 16, 128), B16), ((64, 128), F32), ((64, 128), F32), ((32, 128), F32),
        ((128, 128), F32), ((8, 16, 128), B16), ((8, 16, 128), B16), ((2, 128, 128), F32),
        ((8, 128, 128), B16), ((8, 128, 128), B16), ((8, 16, 128), B16), ((8, 16, 128), B16), ((16, 128), B16),
        ((8, 16, 128), B16), ((16, 128), B16), ((8, 16, 128), B16), ((128, 128), B16),
        ((8, 128, 128), B16),
        ((192, 128), F32), ((8, 24, 128), F32), ((24, 128), B16), ((8, 24, 128), B16), ((24, 128), B16),
        ((8, 24, 128), B16), ((24, 128), B16), ((8, 24, 128), B16),
    ]
    return pl.pallas_call(
        kernel,
        out_shape=(
            pltpu.VMEM((128, 256), B16),
            pltpu.VMEM((64, 256), F32),
            pltpu.VMEM((2, 32), F32),
            pltpu.VMEM((2, 256), F32),
            pltpu.VMEM((1024, 128), F32),
        ),
        in_specs=[vmem, hbm, vmem, vmem, vmem, vmem, hbm],
        out_specs=(vmem,) * 5,
        scratch_shapes=[pltpu.VMEM(shape, kind) for shape, kind in scratch]
        + [pltpu.SemaphoreType.DMA((STAGES,)), pltpu.SemaphoreType.DMA((STAGES,)), pltpu.SemaphoreType.DMA((2,))],
        compiler_params=pltpu.CompilerParams(
            collective_id=0, has_side_effects=True, vmem_limit_bytes=56 * 1024 * 1024
        ),
    )(x, pair, gain, shift, weight, bias, out_weight)


def shards(
    alignment_rows,
    pair_output_gradient,
    layer_norm_gain,
    layer_norm_bias,
    projection_weight,
    projection_bias,
    output_weight,
):
    results = everything(
        alignment_rows.reshape(128, 256),
        pair_output_gradient,
        layer_norm_gain.reshape(1, 256),
        layer_norm_bias.reshape(1, 256),
        jnp.transpose(projection_weight, (0, 2, 1)).reshape(64, 256),
        projection_bias,
        output_weight,
    )
    align, proj, bias, norm, weight_grad = put(results)
    return (
        align.reshape(2, 64, 256),
        jnp.transpose(proj.reshape(2, 32, 256), (0, 2, 1)),
        bias,
        weight_grad,
        norm,
    )


def solution(mesh):
    return jax.shard_map(
        shards,
        mesh=mesh,
        in_specs=(P("wide", "narrow", None), P("wide", "narrow", None), P(), P(), P(), P(), P()),
        out_specs=(P("wide", "narrow", None), P(), P(), P(), P()),
        check_vma=False,
    )
```

```python
import jax
import jax.numpy as jnp
from jax import lax
from jax.experimental import pallas as pl
from jax.experimental.pallas import tpu as pltpu
from jax.sharding import PartitionSpec as P

F32, B16 = jnp.float32, jnp.bfloat16
MESH_ID = pl.DeviceIdType.MESH
OFFSETS = {"depth": (4, 3, 5, 2, 6, 1, 7), "narrow": (4, 3, 5, 2, 6, 1, 7), "plane": (6, 5, 7, 4, 2, 1, 3)}
STAGES = 22
SEQUENCES = 128
(
    ROW_DEPTH, COL_DEPTH, ROW_PAIR, COL_PLANE, COLG_PLANE, ROWG_PAIR, BIG_PLANE, ROWG_DEPTH, COLG_DEPTH,
    BIG_DEPTH, SMALL_PLANE, BIG_NARROW, SMALL_DEPTH, BIG_BACK, SMALL_NARROW, BIG_OUT, SMALL_OUT,
    PAIR_HALF, ROW_CORE, ROWG_CORE, BIG_CORE, BIG_JOIN,
) = range(STAGES)


def dot(a, b, dims):
    return lax.dot_general(a, b, ((dims[:1], dims[1:]), ((), ())), preferred_element_type=F32)


def total(ref):
    acc = ref[0].astype(F32)
    for k in range(1, 8):
        acc = acc + ref[k].astype(F32)
    return acc


def lanes(shape):
    return lax.broadcasted_iota(jnp.int32, shape, len(shape) - 1)


def half_swap(x):
    return pltpu.roll(x, 64, 1)


def kernel(
    x_hbm, pair_hbm, gain_hbm, shift_hbm, weight_hbm, bias_hbm, out_weight_hbm,
    align_out, proj_out, bias_out, norm_out, weight_out,
    x_ref, gain_ref, shift_ref, weight_ref, bias_ref,
    normed, scaled, scaled32, inverse, row_tmp,
    row_send, col_send, row_got, col_got, col_wide, row_next, col_next,
    row_pair, col_plane, pair_ref, pair_tile, out_weight_ref, pair_two, weight32, weight_order, upstream, rows, rows_t, outer,
    colg_send, colg_got, rowg_acc, rowg_core, rowg_sum, rowg_send, rowg_got, rowg_next, rowg_depth, rowg,
    colg_wide, colg_next, colg_depth, scaled_grad,
    big_send, big_core, big_one, big_depth, big_part, big_plane, big_two, big_narrow, big_three, big_back, big_half,
    big_most, big_rest,
    small_in, small_plane, small_part, small_depth, small_two, small_narrow, small_three, small_all,
    send_sem, recv_sem, local_sem, ready,
):
    wide = lax.axis_index("wide")
    narrow = lax.axis_index("narrow")
    plane = wide // 8
    depth = wide % 8
    own_pair = plane == narrow
    other_pair = plane != narrow
    lead = plane % 2 == narrow % 2
    follow = plane % 2 != narrow % 2
    barrier = pltpu.get_barrier_semaphore()
    inputs = (
        (x_hbm, x_ref), (gain_hbm, gain_ref), (shift_hbm, shift_ref), (weight_hbm, weight_ref), (bias_hbm, bias_ref),
        (pair_hbm, pair_ref), (out_weight_hbm, out_weight_ref),
    )
    fetches = [pltpu.make_async_copy(a, b, local_sem.at[k]) for k, (a, b) in enumerate(inputs)]
    for c in fetches:
        c.start()
    fetch_pair, fetch_weight = fetches[5:]
    place = {"plane": plane, "depth": depth, "narrow": narrow}

    def peer(kind, k):
        if kind == "plane":
            return (k * 8 + depth, narrow)
        if kind == "depth":
            return (plane * 8 + k, narrow)
        return (wide, k)

    def holder(d):
        return (narrow * 8 + depth, (narrow + 2 * d) % 8)

    def source(d):
        return (((plane + d) % 8) * 8 + depth, plane)

    def greet(device):
        pl.semaphore_signal(barrier, 1, device_id=device, device_id_type=MESH_ID)

    for kind in ("plane", "depth", "narrow"):
        for d in OFFSETS[kind]:
            greet(peer(kind, (place[kind] + d) % 8))
    def copies(stage, kind, give, target, size=1):
        me = place[kind]
        lead = pl.ds(pl.multiple_of(me * size, size), size) if size > 1 else me
        for d in OFFSETS[kind]:
            k = (me + d) % 8
            pltpu.make_async_remote_copy(
                src_ref=give(k),
                dst_ref=target.at[lead],
                send_sem=send_sem.at[stage],
                recv_sem=recv_sem.at[stage],
                device_id=peer(kind, k),
                device_id_type=MESH_ID,
            ).start()
        whole = target.at[pl.ds(0, 7 * size)]
        return pltpu.make_async_remote_copy(
            src_ref=whole,
            dst_ref=whole,
            send_sem=send_sem.at[stage],
            recv_sem=recv_sem.at[stage],
            device_id=peer(kind, (me + 1) % 8),
            device_id_type=MESH_ID,
        )

    def finish(c):
        c.wait()

    def sent(stage, device, source_ref, target_ref):
        return pltpu.make_async_remote_copy(
            src_ref=source_ref,
            dst_ref=target_ref,
            send_sem=send_sem.at[stage],
            recv_sem=recv_sem.at[stage],
            device_id=device,
            device_id_type=MESH_ID,
        )

    partner = (wide, narrow + 1 - 2 * (narrow % 2))

    def for_own(what):
        pl.when(own_pair)(lambda: what(True))
        pl.when(other_pair)(lambda: what(False))

    for c in fetches[:5]:
        c.wait()
    value = x_ref[...].astype(F32)
    centre = value - jnp.mean(value, axis=-1, keepdims=True)
    inv = lax.rsqrt(jnp.mean(centre * centre, axis=-1, keepdims=True) + 1e-05)
    norm = centre * inv
    inverse[...] = jnp.broadcast_to(inv, (128, 128))
    normed[...] = norm
    scaled_b = (norm * gain_ref[...] + shift_ref[...]).astype(B16)
    scaled[...] = scaled_b
    for c in range(2):
        scaled32[c] = scaled_b[:, c * 128 : c * 128 + 128].astype(F32)

    def every_fourth(g):
        both = [scaled32[c, pl.ds(g, 32, stride=4), :] for c in range(2)]
        return jnp.concatenate(both, axis=1).astype(B16)

    w_row = weight_ref[0:32, :]
    w_col = weight_ref[32:64, :]
    w_row4 = jnp.concatenate([w_row] * 4, axis=0)
    sub = lax.broadcasted_iota(jnp.int32, (32, 32), 0)
    diagonal = sub == lanes((32, 32))
    row_bias = jnp.sum(jnp.where(diagonal, bias_ref[0:1, :], 0.0), axis=1, keepdims=True)
    col_bias = jnp.sum(jnp.where(diagonal, bias_ref[1:2, :], 0.0), axis=1, keepdims=True)
    lane128 = lanes((32, 128))
    sub128 = lax.broadcasted_iota(jnp.int32, (32, 128), 0)
    row_bias4 = jnp.sum(jnp.where(sub128 == lane128 % 32, row_bias, 0.0), axis=0, keepdims=True)
    group = lane128 // 32
    row_fac = jnp.zeros((32, 128), F32)
    for g in range(4):
        row_fac = jnp.where(group == g, dot(every_fourth(g), w_row4, (1, 1)), row_fac)
    row_tmp[...] = (row_fac + row_bias4).astype(B16).astype(F32)
    for g in range(4):
        for r in range(2):
            row_send[pl.ds(g * 8 + r * 4, 4), :] = row_tmp[pl.ds(r * 16 + g * 4, 4), :]
    even_lane = lanes((16, 128)) // 32 % 2 == 0
    col_fac = dot(w_col, scaled_b, (1, 1)) + col_bias
    fac_a, fac_b = col_fac[:16], col_fac[16:]
    col_send[0] = jnp.where(even_lane, fac_a, pltpu.roll(fac_b, 32, 1)).astype(B16)
    col_send[1] = jnp.where(even_lane, pltpu.roll(fac_a, 96, 1), fac_b).astype(B16)
    pl.semaphore_wait(barrier, 21)
    for d in (2, 4, 6):
        pl.semaphore_signal(ready, 1, device_id=(wide, (narrow + d) % 8), device_id_type=MESH_ID)


    def eight(ref, k):
        return ref.at[pl.ds(pl.multiple_of(k * 8, 8), 8)]

    parity = depth % 2
    row_depth_c = copies(ROW_DEPTH, "depth", lambda k: eight(row_send, k // 2), row_got, 8)
    col_depth_c = copies(COL_DEPTH, "depth", lambda k: col_send.at[k % 2], col_got)
    mine = pl.ds(pl.multiple_of(depth * 8, 8), 8)
    row_got[mine, :] = row_send[pl.ds(pl.multiple_of(depth // 2 * 8, 8), 8), :]
    col_got[depth] = col_send[parity]
    fetch_weight.wait()
    weight32[...] = out_weight_ref[...].astype(F32)
    for b in range(8):
        for c in range(4):
            q = c % 2 * 16 + b * 2 + c // 2
            weight_order[pl.ds((b * 4 + c) * 32, 32), :] = weight32[pl.ds(q, 32, stride=32), :].astype(B16)

    finish(row_depth_c)
    for g in range(4):
        both = [row_got[pl.ds(r * 4 + g, 8, stride=8), :] for r in range(2)]
        row_next[g] = jnp.concatenate(both, axis=0).astype(B16)

    pl.semaphore_wait(ready, 3)
    for d in (2, 1, 3):
        sent(ROW_PAIR, holder(d), row_next, row_pair.at[plane]).start()

    @pl.when(other_pair)
    def _():
        sent(ROW_PAIR, holder(0), row_next, row_pair.at[plane]).start()

    @pl.when(own_pair)
    def _():
        row_pair[plane] = row_next[...]

    fetch_pair.wait()
    own_rows = pl.ds(pl.multiple_of(parity * 8, 8), 8)
    pair_half_c = pltpu.make_async_remote_copy(
        src_ref=pair_ref.at[:, pl.ds(pl.multiple_of((1 - parity) * 32, 32), 32)],
        dst_ref=pair_tile.at[own_rows],
        send_sem=send_sem.at[PAIR_HALF],
        recv_sem=recv_sem.at[PAIR_HALF],
        device_id=peer("depth", depth + 1 - 2 * parity),
        device_id_type=MESH_ID,
    )
    pair_half_c.start()
    pair_tile[own_rows] = pair_ref[:, pl.ds(pl.multiple_of(parity * 32, 32), 32), :]

    finish(col_depth_c)
    col_wide[...] = col_got[...].astype(F32).reshape(128, 128)
    low8 = lanes((8, 128)) < 64

    for b in range(8):
        x0 = col_wide[pl.ds(b * 2, 8, stride=16), :]
        x1 = col_wide[pl.ds(b * 2 + 1, 8, stride=16), :]
        r0 = jnp.where(low8, x0, half_swap(x1))
        r1 = jnp.where(low8, half_swap(x0), x1)
        col_next[b] = jnp.concatenate([r0, r1], axis=0).astype(B16)
    col_plane_c = copies(COL_PLANE, "plane", lambda k: col_next, col_plane)
    col_plane[plane] = col_next[...]

    low32 = lane128 < 64
    even32 = group % 2 == 0
    pair_half_c.wait()

    def up(t, _):
        tile = pair_tile[...].reshape(512, 128)
        for h in range(2):
            w = weight_order[pl.ds(pl.multiple_of(t * 256 + h * 128, 128), 128), :]
            res = dot(w, tile, (1, 1))
            for i in range(4):
                a = [res[c * 32 : c * 32 + 32, i * 128 : i * 128 + 128] for c in range(4)]
                first = [jnp.where(low32, a[c], half_swap(a[c + 2])) for c in range(2)]
                second = [jnp.where(low32, half_swap(a[c]), a[c + 2]) for c in range(2)]
                out = []
                for f in (first, second):
                    out.append(jnp.where(even32, f[0], pltpu.roll(f[1], 32, 1)))
                    out.append(jnp.where(even32, pltpu.roll(f[0], 96, 1), f[1]))
                upstream[t, pl.ds(i * 128, 128), pl.ds(h * 128, 128)] = jnp.concatenate(out, axis=0).astype(B16)
        return 0

    lax.fori_loop(0, 4, up, 0)

    pair_two[...] = jnp.zeros((2048, 512), B16)
    for i in range(16):
        for c in range(4):
            pair_two[pl.ds(i * 128 + c * 32, 32), pl.ds(c * 128, 128)] = pair_tile[i]

    def sent_rows(own):
        part = row_pair.at[pl.ds(0, 3 if own else 4)]
        sent(ROW_PAIR, partner, part, part).wait_send()

    for_own(sent_rows)

    @pl.when(lead)
    def _():
        def came(own):
            part = row_pair.at[pl.ds(0, 7 if own else 8)]
            sent(ROW_PAIR, partner, part, part).wait_recv()

        for_own(came)
        sent(ROW_CORE, partner, row_pair, row_pair).start()

    @pl.when(follow)
    def _():
        sent(ROW_CORE, partner, row_pair, row_pair).wait_recv()

    for g in range(4):
        rows[:, pl.ds(g * 128, 128)] = row_pair[:, g].reshape(128, 128)
    for t in range(4):
        r = (dot(rows[...], upstream[t], (1, 0)) * (1.0 / SEQUENCES)).astype(B16)
        for h in range(2):
            colg_send[:, t * 2 + h] = r[:, h * 128 : h * 128 + 128].reshape(8, 16, 128)
    colg_plane_c = copies(COLG_PLANE, "plane", lambda k: colg_send.at[k], colg_got)
    colg_got[plane] = colg_send[plane]
    rows_t[...] = rows[...].astype(F32).T.astype(B16)
    finish(col_plane_c)

    def col_tile(t):
        both = [col_plane[:, t * 2 + h].reshape(128, 128) for h in range(2)]
        return jnp.concatenate(both, axis=1)

    row_part = dot(col_tile(0), upstream[0], (1, 1))
    for t in range(1, 4):
        row_part = row_part + dot(col_tile(t), upstream[t], (1, 1))
    row_part = row_part * (1.0 / SEQUENCES)
    rowg_acc[...] = row_part
    row_part = row_part.astype(B16)
    for g in range(4):
        rowg_send[:, g] = row_part[:, g * 128 : g * 128 + 128].reshape(8, 16, 128)

    @pl.when(follow)
    def _():
        sent(ROWG_CORE, partner, rowg_send, rowg_core).start()

    for t in range(4):
        o = (dot(rows_t[...], col_tile(t), (1, 0)) * (1.0 / SEQUENCES)).astype(B16)
        for h in range(2):
            for i in range(16):
                outer[t * 2 + h, :, pl.ds(i * 128, 128)] = o[i * 32 : i * 32 + 32, h * 128 : h * 128 + 128]

    @pl.when(lead)
    def _():
        sent(ROWG_CORE, partner, rowg_send, rowg_core).wait_recv()
        for g in range(4):
            both = rowg_acc[:, pl.ds(g * 128, 128)] + rowg_core[:, g].reshape(128, 128).astype(F32)
            rowg_sum[:, g] = both.astype(B16).reshape(8, 16, 128)
        for d in range(1, 8):
            sent(ROWG_PAIR, source(d), rowg_sum.at[(plane + d) % 8], rowg_got.at[narrow // 2]).start()

    @pl.when(lead & other_pair)
    def _():
        sent(ROWG_PAIR, source(0), rowg_sum.at[plane], rowg_got.at[narrow // 2]).start()

    @pl.when(own_pair)
    def _():
        rowg_got[narrow // 2] = rowg_sum[plane]

    for g in range(2):
        res = dot(outer[pl.ds(g * 4, 4)].reshape(128, 2048), pair_two[...], (1, 0)).astype(B16)
        for k in range(4):
            for c in range(4):
                big_send[g * 4 + k, pl.ds(c * 32, 32), :] = res[k * 32 : k * 32 + 32, c * 128 : c * 128 + 128]
    core = narrow % 2
    own_half = pl.ds(pl.multiple_of(core * 64, 64), 64)
    other_half = pl.ds(pl.multiple_of(64 - core * 64, 64), 64)
    big_core_c = sent(BIG_CORE, partner, big_send.at[:, other_half], big_core)
    big_core_c.start()
    big_core_c.wait()
    big_one[...] = (big_send[:, own_half, :].astype(F32) + big_core[...].astype(F32)).astype(B16)
    big_depth_c = copies(BIG_DEPTH, "depth", lambda k: big_one.at[k], big_depth)
    big_depth[depth] = big_one[depth]

    def came_rowg(own):
        part = rowg_got.at[pl.ds(0, 3 if own else 4)]
        sent(ROWG_PAIR, partner, part, part).wait_recv()

    for_own(came_rowg)
    row_sum = rowg_got[0].astype(F32)
    for k in range(1, 4):
        row_sum = row_sum + rowg_got[k].astype(F32)
    for g in range(4):
        for r in range(2):
            rowg_next[pl.ds(r * 4 + g, 8, stride=8), :] = row_sum[g, r * 8 : r * 8 + 8, :]
    rowg_depth_c = copies(ROWG_DEPTH, "depth", lambda k: eight(rowg_next, k), rowg_depth, 8)
    rowg_depth[mine, :] = rowg_next[mine, :]

    finish(colg_plane_c)

    for b in range(8):
        acc = colg_got[0, b].astype(F32)
        for k in range(1, 8):
            acc = acc + colg_got[k, b].astype(F32)
        y0, y1 = acc[:8], acc[8:]
        colg_wide[pl.ds(b * 2, 8, stride=16), :] = jnp.where(low8, y0, half_swap(y1))
        colg_wide[pl.ds(b * 2 + 1, 8, stride=16), :] = jnp.where(low8, half_swap(y0), y1)
    colg_next[...] = colg_wide[...].astype(B16).reshape(8, 16, 128)
    colg_depth_c = copies(COLG_DEPTH, "depth", lambda k: colg_next.at[k], colg_depth)
    colg_depth[depth] = colg_next[depth]

    finish(big_depth_c)
    big_part[...] = total(big_depth).astype(B16).reshape(8, 8, 128)
    big_plane_c = copies(BIG_PLANE, "plane", lambda k: big_part.at[k], big_plane)
    big_plane[plane] = big_part[plane]

    finish(rowg_depth_c)
    for g in range(4):
        for r in range(2):
            one = rowg_depth[pl.ds(g * 16 + r * 4, 4), :] + rowg_depth[pl.ds(g * 16 + 8 + r * 4, 4), :]
            rowg[pl.ds(r * 16 + g * 4, 4), :] = one
    row_g = rowg[...]
    row_gb = row_g.astype(B16)
    row_fold = jnp.sum(row_g, axis=0, keepdims=True)
    row_fold = row_fold + pltpu.roll(row_fold, 32, 1) + pltpu.roll(row_fold, 64, 1) + pltpu.roll(row_fold, 96, 1)
    finish(colg_depth_c)
    half = []
    for h in range(2):
        one = colg_depth[h].astype(F32)
        for k in range(1, 4):
            one = one + colg_depth[k * 2 + h].astype(F32)
        half.append(one)
    col_g = jnp.concatenate(
        [
            jnp.where(even_lane, half[0], pltpu.roll(half[1], 32, 1)),
            jnp.where(even_lane, pltpu.roll(half[0], 96, 1), half[1]),
        ],
        axis=0,
    )
    col_gb = col_g.astype(B16)
    col_sum = jnp.sum(col_g, axis=1, keepdims=True)
    col_fold = jnp.sum(jnp.where(sub128 == lane128, col_sum, 0.0), axis=0, keepdims=True)
    from_cols = dot(col_gb, w_col, (0, 0))
    for c in range(2):
        scaled_grad[c] = from_cols[:, c * 128 : c * 128 + 128]
    proj_col = dot(col_gb, scaled[...], (1, 0))
    proj_row4 = jnp.zeros((128, 256), F32)
    for g in range(4):
        masked = jnp.where(group == g, row_gb.astype(F32), 0.0).astype(B16)
        more = dot(masked, w_row4, (1, 0))
        for c in range(2):
            spot = (c, pl.ds(g, 32, stride=4), slice(None))
            scaled_grad[spot] = scaled_grad[spot] + more[:, c * 128 : c * 128 + 128]
        proj_row4 = proj_row4 + dot(masked, every_fourth(g), (0, 0))
    proj_row = proj_row4[0:32] + proj_row4[32:64] + proj_row4[64:96] + proj_row4[96:128]
    grad = jnp.concatenate([scaled_grad[0], scaled_grad[1]], axis=1)
    norm = normed[...]
    gain_grad = jnp.sum(grad * norm, axis=0, keepdims=True)
    shift_grad = jnp.sum(grad, axis=0, keepdims=True)
    small_in[pl.ds(0, 32), :] = proj_row[:, :128]
    small_in[pl.ds(32, 32), :] = proj_col[:, :128]
    small_in[pl.ds(64, 32), :] = proj_row[:, 128:]
    small_in[pl.ds(96, 32), :] = proj_col[:, 128:]
    small_in[pl.ds(128, 64), :] = jnp.zeros((64, 128), F32)
    small_in[pl.ds(128, 1), :] = gain_grad[:, :128]
    small_in[pl.ds(129, 1), :] = gain_grad[:, 128:]
    small_in[pl.ds(130, 1), :] = shift_grad[:, :128]
    small_in[pl.ds(131, 1), :] = shift_grad[:, 128:]
    small_in[pl.ds(132, 1), :] = row_fold
    small_in[pl.ds(133, 1), :] = col_fold

    def strip(ref, k):
        return ref.at[pl.ds(pl.multiple_of(k * 24, 8), 24)]

    small_plane_c = copies(SMALL_PLANE, "plane", lambda k: strip(small_in, k), small_plane)
    small_plane[plane] = small_in[pl.ds(pl.multiple_of(plane * 24, 8), 24), :]

    inv = inverse[...][:, :1]
    gained = grad * gain_ref[...]
    align = inv * (
        gained
        - jnp.mean(gained, axis=-1, keepdims=True)
        - norm * jnp.mean(gained * norm, axis=-1, keepdims=True)
    )
    align_out[...] = align.astype(B16)

    finish(big_plane_c)
    big_two[...] = total(big_plane).astype(B16)
    chip = narrow // 2
    for d in (2, 1, 3):
        sent(BIG_NARROW, (wide, (narrow + 2 * d) % 8), big_two, big_narrow.at[chip]).start()
    big_narrow[chip] = big_two[...]
    three = big_narrow.at[pl.ds(0, 3)]
    big_narrow_c = sent(BIG_NARROW, partner, three, three)

    finish(small_plane_c)
    small_part[...] = total(small_plane).astype(B16)
    small_depth_c = copies(SMALL_DEPTH, "depth", lambda k: small_part, small_depth)
    small_depth[depth] = small_part[...]

    finish(big_narrow_c)
    big_sum = big_narrow[0].astype(F32)
    for k in range(1, 4):
        big_sum = big_sum + big_narrow[k].astype(F32)
    big_three[...] = big_sum.astype(B16)
    big_back_c = copies(BIG_BACK, "plane", lambda k: big_three, big_back)
    big_back[plane] = big_three[...]

    finish(small_depth_c)
    small_two[...] = total(small_depth).astype(B16)
    small_narrow_c = copies(SMALL_NARROW, "narrow", lambda k: small_two, small_narrow)
    small_narrow[narrow] = small_two[...]

    finish(big_back_c)
    big_half[...] = big_back[...].reshape(64, 128)
    big_out_c = copies(BIG_OUT, "depth", lambda k: big_half, big_most)
    big_most[depth] = big_half[...]

    finish(small_narrow_c)
    small_three[...] = total(small_narrow).astype(B16)
    small_out_c = copies(SMALL_OUT, "plane", lambda k: small_three, small_all)
    small_all[plane] = small_three[...]

    finish(big_out_c)
    big_join_c = sent(BIG_JOIN, partner, big_most, big_rest)
    big_join_c.start()

    def put_weight(ref, part):
        for k in range(8):
            for c in range(2):
                piece = ref[k, pl.ds(c * 32, 32), :].astype(F32)
                weight_out[pl.ds(c * 16 + k * 2 + part, 32, stride=32), :] = piece

    put_weight(big_most, core)
    big_join_c.wait()
    put_weight(big_rest, 1 - core)
    @pl.when(lead)
    def _():
        sent(ROW_CORE, partner, row_pair, row_pair).wait_send()

        def sent_sums(own):
            part = rowg_sum.at[pl.ds(0, 7 if own else 8)]
            sent(ROWG_PAIR, partner, part, part).wait_send()

        for_own(sent_sums)

    @pl.when(follow)
    def _():
        sent(ROWG_CORE, partner, rowg_send, rowg_core).wait_send()

    finish(small_out_c)
    small = small_all[...].astype(F32).reshape(192, 128)
    proj_out[:, pl.ds(0, 128)] = small[0:64]
    proj_out[:, pl.ds(128, 128)] = small[64:128]
    norm_out[0:1, pl.ds(0, 128)] = small[128:129]
    norm_out[0:1, pl.ds(128, 128)] = small[129:130]
    norm_out[1:2, pl.ds(0, 128)] = small[130:131]
    norm_out[1:2, pl.ds(128, 128)] = small[131:132]
    bias_out[...] = small[132:134, :32]


def put_kernel(*refs):
    sem = refs[10]
    made = [pltpu.make_async_copy(refs[k], refs[5 + k], sem.at[k]) for k in range(5)]
    for c in made:
        c.start()
    for c in made:
        c.wait()


def put(results):
    return pl.pallas_call(
        put_kernel,
        out_shape=tuple(jax.ShapeDtypeStruct(r.shape, r.dtype) for r in results),
        in_specs=[pl.BlockSpec(memory_space=pltpu.VMEM)] * 5,
        out_specs=(pl.BlockSpec(memory_space=pl.ANY),) * 5,
        scratch_shapes=[pltpu.SemaphoreType.DMA((5,))],
    )(*[pltpu.with_memory_space_constraint(r, pltpu.VMEM) for r in results])


def everything(x, pair, gain, shift, weight, bias, out_weight):
    vmem = pl.BlockSpec(memory_space=pltpu.VMEM)
    hbm = pl.BlockSpec(memory_space=pl.ANY)
    scratch = [
        ((128, 256), B16), ((1, 256), F32), ((1, 256), F32), ((64, 256), B16), ((2, 32), F32),
        ((128, 256), F32), ((128, 256), B16), ((2, 128, 128), F32), ((128, 128), F32), ((32, 128), F32),
        ((32, 128), F32), ((2, 16, 128), B16), ((64, 128), F32), ((8, 16, 128), B16), ((128, 128), F32),
        ((4, 16, 128), B16), ((8, 16, 128), B16),
        ((8, 4, 16, 128), B16), ((8, 8, 16, 128), B16), ((8, 64, 128), B16), ((16, 32, 128), B16), ((1024, 128), B16),
        ((2048, 512), B16), ((1024, 128), F32), ((1024, 128), B16), ((4, 512, 256), B16), ((128, 512), B16),
        ((512, 128), B16), ((8, 32, 2048), B16),
        ((8, 8, 16, 128), B16), ((8, 8, 16, 128), B16), ((128, 512), F32), ((8, 4, 16, 128), B16), ((8, 4, 16, 128), B16),
        ((8, 4, 16, 128), B16),
        ((4, 4, 16, 128), B16), ((64, 128), F32), ((64, 128), F32), ((32, 128), F32),
        ((128, 128), F32), ((8, 16, 128), B16), ((8, 16, 128), B16), ((2, 128, 128), F32),
        ((8, 128, 128), B16), ((8, 64, 128), B16), ((8, 64, 128), B16), ((8, 64, 128), B16), ((8, 8, 128), B16),
        ((8, 8, 128), B16), ((8, 128), B16), ((4, 8, 128), B16), ((8, 128), B16), ((8, 8, 128), B16), ((64, 128), B16),
        ((8, 64, 128), B16), ((8, 64, 128), B16),
        ((192, 128), F32), ((8, 24, 128), F32), ((24, 128), B16), ((8, 24, 128), B16), ((24, 128), B16),
        ((8, 24, 128), B16), ((24, 128), B16), ((8, 24, 128), B16),
    ]
    return pl.pallas_call(
        kernel,
        out_shape=(
            pltpu.VMEM((128, 256), B16),
            pltpu.VMEM((64, 256), F32),
            pltpu.VMEM((2, 32), F32),
            pltpu.VMEM((2, 256), F32),
            pltpu.VMEM((1024, 128), F32),
        ),
        in_specs=[hbm] * 7,
        out_specs=(vmem,) * 5,
        scratch_shapes=[pltpu.VMEM(shape, kind) for shape, kind in scratch]
        + [pltpu.SemaphoreType.DMA((STAGES,)), pltpu.SemaphoreType.DMA((STAGES,)), pltpu.SemaphoreType.DMA((7,)), pltpu.SemaphoreType.REGULAR],
        compiler_params=pltpu.CompilerParams(
            collective_id=0, has_side_effects=True, vmem_limit_bytes=56 * 1024 * 1024
        ),
    )(x, pair, gain, shift, weight, bias, out_weight)


def shards(
    alignment_rows,
    pair_output_gradient,
    layer_norm_gain,
    layer_norm_bias,
    projection_weight,
    projection_bias,
    output_weight,
):
    results = everything(
        alignment_rows.reshape(128, 256),
        pair_output_gradient,
        layer_norm_gain.reshape(1, 256),
        layer_norm_bias.reshape(1, 256),
        jnp.transpose(projection_weight, (0, 2, 1)).reshape(64, 256),
        projection_bias,
        output_weight,
    )
    align, proj, bias, norm, weight_grad = put(results)
    return (
        align.reshape(2, 64, 256),
        jnp.transpose(proj.reshape(2, 32, 256), (0, 2, 1)),
        bias,
        weight_grad,
        norm,
    )


def solution(mesh):
    return jax.shard_map(
        shards,
        mesh=mesh,
        in_specs=(P("wide", "narrow", None), P("wide", "narrow", None), P(), P(), P(), P(), P()),
        out_specs=(P("wide", "narrow", None), P(), P(), P(), P()),
        check_vma=False,
    )
```

```python
import jax
import jax.numpy as jnp
from jax import lax
from jax.experimental import pallas as pl
from jax.experimental.pallas import tpu as pltpu
from jax.sharding import PartitionSpec as P

F32, B16 = jnp.float32, jnp.bfloat16
MESH_ID = pl.DeviceIdType.MESH
OFFSETS = {"depth": (4, 3, 5, 2, 6, 1, 7), "narrow": (4, 3, 5, 2, 6, 1, 7), "plane": (6, 5, 7, 4, 2, 1, 3)}
STAGES = 24
SEQUENCES = 128
(
    ROW_DEPTH, COL_DEPTH, ROW_PAIR, COL_PLANE, COLG_PLANE, ROWG_PAIR, BIG_PLANE, ROWG_DEPTH, COLG_DEPTH,
    BIG_DEPTH, SMALL_PLANE, BIG_NARROW, SMALL_DEPTH, BIG_BACK, SMALL_NARROW, BIG_OUT, SMALL_OUT,
    PAIR_HALF, ROW_CORE, ROWG_CORE, BIG_CORE, BIG_JOIN, NORM_ROW, NORM_COL,
) = range(STAGES)


def dot(a, b, dims):
    return lax.dot_general(a, b, ((dims[:1], dims[1:]), ((), ())), preferred_element_type=F32)


def total(ref):
    acc = ref[0].astype(F32)
    for k in range(1, 8):
        acc = acc + ref[k].astype(F32)
    return acc


def lanes(shape):
    return lax.broadcasted_iota(jnp.int32, shape, len(shape) - 1)


def half_swap(x):
    return pltpu.roll(x, 64, 1)


def kernel(
    x_hbm, pair_hbm, gain_hbm, shift_hbm, weight_hbm, bias_hbm, out_weight_hbm,
    align_out, proj_out, bias_out, norm_out, weight_out,
    x_ref, gain_ref, shift_ref, weight_ref, bias_ref,
    normed, scaled, scaled32, inverse, row_tmp,
    row_send, col_send, row_got, col_got, col_wide, row_next, col_next,
    row_pair, col_plane, pair_ref, pair_tile, out_weight_ref, pair_two, weight32, weight_order, upstream, rows, rows_t, outer,
    colg_send, colg_got, rowg_acc, rowg_core, rowg_sum, rowg_send, rowg_got, rowg_next, rowg_depth, rowg,
    colg_wide, colg_next, colg_depth, scaled_grad,
    big_send, big_core, big_one, big_depth, big_part, big_plane, big_two, big_narrow, big_three, big_back,
    big_all,
    small_in, small_plane, small_part, small_depth, small_two, small_narrow, small_three, small_all,
    norm_tmp, norm_row_send, norm_col_send, norm_row, norm_col, norm_two,
    send_sem, recv_sem, local_sem, ready,
):
    wide = lax.axis_index("wide")
    narrow = lax.axis_index("narrow")
    plane = wide // 8
    depth = wide % 8
    own_pair = plane == narrow
    other_pair = plane != narrow
    lead = plane % 2 == narrow % 2
    follow = plane % 2 != narrow % 2
    barrier = pltpu.get_barrier_semaphore()
    inputs = (
        (x_hbm, x_ref), (gain_hbm, gain_ref), (shift_hbm, shift_ref), (weight_hbm, weight_ref), (bias_hbm, bias_ref),
        (pair_hbm, pair_ref), (out_weight_hbm, out_weight_ref),
    )
    fetches = [pltpu.make_async_copy(a, b, local_sem.at[k]) for k, (a, b) in enumerate(inputs)]
    place = {"plane": plane, "depth": depth, "narrow": narrow}

    def peer(kind, k):
        if kind == "plane":
            return (k * 8 + depth, narrow)
        if kind == "depth":
            return (plane * 8 + k, narrow)
        return (wide, k)

    def holder(d):
        return (narrow * 8 + depth, (narrow + 2 * d) % 8)

    def source(d):
        return (((plane + d) % 8) * 8 + depth, plane)

    def greet(device):
        pl.semaphore_signal(barrier, 1, device_id=device, device_id_type=MESH_ID)

    def greet_all(kind):
        for d in OFFSETS[kind]:
            greet(peer(kind, (place[kind] + d) % 8))

    greet_all("depth")
    for c in fetches:
        c.start()
    fetch_pair, fetch_weight = fetches[5:]
    greet_all("narrow")
    greet_all("plane")

    def copies(stage, kind, give, target, size=1):
        me = place[kind]
        lead = pl.ds(pl.multiple_of(me * size, size), size) if size > 1 else me
        for d in OFFSETS[kind]:
            k = (me + d) % 8
            pltpu.make_async_remote_copy(
                src_ref=give(k),
                dst_ref=target.at[lead],
                send_sem=send_sem.at[stage],
                recv_sem=recv_sem.at[stage],
                device_id=peer(kind, k),
                device_id_type=MESH_ID,
            ).start()
        whole = target.at[pl.ds(0, 7 * size)]
        return pltpu.make_async_remote_copy(
            src_ref=whole,
            dst_ref=whole,
            send_sem=send_sem.at[stage],
            recv_sem=recv_sem.at[stage],
            device_id=peer(kind, (me + 1) % 8),
            device_id_type=MESH_ID,
        )

    def finish(c):
        c.wait()

    def sent(stage, device, source_ref, target_ref):
        return pltpu.make_async_remote_copy(
            src_ref=source_ref,
            dst_ref=target_ref,
            send_sem=send_sem.at[stage],
            recv_sem=recv_sem.at[stage],
            device_id=device,
            device_id_type=MESH_ID,
        )

    partner = (wide, narrow + 1 - 2 * (narrow % 2))

    def for_own(what):
        pl.when(own_pair)(lambda: what(True))
        pl.when(other_pair)(lambda: what(False))

    for c in fetches[:5]:
        c.wait()
    value = x_ref[...].astype(F32)
    centre = value - jnp.mean(value, axis=-1, keepdims=True)
    inv = lax.rsqrt(jnp.mean(centre * centre, axis=-1, keepdims=True) + 1e-05)
    norm = centre * inv
    inverse[...] = jnp.broadcast_to(inv, (128, 128))
    normed[...] = norm
    scaled_b = (norm * gain_ref[...] + shift_ref[...]).astype(B16)
    scaled[...] = scaled_b
    for c in range(2):
        scaled32[c] = scaled_b[:, c * 128 : c * 128 + 128].astype(F32)

    def every_fourth(g):
        both = [scaled32[c, pl.ds(g, 32, stride=4), :] for c in range(2)]
        return jnp.concatenate(both, axis=1).astype(B16)

    w_row = weight_ref[0:32, :]
    w_col = weight_ref[32:64, :]
    w_row4 = jnp.concatenate([w_row] * 4, axis=0)
    sub = lax.broadcasted_iota(jnp.int32, (32, 32), 0)
    diagonal = sub == lanes((32, 32))
    row_bias = jnp.sum(jnp.where(diagonal, bias_ref[0:1, :], 0.0), axis=1, keepdims=True)
    col_bias = jnp.sum(jnp.where(diagonal, bias_ref[1:2, :], 0.0), axis=1, keepdims=True)
    lane128 = lanes((32, 128))
    sub128 = lax.broadcasted_iota(jnp.int32, (32, 128), 0)
    row_bias4 = jnp.sum(jnp.where(sub128 == lane128 % 32, row_bias, 0.0), axis=0, keepdims=True)
    group = lane128 // 32
    row_fac = jnp.zeros((32, 128), F32)
    for g in range(4):
        row_fac = jnp.where(group == g, dot(every_fourth(g), w_row4, (1, 1)), row_fac)
    row_tmp[...] = (row_fac + row_bias4).astype(B16).astype(F32)
    for g in range(4):
        for r in range(2):
            row_send[pl.ds(g * 8 + r * 4, 4), :] = row_tmp[pl.ds(r * 16 + g * 4, 4), :]
    even_lane = lanes((16, 128)) // 32 % 2 == 0
    col_fac = dot(w_col, scaled_b, (1, 1)) + col_bias
    fac_a, fac_b = col_fac[:16], col_fac[16:]
    col_send[0] = jnp.where(even_lane, fac_a, pltpu.roll(fac_b, 32, 1)).astype(B16)
    col_send[1] = jnp.where(even_lane, pltpu.roll(fac_a, 96, 1), fac_b).astype(B16)
    pl.semaphore_wait(barrier, 21)
    for d in (2, 4, 6):
        pl.semaphore_signal(ready, 1, device_id=(wide, (narrow + d) % 8), device_id_type=MESH_ID)


    def eight(ref, k):
        return ref.at[pl.ds(pl.multiple_of(k * 8, 8), 8)]

    parity = depth % 2
    row_depth_c = copies(ROW_DEPTH, "depth", lambda k: eight(row_send, k // 2), row_got, 8)
    col_depth_c = copies(COL_DEPTH, "depth", lambda k: col_send.at[k % 2], col_got)
    mine = pl.ds(pl.multiple_of(depth * 8, 8), 8)
    row_got[mine, :] = row_send[pl.ds(pl.multiple_of(depth // 2 * 8, 8), 8), :]
    col_got[depth] = col_send[parity]
    fetch_weight.wait()
    weight32[...] = out_weight_ref[...].astype(F32)
    for b in range(8):
        for c in range(4):
            q = c % 2 * 16 + b * 2 + c // 2
            weight_order[pl.ds((b * 4 + c) * 32, 32), :] = weight32[pl.ds(q, 32, stride=32), :].astype(B16)

    finish(row_depth_c)
    for g in range(4):
        both = [row_got[pl.ds(r * 4 + g, 8, stride=8), :] for r in range(2)]
        row_next[g] = jnp.concatenate(both, axis=0).astype(B16)

    pl.semaphore_wait(ready, 3)
    for d in (2, 1, 3):
        sent(ROW_PAIR, holder(d), row_next, row_pair.at[plane]).start()

    @pl.when(other_pair)
    def _():
        sent(ROW_PAIR, holder(0), row_next, row_pair.at[plane]).start()

    @pl.when(own_pair)
    def _():
        row_pair[plane] = row_next[...]

    fetch_pair.wait()
    own_rows = pl.ds(pl.multiple_of(parity * 8, 8), 8)
    pair_half_c = pltpu.make_async_remote_copy(
        src_ref=pair_ref.at[:, pl.ds(pl.multiple_of((1 - parity) * 32, 32), 32)],
        dst_ref=pair_tile.at[own_rows],
        send_sem=send_sem.at[PAIR_HALF],
        recv_sem=recv_sem.at[PAIR_HALF],
        device_id=peer("depth", depth + 1 - 2 * parity),
        device_id_type=MESH_ID,
    )
    pair_half_c.start()
    pair_tile[own_rows] = pair_ref[:, pl.ds(pl.multiple_of(parity * 32, 32), 32), :]

    finish(col_depth_c)
    col_wide[...] = col_got[...].astype(F32).reshape(128, 128)
    low8 = lanes((8, 128)) < 64

    for b in range(8):
        x0 = col_wide[pl.ds(b * 2, 8, stride=16), :]
        x1 = col_wide[pl.ds(b * 2 + 1, 8, stride=16), :]
        r0 = jnp.where(low8, x0, half_swap(x1))
        r1 = jnp.where(low8, half_swap(x0), x1)
        col_next[b] = jnp.concatenate([r0, r1], axis=0).astype(B16)
    col_plane_c = copies(COL_PLANE, "plane", lambda k: col_next, col_plane)
    col_plane[plane] = col_next[...]

    low32 = lane128 < 64
    even32 = group % 2 == 0
    for c in range(2):
        norm_tmp[c] = normed[:, pl.ds(c * 128, 128)]
    for g in range(4):
        one = jnp.concatenate([norm_tmp[c, pl.ds(g, 32, stride=4), :] for c in range(2)], axis=1)
        for k in range(4):
            rs = [one[r * 16 + k * 4 : r * 16 + k * 4 + 4] for r in range(2)]
            norm_row_send[k, g] = jnp.concatenate(rs, axis=0).astype(B16)
    for h in range(2):
        for r in range(2):
            norm_col_send[h, pl.ds(r * 32, 32), :] = normed[pl.ds(r * 64 + h * 32, 32), :].astype(B16)
    pair_half_c.wait()
    norm_row_c = copies(NORM_ROW, "depth", lambda k: norm_row_send.at[k // 2], norm_row)
    norm_col_c = copies(NORM_COL, "depth", lambda k: norm_col_send.at[k % 2], norm_col)
    norm_row[depth] = norm_row_send[depth // 2]
    norm_col[depth] = norm_col_send[parity]

    def up(t, _):
        tile = pair_tile[...].reshape(512, 128)
        for h in range(2):
            w = weight_order[pl.ds(pl.multiple_of(t * 256 + h * 128, 128), 128), :]
            res = dot(w, tile, (1, 1))
            for i in range(4):
                a = [res[c * 32 : c * 32 + 32, i * 128 : i * 128 + 128] for c in range(4)]
                first = [jnp.where(low32, a[c], half_swap(a[c + 2])) for c in range(2)]
                second = [jnp.where(low32, half_swap(a[c]), a[c + 2]) for c in range(2)]
                out = []
                for f in (first, second):
                    out.append(jnp.where(even32, f[0], pltpu.roll(f[1], 32, 1)))
                    out.append(jnp.where(even32, pltpu.roll(f[0], 96, 1), f[1]))
                upstream[t, pl.ds(i * 128, 128), pl.ds(h * 128, 128)] = jnp.concatenate(out, axis=0).astype(B16)
        return 0

    lax.fori_loop(0, 4, up, 0)

    pair_two[...] = jnp.zeros((2048, 512), B16)
    for i in range(16):
        for c in range(4):
            pair_two[pl.ds(i * 128 + c * 32, 32), pl.ds(c * 128, 128)] = pair_tile[i]

    def sent_rows(own):
        part = row_pair.at[pl.ds(0, 3 if own else 4)]
        sent(ROW_PAIR, partner, part, part).wait_send()

    for_own(sent_rows)

    @pl.when(lead)
    def _():
        def came(own):
            part = row_pair.at[pl.ds(0, 7 if own else 8)]
            sent(ROW_PAIR, partner, part, part).wait_recv()

        for_own(came)
        sent(ROW_CORE, partner, row_pair, row_pair).start()

    finish(col_plane_c)

    def col_tile(t):
        both = [col_plane[:, t * 2 + h].reshape(128, 128) for h in range(2)]
        return jnp.concatenate(both, axis=1)

    row_part = dot(col_tile(0), upstream[0], (1, 1))
    for t in range(1, 4):
        row_part = row_part + dot(col_tile(t), upstream[t], (1, 1))
    row_part = row_part * (1.0 / SEQUENCES)
    rowg_acc[...] = row_part
    row_part = row_part.astype(B16)
    for g in range(4):
        rowg_send[:, g] = row_part[:, g * 128 : g * 128 + 128].reshape(8, 16, 128)

    @pl.when(follow)
    def _():
        sent(ROWG_CORE, partner, rowg_send, rowg_core).start()
        sent(ROW_CORE, partner, row_pair, row_pair).wait_recv()

    for g in range(4):
        rows[:, pl.ds(g * 128, 128)] = row_pair[:, g].reshape(128, 128)
    for t in range(4):
        r = (dot(rows[...], upstream[t], (1, 0)) * (1.0 / SEQUENCES)).astype(B16)
        for h in range(2):
            colg_send[:, t * 2 + h] = r[:, h * 128 : h * 128 + 128].reshape(8, 16, 128)

    @pl.when(lead)
    def _():
        sent(ROWG_CORE, partner, rowg_send, rowg_core).wait_recv()
        for g in range(4):
            both = rowg_acc[:, pl.ds(g * 128, 128)] + rowg_core[:, g].reshape(128, 128).astype(F32)
            rowg_sum[:, g] = both.astype(B16).reshape(8, 16, 128)
        for d in range(1, 8):
            sent(ROWG_PAIR, source(d), rowg_sum.at[(plane + d) % 8], rowg_got.at[narrow // 2]).start()

    @pl.when(lead & other_pair)
    def _():
        sent(ROWG_PAIR, source(0), rowg_sum.at[plane], rowg_got.at[narrow // 2]).start()

    @pl.when(own_pair)
    def _():
        rowg_got[narrow // 2] = rowg_sum[plane]

    colg_plane_c = copies(COLG_PLANE, "plane", lambda k: colg_send.at[k], colg_got)
    colg_got[plane] = colg_send[plane]
    rows_t[...] = rows[...].astype(F32).T.astype(B16)

    for t in range(4):
        o = (dot(rows_t[...], col_tile(t), (1, 0)) * (1.0 / SEQUENCES)).astype(B16)
        for h in range(2):
            for i in range(16):
                outer[t * 2 + h, :, pl.ds(i * 128, 128)] = o[i * 32 : i * 32 + 32, h * 128 : h * 128 + 128]
    for g in range(2):
        res = dot(outer[pl.ds(g * 4, 4)].reshape(128, 2048), pair_two[...], (1, 0)).astype(B16)
        for k in range(4):
            for c in range(4):
                big_send[g * 4 + k, pl.ds(c * 32, 32), :] = res[k * 32 : k * 32 + 32, c * 128 : c * 128 + 128]
    core = narrow % 2
    own_half = pl.ds(pl.multiple_of(core * 64, 64), 64)
    other_half = pl.ds(pl.multiple_of(64 - core * 64, 64), 64)
    big_core_c = sent(BIG_CORE, partner, big_send.at[:, other_half], big_core)
    big_core_c.start()
    big_core_c.wait()
    big_one[...] = (big_send[:, own_half, :].astype(F32) + big_core[...].astype(F32)).astype(B16)
    big_depth_c = copies(BIG_DEPTH, "depth", lambda k: big_one.at[k], big_depth)
    big_depth[depth] = big_one[depth]

    def came_rowg(own):
        part = rowg_got.at[pl.ds(0, 3 if own else 4)]
        sent(ROWG_PAIR, partner, part, part).wait_recv()

    for_own(came_rowg)
    row_sum = rowg_got[0].astype(F32)
    for k in range(1, 4):
        row_sum = row_sum + rowg_got[k].astype(F32)
    for g in range(4):
        for r in range(2):
            rowg_next[pl.ds(r * 4 + g, 8, stride=8), :] = row_sum[g, r * 8 : r * 8 + 8, :]
    rowg_depth_c = copies(ROWG_DEPTH, "depth", lambda k: eight(rowg_next, k), rowg_depth, 8)
    rowg_depth[mine, :] = rowg_next[mine, :]

    finish(colg_plane_c)

    for b in range(8):
        acc = colg_got[0, b].astype(F32)
        for k in range(1, 8):
            acc = acc + colg_got[k, b].astype(F32)
        y0, y1 = acc[:8], acc[8:]
        colg_wide[pl.ds(b * 2, 8, stride=16), :] = jnp.where(low8, y0, half_swap(y1))
        colg_wide[pl.ds(b * 2 + 1, 8, stride=16), :] = jnp.where(low8, half_swap(y0), y1)
    colg_next[...] = colg_wide[...].astype(B16).reshape(8, 16, 128)
    colg_depth_c = copies(COLG_DEPTH, "depth", lambda k: colg_next.at[k], colg_depth)
    colg_depth[depth] = colg_next[depth]

    finish(norm_row_c)
    part_row = rowg_next[...]
    part_row_b = part_row.astype(B16)
    from_row = jnp.zeros((32, 256), F32)
    for g in range(4):
        near = norm_row[:, g].astype(F32).reshape(64, 256).astype(B16)
        from_row = from_row + dot(part_row_b, near, (0, 0))[g * 32 : g * 32 + 32]
    row_fold = jnp.sum(part_row, axis=0, keepdims=True)
    row_fold = row_fold + pltpu.roll(row_fold, 32, 1) + pltpu.roll(row_fold, 64, 1) + pltpu.roll(row_fold, 96, 1)
    finish(norm_col_c)
    for k in range(8):
        for r in range(2):
            for h in range(2):
                norm_two[pl.ds(k * 128 + r * 64 + h * 32, 32), :] = norm_col[k, pl.ds(r * 32, 32), :]
    long = jnp.concatenate([colg_wide[pl.ds(k * 16, 16), :] for k in range(8)], axis=1)
    even_long = lanes((16, 1024)) // 32 % 2 == 0
    long2 = jnp.concatenate([jnp.where(even_long, long, 0.0), jnp.where(even_long, 0.0, long)], axis=0)
    from_col = dot(long2.astype(B16), norm_two[...], (1, 0))
    col_sum = jnp.sum(long2, axis=1, keepdims=True)
    col_fold = jnp.sum(jnp.where(sub128 == lane128, col_sum, 0.0), axis=0, keepdims=True)
    small_in[pl.ds(0, 32), :] = from_row[:, :128]
    small_in[pl.ds(32, 32), :] = from_col[:, :128]
    small_in[pl.ds(64, 32), :] = from_row[:, 128:]
    small_in[pl.ds(96, 32), :] = from_col[:, 128:]
    small_in[pl.ds(128, 64), :] = jnp.zeros((64, 128), F32)
    small_in[pl.ds(128, 1), :] = row_fold
    small_in[pl.ds(129, 1), :] = col_fold

    def strip(ref, k):
        return ref.at[pl.ds(pl.multiple_of(k * 24, 8), 24)]

    small_plane_c = copies(SMALL_PLANE, "plane", lambda k: strip(small_in, k), small_plane)
    small_plane[plane] = small_in[pl.ds(pl.multiple_of(plane * 24, 8), 24), :]

    finish(big_depth_c)
    big_part[...] = total(big_depth).astype(B16).reshape(8, 8, 128)
    big_plane_c = copies(BIG_PLANE, "plane", lambda k: big_part.at[k], big_plane)
    big_plane[plane] = big_part[plane]

    finish(big_plane_c)
    big_two[...] = total(big_plane).astype(B16)
    chip = narrow // 2
    for d in (2, 1, 3):
        sent(BIG_NARROW, (wide, (narrow + 2 * d) % 8), big_two, big_narrow.at[chip]).start()
    big_narrow[chip] = big_two[...]
    three = big_narrow.at[pl.ds(0, 3)]
    big_narrow_c = sent(BIG_NARROW, partner, three, three)

    finish(small_plane_c)
    small_part[...] = total(small_plane).astype(B16)
    small_depth_c = copies(SMALL_DEPTH, "depth", lambda k: small_part, small_depth)
    small_depth[depth] = small_part[...]

    finish(rowg_depth_c)
    for g in range(4):
        for r in range(2):
            one = rowg_depth[pl.ds(g * 16 + r * 4, 4), :] + rowg_depth[pl.ds(g * 16 + 8 + r * 4, 4), :]
            rowg[pl.ds(r * 16 + g * 4, 4), :] = one
    row_gb = rowg[...].astype(B16).astype(F32)
    for g in range(4):
        more = dot(jnp.where(group == g, row_gb, 0.0).astype(B16), w_row4, (1, 0))
        for c in range(2):
            scaled_grad[c, pl.ds(g, 32, stride=4), :] = more[:, c * 128 : c * 128 + 128]
    finish(colg_depth_c)
    half = []
    for h in range(2):
        one = colg_depth[h].astype(F32)
        for k in range(1, 4):
            one = one + colg_depth[k * 2 + h].astype(F32)
        half.append(one)
    col_gb = jnp.concatenate(
        [
            jnp.where(even_lane, half[0], pltpu.roll(half[1], 32, 1)),
            jnp.where(even_lane, pltpu.roll(half[0], 96, 1), half[1]),
        ],
        axis=0,
    ).astype(B16)
    grad = jnp.concatenate([scaled_grad[0], scaled_grad[1]], axis=1) + dot(col_gb, w_col, (0, 0))
    norm = normed[...]
    inv = inverse[...][:, :1]
    gained = grad * gain_ref[...]
    align = inv * (
        gained
        - jnp.mean(gained, axis=-1, keepdims=True)
        - norm * jnp.mean(gained * norm, axis=-1, keepdims=True)
    )
    align_out[...] = align.astype(B16)


    finish(big_narrow_c)
    big_sum = big_narrow[0].astype(F32)
    for k in range(1, 4):
        big_sum = big_sum + big_narrow[k].astype(F32)
    big_three[...] = big_sum.astype(B16)
    big_back_c = copies(BIG_BACK, "depth", lambda k: big_three, big_back)
    big_back[depth] = big_three[...]

    finish(small_depth_c)
    small_two[...] = total(small_depth).astype(B16)
    small_narrow_c = copies(SMALL_NARROW, "narrow", lambda k: small_two, small_narrow)
    small_narrow[narrow] = small_two[...]

    finish(big_back_c)
    slot = core * 8 + plane
    other = narrow + 1 - 2 * core
    for d in OFFSETS["plane"]:
        k = (plane + d) % 8
        sent(BIG_OUT, (k * 8 + depth, other), big_back, big_all.at[slot]).start()
        sent(BIG_OUT, (k * 8 + depth, narrow), big_back, big_all.at[slot]).start()
    sent(BIG_OUT, partner, big_back, big_all.at[slot]).start()
    big_all[slot] = big_back[...]
    fifteen = big_all.at[pl.ds(0, 15)]
    big_out_c = sent(BIG_OUT, partner, fifteen, fifteen)

    finish(small_narrow_c)
    small_three[...] = total(small_narrow).astype(B16)
    small_out_c = copies(SMALL_OUT, "plane", lambda k: small_three, small_all)
    small_all[plane] = small_three[...]

    @pl.when(lead)
    def _():
        sent(ROW_CORE, partner, row_pair, row_pair).wait_send()

        def sent_sums(own):
            part = rowg_sum.at[pl.ds(0, 7 if own else 8)]
            sent(ROWG_PAIR, partner, part, part).wait_send()

        for_own(sent_sums)

    @pl.when(follow)
    def _():
        sent(ROWG_CORE, partner, rowg_send, rowg_core).wait_send()

    finish(small_out_c)
    small = small_all[...].astype(F32).reshape(192, 128)
    bias_out[...] = small[128:130, :32]
    first = jnp.sum(jnp.where(sub128 == lane128, small[128:129], 0.0), axis=1, keepdims=True)
    second = jnp.sum(jnp.where(sub128 == lane128, small[129:130], 0.0), axis=1, keepdims=True)
    sums = jnp.concatenate([first, second], axis=0)
    product = jnp.concatenate([small[0:64], small[64:128]], axis=1)
    proj_out[...] = gain_ref[...] * product + shift_ref[...] * sums
    both = weight_ref[...].astype(F32)
    norm_out[0:1, :] = jnp.sum(both * product, axis=0, keepdims=True)
    norm_out[1:2, :] = jnp.sum(both * sums, axis=0, keepdims=True)
    finish(big_out_c)
    for part in range(2):
        for k in range(8):
            slice_k = big_all[pl.ds(part * 8, 8), k].astype(F32).reshape(64, 128)
            for c in range(2):
                weight_out[pl.ds(c * 16 + k * 2 + part, 32, stride=32), :] = slice_k[c * 32 : c * 32 + 32]


def put_kernel(*refs):
    sem = refs[10]
    made = []
    for k in range(4):
        part = pl.ds(k * 256, 256)
        made.append(pltpu.make_async_copy(refs[4].at[part], refs[9].at[part], sem.at[4 + k]))
    made += [pltpu.make_async_copy(refs[k], refs[5 + k], sem.at[k]) for k in range(4)]
    for c in made:
        c.start()
    for c in made:
        c.wait()


def put(results):
    return pl.pallas_call(
        put_kernel,
        out_shape=tuple(jax.ShapeDtypeStruct(r.shape, r.dtype) for r in results),
        in_specs=[pl.BlockSpec(memory_space=pltpu.VMEM)] * 5,
        out_specs=(pl.BlockSpec(memory_space=pl.ANY),) * 5,
        scratch_shapes=[pltpu.SemaphoreType.DMA((8,))],
    )(*[pltpu.with_memory_space_constraint(r, pltpu.VMEM) for r in results])


def everything(x, pair, gain, shift, weight, bias, out_weight):
    vmem = pl.BlockSpec(memory_space=pltpu.VMEM)
    hbm = pl.BlockSpec(memory_space=pl.ANY)
    scratch = [
        ((128, 256), B16), ((1, 256), F32), ((1, 256), F32), ((64, 256), B16), ((2, 32), F32),
        ((128, 256), F32), ((128, 256), B16), ((2, 128, 128), F32), ((128, 128), F32), ((32, 128), F32),
        ((32, 128), F32), ((2, 16, 128), B16), ((64, 128), F32), ((8, 16, 128), B16), ((128, 128), F32),
        ((4, 16, 128), B16), ((8, 16, 128), B16),
        ((8, 4, 16, 128), B16), ((8, 8, 16, 128), B16), ((8, 64, 128), B16), ((16, 32, 128), B16), ((1024, 128), B16),
        ((2048, 512), B16), ((1024, 128), F32), ((1024, 128), B16), ((4, 512, 256), B16), ((128, 512), B16),
        ((512, 128), B16), ((8, 32, 2048), B16),
        ((8, 8, 16, 128), B16), ((8, 8, 16, 128), B16), ((128, 512), F32), ((8, 4, 16, 128), B16), ((8, 4, 16, 128), B16),
        ((8, 4, 16, 128), B16),
        ((4, 4, 16, 128), B16), ((64, 128), F32), ((64, 128), F32), ((32, 128), F32),
        ((128, 128), F32), ((8, 16, 128), B16), ((8, 16, 128), B16), ((2, 128, 128), F32),
        ((8, 128, 128), B16), ((8, 64, 128), B16), ((8, 64, 128), B16), ((8, 64, 128), B16), ((8, 8, 128), B16),
        ((8, 8, 128), B16), ((8, 128), B16), ((4, 8, 128), B16), ((8, 128), B16), ((8, 8, 128), B16),
        ((16, 8, 8, 128), B16),
        ((192, 128), F32), ((8, 24, 128), F32), ((24, 128), B16), ((8, 24, 128), B16), ((24, 128), B16),
        ((8, 24, 128), B16), ((24, 128), B16), ((8, 24, 128), B16),
        ((2, 128, 128), F32), ((4, 4, 8, 256), B16), ((2, 64, 256), B16), ((8, 4, 8, 256), B16), ((8, 64, 256), B16),
        ((1024, 256), B16),
    ]
    return pl.pallas_call(
        kernel,
        out_shape=(
            pltpu.VMEM((128, 256), B16),
            pltpu.VMEM((64, 256), F32),
            pltpu.VMEM((2, 32), F32),
            pltpu.VMEM((2, 256), F32),
            pltpu.VMEM((1024, 128), F32),
        ),
        in_specs=[hbm] * 7,
        out_specs=(vmem,) * 5,
        scratch_shapes=[pltpu.VMEM(shape, kind) for shape, kind in scratch]
        + [pltpu.SemaphoreType.DMA((STAGES,)), pltpu.SemaphoreType.DMA((STAGES,)), pltpu.SemaphoreType.DMA((7,)), pltpu.SemaphoreType.REGULAR],
        compiler_params=pltpu.CompilerParams(
            collective_id=0, has_side_effects=True, vmem_limit_bytes=56 * 1024 * 1024
        ),
    )(x, pair, gain, shift, weight, bias, out_weight)


def shards(
    alignment_rows,
    pair_output_gradient,
    layer_norm_gain,
    layer_norm_bias,
    projection_weight,
    projection_bias,
    output_weight,
):
    results = everything(
        alignment_rows.reshape(128, 256),
        pair_output_gradient,
        layer_norm_gain.reshape(1, 256),
        layer_norm_bias.reshape(1, 256),
        jnp.transpose(projection_weight, (0, 2, 1)).reshape(64, 256),
        projection_bias,
        output_weight,
    )
    align, proj, bias, norm, weight_grad = put(results)
    return (
        align.reshape(2, 64, 256),
        jnp.transpose(proj.reshape(2, 32, 256), (0, 2, 1)),
        bias,
        weight_grad,
        norm,
    )


def solution(mesh):
    return jax.shard_map(
        shards,
        mesh=mesh,
        in_specs=(P("wide", "narrow", None), P("wide", "narrow", None), P(), P(), P(), P(), P()),
        out_specs=(P("wide", "narrow", None), P(), P(), P(), P()),
        check_vma=False,
    )
```

```python
import jax
import jax.numpy as jnp
from jax import lax
from jax.experimental import pallas as pl
from jax.experimental.pallas import tpu as pltpu
from jax.sharding import PartitionSpec as P

F32, B16 = jnp.float32, jnp.bfloat16
MESH_ID = pl.DeviceIdType.MESH
OFFSETS = {"depth": (4, 3, 5, 2, 6, 1, 7), "narrow": (4, 3, 5, 2, 6, 1, 7), "plane": (6, 5, 7, 4, 2, 1, 3)}
STAGES = 24
SEQUENCES = 128
(
    ROW_DEPTH, COL_DEPTH, ROW_PAIR, COL_PLANE, COLG_PLANE, ROWG_PAIR, BIG_PLANE, ROWG_DEPTH, COLG_DEPTH,
    BIG_DEPTH, SMALL_PLANE, BIG_NARROW, SMALL_DEPTH, BIG_BACK, SMALL_NARROW, BIG_OUT, SMALL_OUT,
    PAIR_HALF, ROW_CORE, ROWG_CORE, BIG_CORE, BIG_JOIN, NORM_ROW, NORM_COL,
) = range(STAGES)


def dot(a, b, dims):
    return lax.dot_general(a, b, ((dims[:1], dims[1:]), ((), ())), preferred_element_type=F32)


def total(ref):
    acc = ref[0].astype(F32)
    for k in range(1, 8):
        acc = acc + ref[k].astype(F32)
    return acc


def lanes(shape):
    return lax.broadcasted_iota(jnp.int32, shape, len(shape) - 1)


def half_swap(x):
    return pltpu.roll(x, 64, 1)


def kernel(
    x_hbm, pair_hbm, gain_hbm, shift_hbm, weight_hbm, bias_hbm, out_weight_hbm,
    align_out, proj_out, bias_out, norm_out, weight_out,
    x_ref, gain_ref, shift_ref, weight_ref, bias_ref,
    normed, scaled, scaled32, inverse, row_tmp,
    row_send, col_send, row_got, col_got, col_wide, row_next, col_next,
    row_pair, col_plane, pair_ref, pair_tile, out_weight_ref, pair_two, weight32, weight_order, upstream, rows, rows_t, outer,
    colg_send, colg_got, rowg_acc, rowg_core, rowg_sum, rowg_send, rowg_got, rowg_next, rowg_depth, rowg,
    colg_wide, colg_next, colg_depth, scaled_grad,
    big_send, big_core, big_one, big_depth, big_part, big_plane, big_two, big_narrow, big_three, big_back,
    big_all,
    small_in, small_plane, small_part, small_depth, small_two, small_narrow, small_three, small_all,
    norm_tmp, norm_row_send, norm_col_send, norm_row, norm_col, norm_two,
    send_sem, recv_sem, local_sem, ready,
):
    wide = lax.axis_index("wide")
    narrow = lax.axis_index("narrow")
    plane = wide // 8
    depth = wide % 8
    own_pair = plane == narrow
    other_pair = plane != narrow
    lead = plane % 2 == narrow % 2
    follow = plane % 2 != narrow % 2
    barrier = pltpu.get_barrier_semaphore()
    inputs = (
        (x_hbm, x_ref), (gain_hbm, gain_ref), (shift_hbm, shift_ref), (weight_hbm, weight_ref), (bias_hbm, bias_ref),
        (pair_hbm, pair_ref), (out_weight_hbm, out_weight_ref),
    )
    fetches = [pltpu.make_async_copy(a, b, local_sem.at[k]) for k, (a, b) in enumerate(inputs)]
    place = {"plane": plane, "depth": depth, "narrow": narrow}

    def peer(kind, k):
        if kind == "plane":
            return (k * 8 + depth, narrow)
        if kind == "depth":
            return (plane * 8 + k, narrow)
        return (wide, k)

    def holder(d):
        return (narrow * 8 + depth, (narrow + 2 * d) % 8)

    def source(d):
        return (((plane + d) % 8) * 8 + depth, plane)

    def greet(device):
        pl.semaphore_signal(barrier, 1, device_id=device, device_id_type=MESH_ID)

    def greet_all(kind):
        for d in OFFSETS[kind]:
            greet(peer(kind, (place[kind] + d) % 8))

    greet_all("depth")
    greet_all("narrow")
    for c in fetches:
        c.start()
    fetch_pair, fetch_weight = fetches[5:]
    greet_all("plane")

    def copies(stage, kind, give, target, size=1):
        me = place[kind]
        lead = pl.ds(pl.multiple_of(me * size, size), size) if size > 1 else me
        for d in OFFSETS[kind]:
            k = (me + d) % 8
            pltpu.make_async_remote_copy(
                src_ref=give(k),
                dst_ref=target.at[lead],
                send_sem=send_sem.at[stage],
                recv_sem=recv_sem.at[stage],
                device_id=peer(kind, k),
                device_id_type=MESH_ID,
            ).start()
        whole = target.at[pl.ds(0, 7 * size)]
        return pltpu.make_async_remote_copy(
            src_ref=whole,
            dst_ref=whole,
            send_sem=send_sem.at[stage],
            recv_sem=recv_sem.at[stage],
            device_id=peer(kind, (me + 1) % 8),
            device_id_type=MESH_ID,
        )

    def finish(c):
        c.wait()

    def sent(stage, device, source_ref, target_ref):
        return pltpu.make_async_remote_copy(
            src_ref=source_ref,
            dst_ref=target_ref,
            send_sem=send_sem.at[stage],
            recv_sem=recv_sem.at[stage],
            device_id=device,
            device_id_type=MESH_ID,
        )

    partner = (wide, narrow + 1 - 2 * (narrow % 2))

    def for_own(what):
        pl.when(own_pair)(lambda: what(True))
        pl.when(other_pair)(lambda: what(False))

    for c in fetches[:5]:
        c.wait()
    value = x_ref[...].astype(F32)
    centre = value - jnp.mean(value, axis=-1, keepdims=True)
    inv = lax.rsqrt(jnp.mean(centre * centre, axis=-1, keepdims=True) + 1e-05)
    norm = centre * inv
    inverse[...] = jnp.broadcast_to(inv, (128, 128))
    normed[...] = norm
    scaled_b = (norm * gain_ref[...] + shift_ref[...]).astype(B16)
    scaled[...] = scaled_b
    for c in range(2):
        scaled32[c] = scaled_b[:, c * 128 : c * 128 + 128].astype(F32)

    def every_fourth(g):
        both = [scaled32[c, pl.ds(g, 32, stride=4), :] for c in range(2)]
        return jnp.concatenate(both, axis=1).astype(B16)

    w_row = weight_ref[0:32, :]
    w_col = weight_ref[32:64, :]
    w_row4 = jnp.concatenate([w_row] * 4, axis=0)
    sub = lax.broadcasted_iota(jnp.int32, (32, 32), 0)
    diagonal = sub == lanes((32, 32))
    row_bias = jnp.sum(jnp.where(diagonal, bias_ref[0:1, :], 0.0), axis=1, keepdims=True)
    col_bias = jnp.sum(jnp.where(diagonal, bias_ref[1:2, :], 0.0), axis=1, keepdims=True)
    lane128 = lanes((32, 128))
    sub128 = lax.broadcasted_iota(jnp.int32, (32, 128), 0)
    row_bias4 = jnp.sum(jnp.where(sub128 == lane128 % 32, row_bias, 0.0), axis=0, keepdims=True)
    group = lane128 // 32
    row_fac = jnp.zeros((32, 128), F32)
    for g in range(4):
        row_fac = jnp.where(group == g, dot(every_fourth(g), w_row4, (1, 1)), row_fac)
    row_tmp[...] = (row_fac + row_bias4).astype(B16).astype(F32)
    for g in range(4):
        for r in range(2):
            row_send[pl.ds(g * 8 + r * 4, 4), :] = row_tmp[pl.ds(r * 16 + g * 4, 4), :]
    even_lane = lanes((16, 128)) // 32 % 2 == 0
    col_fac = dot(w_col, scaled_b, (1, 1)) + col_bias
    fac_a, fac_b = col_fac[:16], col_fac[16:]
    col_send[0] = jnp.where(even_lane, fac_a, pltpu.roll(fac_b, 32, 1)).astype(B16)
    col_send[1] = jnp.where(even_lane, pltpu.roll(fac_a, 96, 1), fac_b).astype(B16)
    pl.semaphore_wait(barrier, 21)
    for d in (2, 4, 6):
        pl.semaphore_signal(ready, 1, device_id=(wide, (narrow + d) % 8), device_id_type=MESH_ID)


    def eight(ref, k):
        return ref.at[pl.ds(pl.multiple_of(k * 8, 8), 8)]

    parity = depth % 2
    row_depth_c = copies(ROW_DEPTH, "depth", lambda k: eight(row_send, k // 2), row_got, 8)
    col_depth_c = copies(COL_DEPTH, "depth", lambda k: col_send.at[k % 2], col_got)
    mine = pl.ds(pl.multiple_of(depth * 8, 8), 8)
    row_got[mine, :] = row_send[pl.ds(pl.multiple_of(depth // 2 * 8, 8), 8), :]
    col_got[depth] = col_send[parity]
    fetch_weight.wait()
    weight32[...] = out_weight_ref[...].astype(F32)
    for b in range(8):
        for c in range(4):
            q = c % 2 * 16 + b * 2 + c // 2
            weight_order[pl.ds((b * 4 + c) * 32, 32), :] = weight32[pl.ds(q, 32, stride=32), :].astype(B16)

    finish(row_depth_c)
    for g in range(4):
        both = [row_got[pl.ds(r * 4 + g, 8, stride=8), :] for r in range(2)]
        row_next[g] = jnp.concatenate(both, axis=0).astype(B16)

    pl.semaphore_wait(ready, 3)
    for d in (2, 1, 3):
        sent(ROW_PAIR, holder(d), row_next, row_pair.at[plane]).start()

    @pl.when(other_pair)
    def _():
        sent(ROW_PAIR, holder(0), row_next, row_pair.at[plane]).start()

    @pl.when(own_pair)
    def _():
        row_pair[plane] = row_next[...]

    fetch_pair.wait()
    own_rows = pl.ds(pl.multiple_of(parity * 8, 8), 8)
    pair_half_c = pltpu.make_async_remote_copy(
        src_ref=pair_ref.at[:, pl.ds(pl.multiple_of((1 - parity) * 32, 32), 32)],
        dst_ref=pair_tile.at[own_rows],
        send_sem=send_sem.at[PAIR_HALF],
        recv_sem=recv_sem.at[PAIR_HALF],
        device_id=peer("depth", depth + 1 - 2 * parity),
        device_id_type=MESH_ID,
    )
    pair_half_c.start()
    pair_tile[own_rows] = pair_ref[:, pl.ds(pl.multiple_of(parity * 32, 32), 32), :]

    finish(col_depth_c)
    col_wide[...] = col_got[...].astype(F32).reshape(128, 128)
    low8 = lanes((8, 128)) < 64

    for b in range(8):
        x0 = col_wide[pl.ds(b * 2, 8, stride=16), :]
        x1 = col_wide[pl.ds(b * 2 + 1, 8, stride=16), :]
        r0 = jnp.where(low8, x0, half_swap(x1))
        r1 = jnp.where(low8, half_swap(x0), x1)
        col_next[b] = jnp.concatenate([r0, r1], axis=0).astype(B16)
    col_plane_c = copies(COL_PLANE, "plane", lambda k: col_next, col_plane)
    col_plane[plane] = col_next[...]

    low32 = lane128 < 64
    even32 = group % 2 == 0
    for c in range(2):
        norm_tmp[c] = normed[:, pl.ds(c * 128, 128)]
    for g in range(4):
        one = jnp.concatenate([norm_tmp[c, pl.ds(g, 32, stride=4), :] for c in range(2)], axis=1)
        for k in range(4):
            rs = [one[r * 16 + k * 4 : r * 16 + k * 4 + 4] for r in range(2)]
            norm_row_send[k, g] = jnp.concatenate(rs, axis=0).astype(B16)
    for h in range(2):
        for r in range(2):
            norm_col_send[h, pl.ds(r * 32, 32), :] = normed[pl.ds(r * 64 + h * 32, 32), :].astype(B16)

    def up_half(which):
        tile = pair_tile[pl.ds(pl.multiple_of(which * 8, 8), 8)].reshape(256, 128)

        def up(t, _):
            for h in range(2):
                w = weight_order[pl.ds(pl.multiple_of(t * 256 + h * 128, 128), 128), :]
                res = dot(w, tile, (1, 1))
                for i in range(2):
                    a = [res[c * 32 : c * 32 + 32, i * 128 : i * 128 + 128] for c in range(4)]
                    first = [jnp.where(low32, a[c], half_swap(a[c + 2])) for c in range(2)]
                    second = [jnp.where(low32, half_swap(a[c]), a[c + 2]) for c in range(2)]
                    out = []
                    for f in (first, second):
                        out.append(jnp.where(even32, f[0], pltpu.roll(f[1], 32, 1)))
                        out.append(jnp.where(even32, pltpu.roll(f[0], 96, 1), f[1]))
                    spot = pl.ds(pl.multiple_of(which * 256 + i * 128, 128), 128)
                    upstream[t, spot, pl.ds(h * 128, 128)] = jnp.concatenate(out, axis=0).astype(B16)
            return 0

        lax.fori_loop(0, 4, up, 0)

    up_half(parity)
    pair_half_c.wait()
    norm_row_c = copies(NORM_ROW, "depth", lambda k: norm_row_send.at[k // 2], norm_row)
    norm_row[depth] = norm_row_send[depth // 2]
    up_half(1 - parity)
    norm_col_c = copies(NORM_COL, "depth", lambda k: norm_col_send.at[k % 2], norm_col)
    norm_col[depth] = norm_col_send[parity]

    pair_two[...] = jnp.zeros((2048, 512), B16)
    for i in range(16):
        for c in range(4):
            pair_two[pl.ds(i * 128 + c * 32, 32), pl.ds(c * 128, 128)] = pair_tile[i]

    def sent_rows(own):
        part = row_pair.at[pl.ds(0, 3 if own else 4)]
        sent(ROW_PAIR, partner, part, part).wait_send()

    for_own(sent_rows)

    @pl.when(lead)
    def _():
        def came(own):
            part = row_pair.at[pl.ds(0, 7 if own else 8)]
            sent(ROW_PAIR, partner, part, part).wait_recv()

        for_own(came)
        sent(ROW_CORE, partner, row_pair, row_pair).start()

    finish(col_plane_c)

    def col_tile(t):
        both = [col_plane[:, t * 2 + h].reshape(128, 128) for h in range(2)]
        return jnp.concatenate(both, axis=1)

    row_part = dot(col_tile(0), upstream[0], (1, 1))
    for t in range(1, 4):
        row_part = row_part + dot(col_tile(t), upstream[t], (1, 1))
    row_part = row_part * (1.0 / SEQUENCES)
    rowg_acc[...] = row_part
    row_part = row_part.astype(B16)
    for g in range(4):
        rowg_send[:, g] = row_part[:, g * 128 : g * 128 + 128].reshape(8, 16, 128)

    @pl.when(follow)
    def _():
        sent(ROWG_CORE, partner, rowg_send, rowg_core).start()
        sent(ROW_CORE, partner, row_pair, row_pair).wait_recv()

    for g in range(4):
        rows[:, pl.ds(g * 128, 128)] = row_pair[:, g].reshape(128, 128)
    for t in range(4):
        r = (dot(rows[...], upstream[t], (1, 0)) * (1.0 / SEQUENCES)).astype(B16)
        for h in range(2):
            colg_send[:, t * 2 + h] = r[:, h * 128 : h * 128 + 128].reshape(8, 16, 128)

    @pl.when(lead)
    def _():
        sent(ROWG_CORE, partner, rowg_send, rowg_core).wait_recv()
        for g in range(4):
            both = rowg_acc[:, pl.ds(g * 128, 128)] + rowg_core[:, g].reshape(128, 128).astype(F32)
            rowg_sum[:, g] = both.astype(B16).reshape(8, 16, 128)
        for d in range(1, 8):
            sent(ROWG_PAIR, source(d), rowg_sum.at[(plane + d) % 8], rowg_got.at[narrow // 2]).start()

    @pl.when(lead & other_pair)
    def _():
        sent(ROWG_PAIR, source(0), rowg_sum.at[plane], rowg_got.at[narrow // 2]).start()

    @pl.when(own_pair)
    def _():
        rowg_got[narrow // 2] = rowg_sum[plane]

    colg_plane_c = copies(COLG_PLANE, "plane", lambda k: colg_send.at[k], colg_got)
    colg_got[plane] = colg_send[plane]
    rows_t[...] = rows[...].astype(F32).T.astype(B16)

    for t in range(4):
        o = (dot(rows_t[...], col_tile(t), (1, 0)) * (1.0 / SEQUENCES)).astype(B16)
        for h in range(2):
            for i in range(16):
                outer[t * 2 + h, :, pl.ds(i * 128, 128)] = o[i * 32 : i * 32 + 32, h * 128 : h * 128 + 128]
    for g in range(2):
        res = dot(outer[pl.ds(g * 4, 4)].reshape(128, 2048), pair_two[...], (1, 0)).astype(B16)
        for k in range(4):
            for c in range(4):
                big_send[g * 4 + k, pl.ds(c * 32, 32), :] = res[k * 32 : k * 32 + 32, c * 128 : c * 128 + 128]
    core = narrow % 2
    own_half = pl.ds(pl.multiple_of(core * 64, 64), 64)
    other_half = pl.ds(pl.multiple_of(64 - core * 64, 64), 64)
    big_core_c = sent(BIG_CORE, partner, big_send.at[:, other_half], big_core)
    big_core_c.start()
    big_core_c.wait()
    big_one[...] = (big_send[:, own_half, :].astype(F32) + big_core[...].astype(F32)).astype(B16)
    big_depth_c = copies(BIG_DEPTH, "depth", lambda k: big_one.at[k], big_depth)
    big_depth[depth] = big_one[depth]

    def came_rowg(own):
        part = rowg_got.at[pl.ds(0, 3 if own else 4)]
        sent(ROWG_PAIR, partner, part, part).wait_recv()

    for_own(came_rowg)
    row_sum = rowg_got[0].astype(F32)
    for k in range(1, 4):
        row_sum = row_sum + rowg_got[k].astype(F32)
    for g in range(4):
        for r in range(2):
            rowg_next[pl.ds(r * 4 + g, 8, stride=8), :] = row_sum[g, r * 8 : r * 8 + 8, :]
    rowg_depth_c = copies(ROWG_DEPTH, "depth", lambda k: eight(rowg_next, k), rowg_depth, 8)
    rowg_depth[mine, :] = rowg_next[mine, :]

    finish(colg_plane_c)

    for b in range(8):
        acc = colg_got[0, b].astype(F32)
        for k in range(1, 8):
            acc = acc + colg_got[k, b].astype(F32)
        y0, y1 = acc[:8], acc[8:]
        colg_wide[pl.ds(b * 2, 8, stride=16), :] = jnp.where(low8, y0, half_swap(y1))
        colg_wide[pl.ds(b * 2 + 1, 8, stride=16), :] = jnp.where(low8, half_swap(y0), y1)
    colg_next[...] = colg_wide[...].astype(B16).reshape(8, 16, 128)
    colg_depth_c = copies(COLG_DEPTH, "depth", lambda k: colg_next.at[k], colg_depth)
    colg_depth[depth] = colg_next[depth]

    finish(norm_row_c)
    part_row = rowg_next[...]
    part_row_b = part_row.astype(B16)
    from_row = jnp.zeros((32, 256), F32)
    for g in range(4):
        near = norm_row[:, g].astype(F32).reshape(64, 256).astype(B16)
        from_row = from_row + dot(part_row_b, near, (0, 0))[g * 32 : g * 32 + 32]
    row_fold = jnp.sum(part_row, axis=0, keepdims=True)
    row_fold = row_fold + pltpu.roll(row_fold, 32, 1) + pltpu.roll(row_fold, 64, 1) + pltpu.roll(row_fold, 96, 1)
    finish(norm_col_c)
    for k in range(8):
        for r in range(2):
            for h in range(2):
                norm_two[pl.ds(k * 128 + r * 64 + h * 32, 32), :] = norm_col[k, pl.ds(r * 32, 32), :]
    long = jnp.concatenate([colg_wide[pl.ds(k * 16, 16), :] for k in range(8)], axis=1)
    even_long = lanes((16, 1024)) // 32 % 2 == 0
    long2 = jnp.concatenate([jnp.where(even_long, long, 0.0), jnp.where(even_long, 0.0, long)], axis=0)
    from_col = dot(long2.astype(B16), norm_two[...], (1, 0))
    col_sum = jnp.sum(long2, axis=1, keepdims=True)
    col_fold = jnp.sum(jnp.where(sub128 == lane128, col_sum, 0.0), axis=0, keepdims=True)
    small_in[pl.ds(0, 32), :] = from_row[:, :128]
    small_in[pl.ds(32, 32), :] = from_col[:, :128]
    small_in[pl.ds(64, 32), :] = from_row[:, 128:]
    small_in[pl.ds(96, 32), :] = from_col[:, 128:]
    small_in[pl.ds(128, 64), :] = jnp.zeros((64, 128), F32)
    small_in[pl.ds(128, 1), :] = row_fold
    small_in[pl.ds(129, 1), :] = col_fold

    def strip(ref, k):
        return ref.at[pl.ds(pl.multiple_of(k * 24, 8), 24)]

    small_plane_c = copies(SMALL_PLANE, "plane", lambda k: strip(small_in, k), small_plane)
    small_plane[plane] = small_in[pl.ds(pl.multiple_of(plane * 24, 8), 24), :]

    finish(big_depth_c)
    big_part[...] = total(big_depth).astype(B16).reshape(8, 8, 128)
    big_plane_c = copies(BIG_PLANE, "plane", lambda k: big_part.at[k], big_plane)
    big_plane[plane] = big_part[plane]

    finish(big_plane_c)
    big_two[...] = total(big_plane).astype(B16)
    chip = narrow // 2
    for d in (2, 1, 3):
        sent(BIG_NARROW, (wide, (narrow + 2 * d) % 8), big_two, big_narrow.at[chip]).start()
    big_narrow[chip] = big_two[...]
    three = big_narrow.at[pl.ds(0, 3)]
    big_narrow_c = sent(BIG_NARROW, partner, three, three)

    finish(small_plane_c)
    small_part[...] = total(small_plane).astype(B16)
    small_depth_c = copies(SMALL_DEPTH, "depth", lambda k: small_part, small_depth)
    small_depth[depth] = small_part[...]

    finish(rowg_depth_c)
    for g in range(4):
        for r in range(2):
            one = rowg_depth[pl.ds(g * 16 + r * 4, 4), :] + rowg_depth[pl.ds(g * 16 + 8 + r * 4, 4), :]
            rowg[pl.ds(r * 16 + g * 4, 4), :] = one
    row_gb = rowg[...].astype(B16).astype(F32)
    for g in range(4):
        more = dot(jnp.where(group == g, row_gb, 0.0).astype(B16), w_row4, (1, 0))
        for c in range(2):
            scaled_grad[c, pl.ds(g, 32, stride=4), :] = more[:, c * 128 : c * 128 + 128]
    finish(colg_depth_c)
    half = []
    for h in range(2):
        one = colg_depth[h].astype(F32)
        for k in range(1, 4):
            one = one + colg_depth[k * 2 + h].astype(F32)
        half.append(one)
    col_gb = jnp.concatenate(
        [
            jnp.where(even_lane, half[0], pltpu.roll(half[1], 32, 1)),
            jnp.where(even_lane, pltpu.roll(half[0], 96, 1), half[1]),
        ],
        axis=0,
    ).astype(B16)
    grad = jnp.concatenate([scaled_grad[0], scaled_grad[1]], axis=1) + dot(col_gb, w_col, (0, 0))
    norm = normed[...]
    inv = inverse[...][:, :1]
    gained = grad * gain_ref[...]
    align = inv * (
        gained
        - jnp.mean(gained, axis=-1, keepdims=True)
        - norm * jnp.mean(gained * norm, axis=-1, keepdims=True)
    )
    align_out[...] = align.astype(B16)


    finish(big_narrow_c)
    big_sum = big_narrow[0].astype(F32)
    for k in range(1, 4):
        big_sum = big_sum + big_narrow[k].astype(F32)
    big_three[...] = big_sum.astype(B16)
    big_back_c = copies(BIG_BACK, "depth", lambda k: big_three, big_back)
    big_back[depth] = big_three[...]

    finish(small_depth_c)
    small_two[...] = total(small_depth).astype(B16)
    small_narrow_c = copies(SMALL_NARROW, "narrow", lambda k: small_two, small_narrow)
    small_narrow[narrow] = small_two[...]

    finish(big_back_c)
    slot = core * 8 + plane
    other = narrow + 1 - 2 * core
    for d in OFFSETS["plane"]:
        k = (plane + d) % 8
        sent(BIG_OUT, (k * 8 + depth, narrow), big_back, big_all.at[slot]).start()
    big_all[slot] = big_back[...]
    seven = big_all.at[pl.ds(0, 7)]
    big_out_c = sent(BIG_OUT, partner, seven, seven)

    for d in OFFSETS["plane"]:
        k = (plane + d) % 8
        sent(BIG_JOIN, (k * 8 + depth, other), big_back, big_all.at[slot]).start()
    sent(BIG_JOIN, partner, big_back, big_all.at[slot]).start()
    eight_more = big_all.at[pl.ds(0, 8)]
    big_join_c = sent(BIG_JOIN, partner, eight_more, eight_more)

    finish(small_narrow_c)
    small_three[...] = total(small_narrow).astype(B16)
    small_out_c = copies(SMALL_OUT, "plane", lambda k: small_three, small_all)
    small_all[plane] = small_three[...]

    def put_weight(part):
        for k in range(8):
            slice_k = big_all[pl.ds(pl.multiple_of(part * 8, 8), 8), k].astype(F32).reshape(64, 128)
            for c in range(2):
                weight_out[pl.ds(c * 16 + k * 2 + part, 32, stride=32), :] = slice_k[c * 32 : c * 32 + 32]

    finish(big_out_c)
    put_weight(core)

    @pl.when(lead)
    def _():
        sent(ROW_CORE, partner, row_pair, row_pair).wait_send()

        def sent_sums(own):
            part = rowg_sum.at[pl.ds(0, 7 if own else 8)]
            sent(ROWG_PAIR, partner, part, part).wait_send()

        for_own(sent_sums)

    @pl.when(follow)
    def _():
        sent(ROWG_CORE, partner, rowg_send, rowg_core).wait_send()

    finish(small_out_c)
    small = small_all[...].astype(F32).reshape(192, 128)
    bias_out[...] = small[128:130, :32]
    first = jnp.sum(jnp.where(sub128 == lane128, small[128:129], 0.0), axis=1, keepdims=True)
    second = jnp.sum(jnp.where(sub128 == lane128, small[129:130], 0.0), axis=1, keepdims=True)
    sums = jnp.concatenate([first, second], axis=0)
    product = jnp.concatenate([small[0:64], small[64:128]], axis=1)
    proj_out[...] = gain_ref[...] * product + shift_ref[...] * sums
    both = weight_ref[...].astype(F32)
    norm_out[0:1, :] = jnp.sum(both * product, axis=0, keepdims=True)
    norm_out[1:2, :] = jnp.sum(both * sums, axis=0, keepdims=True)
    finish(big_join_c)
    put_weight(1 - core)


def put_kernel(*refs):
    sem = refs[10]
    made = []
    for k in range(4):
        part = pl.ds(k * 256, 256)
        made.append(pltpu.make_async_copy(refs[4].at[part], refs[9].at[part], sem.at[4 + k]))
    made += [pltpu.make_async_copy(refs[k], refs[5 + k], sem.at[k]) for k in range(4)]
    for c in made:
        c.start()
    for c in made:
        c.wait()


def put(results):
    return pl.pallas_call(
        put_kernel,
        out_shape=tuple(jax.ShapeDtypeStruct(r.shape, r.dtype) for r in results),
        in_specs=[pl.BlockSpec(memory_space=pltpu.VMEM)] * 5,
        out_specs=(pl.BlockSpec(memory_space=pl.ANY),) * 5,
        scratch_shapes=[pltpu.SemaphoreType.DMA((8,))],
    )(*[pltpu.with_memory_space_constraint(r, pltpu.VMEM) for r in results])


def everything(x, pair, gain, shift, weight, bias, out_weight):
    vmem = pl.BlockSpec(memory_space=pltpu.VMEM)
    hbm = pl.BlockSpec(memory_space=pl.ANY)
    scratch = [
        ((128, 256), B16), ((1, 256), F32), ((1, 256), F32), ((64, 256), B16), ((2, 32), F32),
        ((128, 256), F32), ((128, 256), B16), ((2, 128, 128), F32), ((128, 128), F32), ((32, 128), F32),
        ((32, 128), F32), ((2, 16, 128), B16), ((64, 128), F32), ((8, 16, 128), B16), ((128, 128), F32),
        ((4, 16, 128), B16), ((8, 16, 128), B16),
        ((8, 4, 16, 128), B16), ((8, 8, 16, 128), B16), ((8, 64, 128), B16), ((16, 32, 128), B16), ((1024, 128), B16),
        ((2048, 512), B16), ((1024, 128), F32), ((1024, 128), B16), ((4, 512, 256), B16), ((128, 512), B16),
        ((512, 128), B16), ((8, 32, 2048), B16),
        ((8, 8, 16, 128), B16), ((8, 8, 16, 128), B16), ((128, 512), F32), ((8, 4, 16, 128), B16), ((8, 4, 16, 128), B16),
        ((8, 4, 16, 128), B16),
        ((4, 4, 16, 128), B16), ((64, 128), F32), ((64, 128), F32), ((32, 128), F32),
        ((128, 128), F32), ((8, 16, 128), B16), ((8, 16, 128), B16), ((2, 128, 128), F32),
        ((8, 128, 128), B16), ((8, 64, 128), B16), ((8, 64, 128), B16), ((8, 64, 128), B16), ((8, 8, 128), B16),
        ((8, 8, 128), B16), ((8, 128), B16), ((4, 8, 128), B16), ((8, 128), B16), ((8, 8, 128), B16),
        ((16, 8, 8, 128), B16),
        ((192, 128), F32), ((8, 24, 128), F32), ((24, 128), B16), ((8, 24, 128), B16), ((24, 128), B16),
        ((8, 24, 128), B16), ((24, 128), B16), ((8, 24, 128), B16),
        ((2, 128, 128), F32), ((4, 4, 8, 256), B16), ((2, 64, 256), B16), ((8, 4, 8, 256), B16), ((8, 64, 256), B16),
        ((1024, 256), B16),
    ]
    return pl.pallas_call(
        kernel,
        out_shape=(
            pltpu.VMEM((128, 256), B16),
            pltpu.VMEM((64, 256), F32),
            pltpu.VMEM((2, 32), F32),
            pltpu.VMEM((2, 256), F32),
            pltpu.VMEM((1024, 128), F32),
        ),
        in_specs=[hbm] * 7,
        out_specs=(vmem,) * 5,
        scratch_shapes=[pltpu.VMEM(shape, kind) for shape, kind in scratch]
        + [pltpu.SemaphoreType.DMA((STAGES,)), pltpu.SemaphoreType.DMA((STAGES,)), pltpu.SemaphoreType.DMA((7,)), pltpu.SemaphoreType.REGULAR],
        compiler_params=pltpu.CompilerParams(
            collective_id=0, has_side_effects=True, vmem_limit_bytes=56 * 1024 * 1024
        ),
    )(x, pair, gain, shift, weight, bias, out_weight)


def shards(
    alignment_rows,
    pair_output_gradient,
    layer_norm_gain,
    layer_norm_bias,
    projection_weight,
    projection_bias,
    output_weight,
):
    results = everything(
        alignment_rows.reshape(128, 256),
        pair_output_gradient,
        layer_norm_gain.reshape(1, 256),
        layer_norm_bias.reshape(1, 256),
        jnp.transpose(projection_weight, (0, 2, 1)).reshape(64, 256),
        projection_bias,
        output_weight,
    )
    align, proj, bias, norm, weight_grad = put(results)
    return (
        align.reshape(2, 64, 256),
        jnp.transpose(proj.reshape(2, 32, 256), (0, 2, 1)),
        bias,
        weight_grad,
        norm,
    )


def solution(mesh):
    return jax.shard_map(
        shards,
        mesh=mesh,
        in_specs=(P("wide", "narrow", None), P("wide", "narrow", None), P(), P(), P(), P(), P()),
        out_specs=(P("wide", "narrow", None), P(), P(), P(), P()),
        check_vma=False,
    )
```

```python
import jax
import jax.numpy as jnp
from jax import lax
from jax.experimental import pallas as pl
from jax.experimental.pallas import tpu as pltpu
from jax.sharding import PartitionSpec as P

F32, B16 = jnp.float32, jnp.bfloat16
MESH_ID = pl.DeviceIdType.MESH
OFFSETS = {"depth": (4, 3, 5, 2, 6, 1, 7), "narrow": (4, 3, 5, 2, 6, 1, 7), "plane": (6, 5, 7, 4, 2, 1, 3)}
STAGES = 24
SEQUENCES = 128
(
    ROW_DEPTH, COL_DEPTH, ROW_PAIR, COL_PLANE, COLG_PLANE, ROWG_PAIR, BIG_PLANE, ROWG_DEPTH, COLG_DEPTH,
    BIG_DEPTH, SMALL_PLANE, BIG_NARROW, SMALL_DEPTH, BIG_BACK, SMALL_NARROW, BIG_OUT, SMALL_OUT,
    PAIR_HALF, ROW_CORE, ROWG_CORE, BIG_CORE, BIG_JOIN, NORM_ROW, NORM_COL,
) = range(STAGES)


def dot(a, b, dims):
    return lax.dot_general(a, b, ((dims[:1], dims[1:]), ((), ())), preferred_element_type=F32)


def total(ref):
    acc = ref[0].astype(F32)
    for k in range(1, 8):
        acc = acc + ref[k].astype(F32)
    return acc


def lanes(shape):
    return lax.broadcasted_iota(jnp.int32, shape, len(shape) - 1)


def half_swap(x):
    return pltpu.roll(x, 64, 1)


def kernel(
    x_hbm, pair_hbm, gain_hbm, shift_hbm, weight_hbm, bias_hbm, out_weight_hbm,
    align_out, proj_out, bias_out, norm_out, weight_out,
    x_ref, gain_ref, shift_ref, weight_ref, bias_ref,
    normed, scaled, scaled32, inverse, row_tmp,
    row_send, col_send, row_got, col_got, col_wide, row_next, col_next,
    row_pair, col_plane, pair_ref, pair_tile, out_weight_ref, pair_two, weight32, weight_order, upstream, rows, rows_t, outer,
    colg_send, colg_got, rowg_acc, rowg_core, rowg_sum, rowg_send, rowg_got, rowg_next, rowg_depth, rowg,
    colg_wide, colg_next, colg_depth, scaled_grad,
    big_send, big_core, big_one, big_depth, big_part, big_plane, big_two, big_narrow, big_three, big_back,
    big_all,
    small_in, small_send, small_plane, small_part, small_depth, small_two, small_narrow, small_three, small_all,
    norm_tmp, norm_row_send, norm_col_send, norm_row, norm_col, norm_two,
    send_sem, recv_sem, local_sem, ready,
):
    wide = lax.axis_index("wide")
    narrow = lax.axis_index("narrow")
    plane = wide // 8
    depth = wide % 8
    own_pair = plane == narrow
    other_pair = plane != narrow
    lead = plane % 2 == narrow % 2
    follow = plane % 2 != narrow % 2
    barrier = pltpu.get_barrier_semaphore()
    inputs = (
        (x_hbm, x_ref), (gain_hbm, gain_ref), (shift_hbm, shift_ref), (weight_hbm, weight_ref), (bias_hbm, bias_ref),
        (pair_hbm, pair_ref), (out_weight_hbm, out_weight_ref),
    )
    fetches = [pltpu.make_async_copy(a, b, local_sem.at[k]) for k, (a, b) in enumerate(inputs)]
    place = {"plane": plane, "depth": depth, "narrow": narrow}

    def peer(kind, k):
        if kind == "plane":
            return (k * 8 + depth, narrow)
        if kind == "depth":
            return (plane * 8 + k, narrow)
        return (wide, k)

    def holder(d):
        return (narrow * 8 + depth, (narrow + 2 * d) % 8)

    def source(d):
        return (((plane + d) % 8) * 8 + depth, plane)

    def greet(device):
        pl.semaphore_signal(barrier, 1, device_id=device, device_id_type=MESH_ID)

    def greet_all(kind):
        for d in OFFSETS[kind]:
            greet(peer(kind, (place[kind] + d) % 8))

    greet_all("depth")
    greet_all("narrow")
    for c in fetches:
        c.start()
    fetch_pair, fetch_weight = fetches[5:]
    greet_all("plane")

    def copies(stage, kind, give, target, size=1):
        me = place[kind]
        lead = pl.ds(pl.multiple_of(me * size, size), size) if size > 1 else me
        for d in OFFSETS[kind]:
            k = (me + d) % 8
            pltpu.make_async_remote_copy(
                src_ref=give(k),
                dst_ref=target.at[lead],
                send_sem=send_sem.at[stage],
                recv_sem=recv_sem.at[stage],
                device_id=peer(kind, k),
                device_id_type=MESH_ID,
            ).start()
        whole = target.at[pl.ds(0, 7 * size)]
        return pltpu.make_async_remote_copy(
            src_ref=whole,
            dst_ref=whole,
            send_sem=send_sem.at[stage],
            recv_sem=recv_sem.at[stage],
            device_id=peer(kind, (me + 1) % 8),
            device_id_type=MESH_ID,
        )

    def finish(c):
        c.wait()

    def sent(stage, device, source_ref, target_ref):
        return pltpu.make_async_remote_copy(
            src_ref=source_ref,
            dst_ref=target_ref,
            send_sem=send_sem.at[stage],
            recv_sem=recv_sem.at[stage],
            device_id=device,
            device_id_type=MESH_ID,
        )

    partner = (wide, narrow + 1 - 2 * (narrow % 2))

    def for_own(what):
        pl.when(own_pair)(lambda: what(True))
        pl.when(other_pair)(lambda: what(False))

    for c in fetches[:5]:
        c.wait()
    value = x_ref[...].astype(F32)
    centre = value - jnp.mean(value, axis=-1, keepdims=True)
    inv = lax.rsqrt(jnp.mean(centre * centre, axis=-1, keepdims=True) + 1e-05)
    norm = centre * inv
    inverse[...] = jnp.broadcast_to(inv, (128, 128))
    normed[...] = norm
    scaled_b = (norm * gain_ref[...] + shift_ref[...]).astype(B16)
    scaled[...] = scaled_b
    for c in range(2):
        scaled32[c] = scaled_b[:, c * 128 : c * 128 + 128].astype(F32)

    def every_fourth(g):
        both = [scaled32[c, pl.ds(g, 32, stride=4), :] for c in range(2)]
        return jnp.concatenate(both, axis=1).astype(B16)

    w_row = weight_ref[0:32, :]
    w_col = weight_ref[32:64, :]
    w_row4 = jnp.concatenate([w_row] * 4, axis=0)
    sub = lax.broadcasted_iota(jnp.int32, (32, 32), 0)
    diagonal = sub == lanes((32, 32))
    row_bias = jnp.sum(jnp.where(diagonal, bias_ref[0:1, :], 0.0), axis=1, keepdims=True)
    col_bias = jnp.sum(jnp.where(diagonal, bias_ref[1:2, :], 0.0), axis=1, keepdims=True)
    lane128 = lanes((32, 128))
    sub128 = lax.broadcasted_iota(jnp.int32, (32, 128), 0)
    row_bias4 = jnp.sum(jnp.where(sub128 == lane128 % 32, row_bias, 0.0), axis=0, keepdims=True)
    group = lane128 // 32
    row_fac = jnp.zeros((32, 128), F32)
    for g in range(4):
        row_fac = jnp.where(group == g, dot(every_fourth(g), w_row4, (1, 1)), row_fac)
    row_tmp[...] = (row_fac + row_bias4).astype(B16).astype(F32)
    for g in range(4):
        for r in range(2):
            row_send[pl.ds(g * 8 + r * 4, 4), :] = row_tmp[pl.ds(r * 16 + g * 4, 4), :]
    even_lane = lanes((16, 128)) // 32 % 2 == 0
    col_fac = dot(w_col, scaled_b, (1, 1)) + col_bias
    fac_a, fac_b = col_fac[:16], col_fac[16:]
    col_send[0] = jnp.where(even_lane, fac_a, pltpu.roll(fac_b, 32, 1)).astype(B16)
    col_send[1] = jnp.where(even_lane, pltpu.roll(fac_a, 96, 1), fac_b).astype(B16)
    pl.semaphore_wait(barrier, 21)
    for d in (2, 4, 6):
        pl.semaphore_signal(ready, 1, device_id=(wide, (narrow + d) % 8), device_id_type=MESH_ID)


    def eight(ref, k):
        return ref.at[pl.ds(pl.multiple_of(k * 8, 8), 8)]

    parity = depth % 2
    row_depth_c = copies(ROW_DEPTH, "depth", lambda k: eight(row_send, k // 2), row_got, 8)
    col_depth_c = copies(COL_DEPTH, "depth", lambda k: col_send.at[k % 2], col_got)
    mine = pl.ds(pl.multiple_of(depth * 8, 8), 8)
    row_got[mine, :] = row_send[pl.ds(pl.multiple_of(depth // 2 * 8, 8), 8), :]
    col_got[depth] = col_send[parity]
    fetch_weight.wait()
    weight32[...] = out_weight_ref[...].astype(F32)
    for b in range(8):
        for c in range(4):
            q = c % 2 * 16 + b * 2 + c // 2
            weight_order[pl.ds((b * 4 + c) * 32, 32), :] = weight32[pl.ds(q, 32, stride=32), :].astype(B16)

    finish(row_depth_c)
    for g in range(4):
        both = [row_got[pl.ds(r * 4 + g, 8, stride=8), :] for r in range(2)]
        row_next[g] = jnp.concatenate(both, axis=0).astype(B16)

    pl.semaphore_wait(ready, 3)
    for d in (2, 1, 3):
        sent(ROW_PAIR, holder(d), row_next, row_pair.at[plane]).start()

    @pl.when(other_pair)
    def _():
        sent(ROW_PAIR, holder(0), row_next, row_pair.at[plane]).start()

    @pl.when(own_pair)
    def _():
        row_pair[plane] = row_next[...]

    fetch_pair.wait()
    own_rows = pl.ds(pl.multiple_of(parity * 8, 8), 8)
    pair_half_c = pltpu.make_async_remote_copy(
        src_ref=pair_ref.at[:, pl.ds(pl.multiple_of((1 - parity) * 32, 32), 32)],
        dst_ref=pair_tile.at[own_rows],
        send_sem=send_sem.at[PAIR_HALF],
        recv_sem=recv_sem.at[PAIR_HALF],
        device_id=peer("depth", depth + 1 - 2 * parity),
        device_id_type=MESH_ID,
    )
    pair_half_c.start()
    pair_tile[own_rows] = pair_ref[:, pl.ds(pl.multiple_of(parity * 32, 32), 32), :]

    finish(col_depth_c)
    col_wide[...] = col_got[...].astype(F32).reshape(128, 128)
    low8 = lanes((8, 128)) < 64

    for b in range(8):
        x0 = col_wide[pl.ds(b * 2, 8, stride=16), :]
        x1 = col_wide[pl.ds(b * 2 + 1, 8, stride=16), :]
        r0 = jnp.where(low8, x0, half_swap(x1))
        r1 = jnp.where(low8, half_swap(x0), x1)
        col_next[b] = jnp.concatenate([r0, r1], axis=0).astype(B16)
    col_plane_c = copies(COL_PLANE, "plane", lambda k: col_next, col_plane)
    col_plane[plane] = col_next[...]

    low32 = lane128 < 64
    even32 = group % 2 == 0
    for c in range(2):
        norm_tmp[c] = normed[:, pl.ds(c * 128, 128)]
    for g in range(4):
        one = jnp.concatenate([norm_tmp[c, pl.ds(g, 32, stride=4), :] for c in range(2)], axis=1)
        for k in range(4):
            rs = [one[r * 16 + k * 4 : r * 16 + k * 4 + 4] for r in range(2)]
            norm_row_send[k, g] = jnp.concatenate(rs, axis=0).astype(B16)
    for h in range(2):
        for r in range(2):
            norm_col_send[h, pl.ds(r * 32, 32), :] = normed[pl.ds(r * 64 + h * 32, 32), :].astype(B16)

    def up_half(which):
        tile = pair_tile[pl.ds(pl.multiple_of(which * 8, 8), 8)].reshape(256, 128)

        def up(t, _):
            for h in range(2):
                w = weight_order[pl.ds(pl.multiple_of(t * 256 + h * 128, 128), 128), :]
                res = dot(w, tile, (1, 1))
                for i in range(2):
                    a = [res[c * 32 : c * 32 + 32, i * 128 : i * 128 + 128] for c in range(4)]
                    first = [jnp.where(low32, a[c], half_swap(a[c + 2])) for c in range(2)]
                    second = [jnp.where(low32, half_swap(a[c]), a[c + 2]) for c in range(2)]
                    out = []
                    for f in (first, second):
                        out.append(jnp.where(even32, f[0], pltpu.roll(f[1], 32, 1)))
                        out.append(jnp.where(even32, pltpu.roll(f[0], 96, 1), f[1]))
                    spot = pl.ds(pl.multiple_of(which * 256 + i * 128, 128), 128)
                    upstream[t, spot, pl.ds(h * 128, 128)] = jnp.concatenate(out, axis=0).astype(B16)
            return 0

        lax.fori_loop(0, 4, up, 0)

    up_half(parity)
    pair_half_c.wait()
    norm_row_c = copies(NORM_ROW, "depth", lambda k: norm_row_send.at[k // 2], norm_row)
    norm_row[depth] = norm_row_send[depth // 2]
    up_half(1 - parity)
    norm_col_c = copies(NORM_COL, "depth", lambda k: norm_col_send.at[k % 2], norm_col)
    norm_col[depth] = norm_col_send[parity]

    pair_two[...] = jnp.zeros((2048, 512), B16)
    for i in range(16):
        for c in range(4):
            pair_two[pl.ds(i * 128 + c * 32, 32), pl.ds(c * 128, 128)] = pair_tile[i]

    def sent_rows(own):
        part = row_pair.at[pl.ds(0, 3 if own else 4)]
        sent(ROW_PAIR, partner, part, part).wait_send()

    for_own(sent_rows)

    @pl.when(lead)
    def _():
        def came(own):
            part = row_pair.at[pl.ds(0, 7 if own else 8)]
            sent(ROW_PAIR, partner, part, part).wait_recv()

        for_own(came)
        sent(ROW_CORE, partner, row_pair, row_pair).start()

    finish(col_plane_c)

    def col_tile(t):
        both = [col_plane[:, t * 2 + h].reshape(128, 128) for h in range(2)]
        return jnp.concatenate(both, axis=1)

    row_part = dot(col_tile(0), upstream[0], (1, 1))
    for t in range(1, 4):
        row_part = row_part + dot(col_tile(t), upstream[t], (1, 1))
    row_part = row_part * (1.0 / SEQUENCES)
    rowg_acc[...] = row_part
    row_part = row_part.astype(B16)
    for g in range(4):
        rowg_send[:, g] = row_part[:, g * 128 : g * 128 + 128].reshape(8, 16, 128)

    @pl.when(follow)
    def _():
        sent(ROWG_CORE, partner, rowg_send, rowg_core).start()
        sent(ROW_CORE, partner, row_pair, row_pair).wait_recv()

    for g in range(4):
        rows[:, pl.ds(g * 128, 128)] = row_pair[:, g].reshape(128, 128)
    for t in range(4):
        r = (dot(rows[...], upstream[t], (1, 0)) * (1.0 / SEQUENCES)).astype(B16)
        for h in range(2):
            colg_send[:, t * 2 + h] = r[:, h * 128 : h * 128 + 128].reshape(8, 16, 128)

    @pl.when(lead)
    def _():
        sent(ROWG_CORE, partner, rowg_send, rowg_core).wait_recv()
        for g in range(4):
            both = rowg_acc[:, pl.ds(g * 128, 128)] + rowg_core[:, g].reshape(128, 128).astype(F32)
            rowg_sum[:, g] = both.astype(B16).reshape(8, 16, 128)
        for d in range(1, 8):
            sent(ROWG_PAIR, source(d), rowg_sum.at[(plane + d) % 8], rowg_got.at[narrow // 2]).start()

    @pl.when(lead & other_pair)
    def _():
        sent(ROWG_PAIR, source(0), rowg_sum.at[plane], rowg_got.at[narrow // 2]).start()

    @pl.when(own_pair)
    def _():
        rowg_got[narrow // 2] = rowg_sum[plane]

    colg_plane_c = copies(COLG_PLANE, "plane", lambda k: colg_send.at[k], colg_got)
    colg_got[plane] = colg_send[plane]
    rows_t[...] = rows[...].astype(F32).T.astype(B16)

    for t in range(4):
        o = (dot(rows_t[...], col_tile(t), (1, 0)) * (1.0 / SEQUENCES)).astype(B16)
        for h in range(2):
            for i in range(16):
                outer[t * 2 + h, :, pl.ds(i * 128, 128)] = o[i * 32 : i * 32 + 32, h * 128 : h * 128 + 128]
    for g in range(2):
        res = dot(outer[pl.ds(g * 4, 4)].reshape(128, 2048), pair_two[...], (1, 0)).astype(B16)
        for k in range(4):
            for c in range(4):
                big_send[g * 4 + k, pl.ds(c * 32, 32), :] = res[k * 32 : k * 32 + 32, c * 128 : c * 128 + 128]
    core = narrow % 2
    own_half = pl.ds(pl.multiple_of(core * 64, 64), 64)
    other_half = pl.ds(pl.multiple_of(64 - core * 64, 64), 64)
    big_core_c = sent(BIG_CORE, partner, big_send.at[:, other_half], big_core)
    big_core_c.start()
    big_core_c.wait()
    big_one[...] = (big_send[:, own_half, :].astype(F32) + big_core[...].astype(F32)).astype(B16)
    big_depth_c = copies(BIG_DEPTH, "depth", lambda k: big_one.at[k], big_depth)
    big_depth[depth] = big_one[depth]

    def came_rowg(own):
        part = rowg_got.at[pl.ds(0, 3 if own else 4)]
        sent(ROWG_PAIR, partner, part, part).wait_recv()

    for_own(came_rowg)
    row_sum = rowg_got[0].astype(F32)
    for k in range(1, 4):
        row_sum = row_sum + rowg_got[k].astype(F32)
    for g in range(4):
        for r in range(2):
            rowg_next[pl.ds(r * 4 + g, 8, stride=8), :] = row_sum[g, r * 8 : r * 8 + 8, :]
    rowg_depth_c = copies(ROWG_DEPTH, "depth", lambda k: eight(rowg_next, k), rowg_depth, 8)
    rowg_depth[mine, :] = rowg_next[mine, :]

    finish(colg_plane_c)

    for b in range(8):
        acc = colg_got[0, b].astype(F32)
        for k in range(1, 8):
            acc = acc + colg_got[k, b].astype(F32)
        y0, y1 = acc[:8], acc[8:]
        colg_wide[pl.ds(b * 2, 8, stride=16), :] = jnp.where(low8, y0, half_swap(y1))
        colg_wide[pl.ds(b * 2 + 1, 8, stride=16), :] = jnp.where(low8, half_swap(y0), y1)
    colg_next[...] = colg_wide[...].astype(B16).reshape(8, 16, 128)
    colg_depth_c = copies(COLG_DEPTH, "depth", lambda k: colg_next.at[k], colg_depth)
    colg_depth[depth] = colg_next[depth]

    finish(norm_row_c)
    part_row = rowg_next[...]
    part_row_b = part_row.astype(B16)
    from_row = jnp.zeros((32, 256), F32)
    for g in range(4):
        near = norm_row[:, g].astype(F32).reshape(64, 256).astype(B16)
        from_row = from_row + dot(part_row_b, near, (0, 0))[g * 32 : g * 32 + 32]
    row_fold = jnp.sum(part_row, axis=0, keepdims=True)
    row_fold = row_fold + pltpu.roll(row_fold, 32, 1) + pltpu.roll(row_fold, 64, 1) + pltpu.roll(row_fold, 96, 1)
    finish(norm_col_c)
    for k in range(8):
        for r in range(2):
            for h in range(2):
                norm_two[pl.ds(k * 128 + r * 64 + h * 32, 32), :] = norm_col[k, pl.ds(r * 32, 32), :]
    long = jnp.concatenate([colg_wide[pl.ds(k * 16, 16), :] for k in range(8)], axis=1)
    even_long = lanes((16, 1024)) // 32 % 2 == 0
    long2 = jnp.concatenate([jnp.where(even_long, long, 0.0), jnp.where(even_long, 0.0, long)], axis=0)
    from_col = dot(long2.astype(B16), norm_two[...], (1, 0))
    col_sum = jnp.sum(long2, axis=1, keepdims=True)
    col_fold = jnp.sum(jnp.where(sub128 == lane128, col_sum, 0.0), axis=0, keepdims=True)
    small_in[pl.ds(0, 32), :] = from_row[:, :128]
    small_in[pl.ds(32, 32), :] = from_col[:, :128]
    small_in[pl.ds(64, 32), :] = from_row[:, 128:]
    small_in[pl.ds(96, 32), :] = from_col[:, 128:]
    small_in[pl.ds(128, 64), :] = jnp.zeros((64, 128), F32)
    small_in[pl.ds(128, 1), :] = row_fold
    small_in[pl.ds(129, 1), :] = col_fold

    small_send[...] = small_in[...].reshape(8, 24, 128).astype(B16)
    small_plane_c = copies(SMALL_PLANE, "plane", lambda k: small_send.at[k], small_plane)
    small_plane[plane] = small_send[plane]

    finish(big_depth_c)
    big_part[...] = total(big_depth).astype(B16).reshape(8, 8, 128)
    big_plane_c = copies(BIG_PLANE, "plane", lambda k: big_part.at[k], big_plane)
    big_plane[plane] = big_part[plane]

    finish(big_plane_c)
    big_two[...] = total(big_plane).astype(B16)
    chip = narrow // 2
    for d in (2, 1, 3):
        sent(BIG_NARROW, (wide, (narrow + 2 * d) % 8), big_two, big_narrow.at[chip]).start()
    big_narrow[chip] = big_two[...]
    three = big_narrow.at[pl.ds(0, 3)]
    big_narrow_c = sent(BIG_NARROW, partner, three, three)

    finish(small_plane_c)
    small_part[...] = total(small_plane).astype(B16)
    small_depth_c = copies(SMALL_DEPTH, "depth", lambda k: small_part, small_depth)
    small_depth[depth] = small_part[...]

    finish(rowg_depth_c)
    for g in range(4):
        for r in range(2):
            one = rowg_depth[pl.ds(g * 16 + r * 4, 4), :] + rowg_depth[pl.ds(g * 16 + 8 + r * 4, 4), :]
            rowg[pl.ds(r * 16 + g * 4, 4), :] = one
    row_gb = rowg[...].astype(B16).astype(F32)
    for g in range(4):
        more = dot(jnp.where(group == g, row_gb, 0.0).astype(B16), w_row4, (1, 0))
        for c in range(2):
            scaled_grad[c, pl.ds(g, 32, stride=4), :] = more[:, c * 128 : c * 128 + 128]
    finish(colg_depth_c)
    half = []
    for h in range(2):
        one = colg_depth[h].astype(F32)
        for k in range(1, 4):
            one = one + colg_depth[k * 2 + h].astype(F32)
        half.append(one)
    col_gb = jnp.concatenate(
        [
            jnp.where(even_lane, half[0], pltpu.roll(half[1], 32, 1)),
            jnp.where(even_lane, pltpu.roll(half[0], 96, 1), half[1]),
        ],
        axis=0,
    ).astype(B16)
    grad = jnp.concatenate([scaled_grad[0], scaled_grad[1]], axis=1) + dot(col_gb, w_col, (0, 0))
    norm = normed[...]
    inv = inverse[...][:, :1]
    gained = grad * gain_ref[...]
    align = inv * (
        gained
        - jnp.mean(gained, axis=-1, keepdims=True)
        - norm * jnp.mean(gained * norm, axis=-1, keepdims=True)
    )
    align_out[...] = align.astype(B16)


    finish(big_narrow_c)
    big_sum = big_narrow[0].astype(F32)
    for k in range(1, 4):
        big_sum = big_sum + big_narrow[k].astype(F32)
    big_three[...] = big_sum.astype(B16)
    big_back_c = copies(BIG_BACK, "depth", lambda k: big_three, big_back)
    big_back[depth] = big_three[...]

    finish(small_depth_c)
    small_two[...] = total(small_depth).astype(B16)
    small_narrow_c = copies(SMALL_NARROW, "narrow", lambda k: small_two, small_narrow)
    small_narrow[narrow] = small_two[...]

    finish(big_back_c)
    slot = core * 8 + plane
    other = narrow + 1 - 2 * core
    for d in OFFSETS["plane"]:
        k = (plane + d) % 8
        sent(BIG_OUT, (k * 8 + depth, narrow), big_back, big_all.at[slot]).start()
    big_all[slot] = big_back[...]
    seven = big_all.at[pl.ds(0, 7)]
    big_out_c = sent(BIG_OUT, partner, seven, seven)

    for d in OFFSETS["plane"]:
        k = (plane + d) % 8
        sent(BIG_JOIN, (k * 8 + depth, other), big_back, big_all.at[slot]).start()
    sent(BIG_JOIN, partner, big_back, big_all.at[slot]).start()
    eight_more = big_all.at[pl.ds(0, 8)]
    big_join_c = sent(BIG_JOIN, partner, eight_more, eight_more)

    finish(small_narrow_c)
    small_three[...] = total(small_narrow).astype(B16)
    small_out_c = copies(SMALL_OUT, "plane", lambda k: small_three, small_all)
    small_all[plane] = small_three[...]

    def put_weight(part):
        for k in range(8):
            slice_k = big_all[pl.ds(pl.multiple_of(part * 8, 8), 8), k].astype(F32).reshape(64, 128)
            for c in range(2):
                weight_out[pl.ds(c * 16 + k * 2 + part, 32, stride=32), :] = slice_k[c * 32 : c * 32 + 32]

    finish(big_out_c)
    put_weight(core)

    @pl.when(lead)
    def _():
        sent(ROW_CORE, partner, row_pair, row_pair).wait_send()

        def sent_sums(own):
            part = rowg_sum.at[pl.ds(0, 7 if own else 8)]
            sent(ROWG_PAIR, partner, part, part).wait_send()

        for_own(sent_sums)

    @pl.when(follow)
    def _():
        sent(ROWG_CORE, partner, rowg_send, rowg_core).wait_send()

    finish(small_out_c)
    small = small_all[...].astype(F32).reshape(192, 128)
    bias_out[...] = small[128:130, :32]
    first = jnp.sum(jnp.where(sub128 == lane128, small[128:129], 0.0), axis=1, keepdims=True)
    second = jnp.sum(jnp.where(sub128 == lane128, small[129:130], 0.0), axis=1, keepdims=True)
    sums = jnp.concatenate([first, second], axis=0)
    product = jnp.concatenate([small[0:64], small[64:128]], axis=1)
    proj_out[...] = gain_ref[...] * product + shift_ref[...] * sums
    both = weight_ref[...].astype(F32)
    norm_out[0:1, :] = jnp.sum(both * product, axis=0, keepdims=True)
    norm_out[1:2, :] = jnp.sum(both * sums, axis=0, keepdims=True)
    finish(big_join_c)
    put_weight(1 - core)


def put_kernel(*refs):
    sem = refs[10]
    made = []
    for k in range(4):
        part = pl.ds(k * 256, 256)
        made.append(pltpu.make_async_copy(refs[4].at[part], refs[9].at[part], sem.at[4 + k]))
    made += [pltpu.make_async_copy(refs[k], refs[5 + k], sem.at[k]) for k in range(4)]
    for c in made:
        c.start()
    for c in made:
        c.wait()


def put(results):
    return pl.pallas_call(
        put_kernel,
        out_shape=tuple(jax.ShapeDtypeStruct(r.shape, r.dtype) for r in results),
        in_specs=[pl.BlockSpec(memory_space=pltpu.VMEM)] * 5,
        out_specs=(pl.BlockSpec(memory_space=pl.ANY),) * 5,
        scratch_shapes=[pltpu.SemaphoreType.DMA((8,))],
    )(*[pltpu.with_memory_space_constraint(r, pltpu.VMEM) for r in results])


def everything(x, pair, gain, shift, weight, bias, out_weight):
    vmem = pl.BlockSpec(memory_space=pltpu.VMEM)
    hbm = pl.BlockSpec(memory_space=pl.ANY)
    scratch = [
        ((128, 256), B16), ((1, 256), F32), ((1, 256), F32), ((64, 256), B16), ((2, 32), F32),
        ((128, 256), F32), ((128, 256), B16), ((2, 128, 128), F32), ((128, 128), F32), ((32, 128), F32),
        ((32, 128), F32), ((2, 16, 128), B16), ((64, 128), F32), ((8, 16, 128), B16), ((128, 128), F32),
        ((4, 16, 128), B16), ((8, 16, 128), B16),
        ((8, 4, 16, 128), B16), ((8, 8, 16, 128), B16), ((8, 64, 128), B16), ((16, 32, 128), B16), ((1024, 128), B16),
        ((2048, 512), B16), ((1024, 128), F32), ((1024, 128), B16), ((4, 512, 256), B16), ((128, 512), B16),
        ((512, 128), B16), ((8, 32, 2048), B16),
        ((8, 8, 16, 128), B16), ((8, 8, 16, 128), B16), ((128, 512), F32), ((8, 4, 16, 128), B16), ((8, 4, 16, 128), B16),
        ((8, 4, 16, 128), B16),
        ((4, 4, 16, 128), B16), ((64, 128), F32), ((64, 128), F32), ((32, 128), F32),
        ((128, 128), F32), ((8, 16, 128), B16), ((8, 16, 128), B16), ((2, 128, 128), F32),
        ((8, 128, 128), B16), ((8, 64, 128), B16), ((8, 64, 128), B16), ((8, 64, 128), B16), ((8, 8, 128), B16),
        ((8, 8, 128), B16), ((8, 128), B16), ((4, 8, 128), B16), ((8, 128), B16), ((8, 8, 128), B16),
        ((16, 8, 8, 128), B16),
        ((192, 128), F32), ((8, 24, 128), B16), ((8, 24, 128), B16), ((24, 128), B16), ((8, 24, 128), B16), ((24, 128), B16),
        ((8, 24, 128), B16), ((24, 128), B16), ((8, 24, 128), B16),
        ((2, 128, 128), F32), ((4, 4, 8, 256), B16), ((2, 64, 256), B16), ((8, 4, 8, 256), B16), ((8, 64, 256), B16),
        ((1024, 256), B16),
    ]
    return pl.pallas_call(
        kernel,
        out_shape=(
            pltpu.VMEM((128, 256), B16),
            pltpu.VMEM((64, 256), F32),
            pltpu.VMEM((2, 32), F32),
            pltpu.VMEM((2, 256), F32),
            pltpu.VMEM((1024, 128), F32),
        ),
        in_specs=[hbm] * 7,
        out_specs=(vmem,) * 5,
        scratch_shapes=[pltpu.VMEM(shape, kind) for shape, kind in scratch]
        + [pltpu.SemaphoreType.DMA((STAGES,)), pltpu.SemaphoreType.DMA((STAGES,)), pltpu.SemaphoreType.DMA((7,)), pltpu.SemaphoreType.REGULAR],
        compiler_params=pltpu.CompilerParams(
            collective_id=0, has_side_effects=True, vmem_limit_bytes=56 * 1024 * 1024
        ),
    )(x, pair, gain, shift, weight, bias, out_weight)


def shards(
    alignment_rows,
    pair_output_gradient,
    layer_norm_gain,
    layer_norm_bias,
    projection_weight,
    projection_bias,
    output_weight,
):
    results = everything(
        alignment_rows.reshape(128, 256),
        pair_output_gradient,
        layer_norm_gain.reshape(1, 256),
        layer_norm_bias.reshape(1, 256),
        jnp.transpose(projection_weight, (0, 2, 1)).reshape(64, 256),
        projection_bias,
        output_weight,
    )
    align, proj, bias, norm, weight_grad = put(results)
    return (
        align.reshape(2, 64, 256),
        jnp.transpose(proj.reshape(2, 32, 256), (0, 2, 1)),
        bias,
        weight_grad,
        norm,
    )


def solution(mesh):
    return jax.shard_map(
        shards,
        mesh=mesh,
        in_specs=(P("wide", "narrow", None), P("wide", "narrow", None), P(), P(), P(), P(), P()),
        out_specs=(P("wide", "narrow", None), P(), P(), P(), P()),
        check_vma=False,
    )
```
